256 devices in a mesh: seq: 32 (over x, z), head: 8 (over y, core).
Axes of the slice: x: 4, y: 4, z: 8, core: 2. Of those that a mesh axis runs over, the one named last changes fastest.
Arguments:
- points: bfloat16 [65536, 512], P(('seq', 'head')), may hold values from -6 to 6
- gain_attn: float32 [512], replicated, may hold values from 0.1 to 1.9
- w_qkv: bfloat16 [512, 1536], replicated
- w_out: bfloat16 [512, 512], replicated, may hold values from -1.1953125 to 1.1953125
- gain_mlp: float32 [512], replicated, may hold values from 0.1 to 1.9
- w_fc1: bfloat16 [512, 2048], P(None, 'head'), may hold values from -0.25 to 0.25
- w_fc2: bfloat16 [2048, 512], P('head'), may hold values from -0.125 to 0.125
- contact_route: int32 [8, 128, 1], P('head'), may hold values from 0 to 7; in each aligned block of 4 rows (0 to 3, 4 to 7, ..., all dimensions but the last counted through in order) at most 2 rows name the same one
- contact_patch: int32 [8, 128], P('head'), may hold values from 0 to 1
- counts: int32 [256], replicated, may hold values from 64 to 256, as said below
Outputs:
- block_out: bfloat16 [65536, 512], P(('seq', 'head'))
The draws below stay inside these ranges and needn't reach their ends.
Inputs may be any that keep to these rules, and one draw needn't show every extreme that they name: `contact_route`: in each head group, among the 4 contacts of the patches of one seq index, no route value appears more than 2 times. `counts`: some shard is full in every draw.
All inputs are finite; a program needn't handle non-finite values.
Results may differ from the reference program's by a relative error of at most 0.03.
Values may be sent and summed in bfloat16 or wider, within the bound.
A program may use at most 128 MiB of HBM per device.

```python
import math
import jax
import jax.numpy as jnp
import numpy as np
from jax import lax

D = 512
HEADS = 32
HEAD_DIM = 16
FF = 2048
PATCH = 1024
CB = 2
TOK_DEV = 256
SHARDS = 256
TOKENS = 65536
NPL = 2
PATCHES = 64
REACH = 4
CAP = 2
N_SEQ = 32
N_HEAD = 8


def draw_w_qkv(key, part):
    weights = jax.random.normal(key, (D, HEADS, 3, HEAD_DIM), jnp.float32) / math.sqrt(D)
    return weights.reshape(D, HEADS * 3 * HEAD_DIM).astype(jnp.bfloat16)


def draw_counts(key, part):
    drawn = jax.random.randint(key, (SHARDS,), TOK_DEV // 4, TOK_DEV + 1)
    full_shard = jax.random.randint(jax.random.fold_in(key, 3), (), 0, SHARDS)
    return jnp.where(jnp.arange(SHARDS) == full_shard, TOK_DEV, drawn).astype(jnp.int32)


def touch_ends(values, rng, smallest, high):
    dims = values.shape
    spot = [jax.random.randint(jax.random.fold_in(rng, axis), (), 0, dims[axis]) for axis in range(len(dims))]
    values = values.at[tuple(spot)].set(smallest)
    longest = dims.index(max(dims))
    spot[longest] = (spot[longest] + 1) % dims[longest]
    return values.at[tuple(spot)].set(high)


def block_scale(key, shape, pieces, smallest, high):
    factor_of, own = 1.0, jax.random.fold_in(key, 6)
    for axis_at, blocks in pieces:
        steps = jnp.exp(jax.random.uniform(jax.random.fold_in(own, axis_at), (blocks,), jnp.float32, smallest / len(pieces), high / len(pieces)))
        factor_of = factor_of * jnp.repeat(steps, shape[axis_at] // blocks).reshape([-1 if axis == axis_at else 1 for axis in range(len(shape))])
    return factor_of


def shared_out(stream_key, own, number, rows, number_of, top, bound, skew):
    order = jax.random.permutation(stream_key, number_of)
    crowded, usual = portions_of(number_of, rows * top, bound, skew, True), portions_of(number_of, rows * top, bound, skew, False)
    places = jnp.arange(number_of)

    def named(tallies, offset_by):
        used = int((tallies > 0).sum())
        fixed = max(1, used // 4)
        shifted = fixed + (places - fixed + offset_by * (used - fixed)) % max(1, number_of - fixed)
        return jnp.zeros((number_of,), jnp.int32).at[order[jnp.where(places < fixed, places, shifted)]].set(jnp.asarray(tallies, jnp.int32))

    tallies = jnp.where(number % 4 == 0, named(crowded, number // 4), named(usual, number - number // 4 - 1))
    mixed = jax.random.permutation(jax.random.fold_in(own, 3), number_of)
    source_of, sink = mixed[0:number_of // 2 * 2:2], mixed[1:number_of // 2 * 2:2]
    room = jnp.minimum(tallies[source_of] - 1, bound - tallies[sink]) // 2
    room = jnp.where((source_of == order[0]) | (sink == order[0]) | (tallies[sink] == 0), 0, jnp.maximum(room, 0))
    shifted = jax.random.randint(jax.random.fold_in(own, 4), (number_of // 2,), 0, 1 << 20) % (room + 1)
    tallies = tallies.at[source_of].add(-shifted).at[sink].add(shifted)
    items = jnp.searchsorted(jnp.cumsum(tallies), jnp.arange(rows * top), side="right").astype(jnp.int32)
    grid = items.reshape(top, rows).T
    grid = grid[jax.random.permutation(jax.random.fold_in(own, 1), rows)]
    offset_by = jax.random.randint(jax.random.fold_in(own, 2), (rows, 1), 0, top)
    return jnp.take_along_axis(grid, (jnp.arange(top)[None, :] + offset_by) % top, axis=1)


def portions_of(count, total, bound, lean, full):
    weights = [(1 << 20) // math.isqrt(standing ** lean) + 1 for standing in range(1, count + 1)]
    largest = bound if full else min(bound, max(-(-total // count), total * weights[0] // sum(weights)))
    least = 1 if total - largest >= count - 1 else 0
    given, rest = [largest] + [least] * (count - 1), total - largest - least * (count - 1)
    while rest > 0:
        free = [i for i in range(1, count) if given[i] < largest] or [i for i in range(1, count) if given[i] < bound]
        mass, budget = sum([weights[i] for i in free]), rest
        for i in free:
            more = min(bound - given[i], max(1, budget * weights[i] // mass), rest)
            given[i] = given[i] + more
            rest = rest - more
    return np.array(given)


def gaussian(own_key, extent, deviation, bound, shards=(), kind=jnp.bfloat16):
    entries = jax.random.normal(own_key, extent, jnp.float32) * deviation
    if len(shards) > 0:
        entries = block_scale(own_key, extent, shards, -0.22, 0.18) * entries
    return jnp.clip(entries, min=-bound, max=bound).astype(kind)


def setup_inputs(seed: int = 0) -> dict:
    splits = jax.random.split(jax.random.key(seed), 11)
    points = gaussian(splits[0], (TOKENS, D), 1.0, 6.0, ((0, 256),))
    gain_attn = jnp.clip(1.0 + 0.18 * jax.random.normal(splits[1], (D,), jnp.float32), 0.1, 1.9)
    w_qkv = draw_w_qkv(jax.random.fold_in(splits[10], 71), 0)
    w_out = gaussian(splits[3], (D, D), 0.2, 1.1953125)
    gain_mlp = jnp.clip(1.0 + 0.18 * jax.random.normal(splits[4], (D,), jnp.float32), 0.1, 1.9)
    w_fc1 = gaussian(splits[5], (D, FF), D ** -0.5, 0.25, ((1, 8),))
    w_fc2 = gaussian(splits[6], (FF, D), FF ** -0.5, 0.125, ((0, 8),))
    contact_route_keys = jax.random.split(jax.random.fold_in(splits[7], 1), N_HEAD * (PATCHES * CB) // (NPL * CB))
    contact_route_turns = jax.random.permutation(jax.random.fold_in(splits[7], 3), N_HEAD * (PATCHES * CB) // (NPL * CB))
    contact_route = jax.vmap(lambda own, number: shared_out(jax.random.fold_in(splits[7], 2), own, number, NPL * CB, 2 * REACH, 1, CAP, 1))(contact_route_keys, contact_route_turns).reshape((N_HEAD, PATCHES * CB, 1))
    contact_patch = touch_ends(jax.random.randint(splits[8], (N_HEAD, PATCHES * CB), 0, NPL), jax.random.fold_in(splits[8], 1), 0, NPL - 1).astype(jnp.int32)
    counts = draw_counts(jax.random.fold_in(splits[10], 71), 0)
    return dict(points=points, gain_attn=gain_attn, w_qkv=w_qkv, w_out=w_out, gain_mlp=gain_mlp, w_fc1=w_fc1, w_fc2=w_fc2, contact_route=contact_route, contact_patch=contact_patch, counts=counts)


def layer_norm(values, gain):
    values = values.astype(jnp.float32)
    centred = values - lax.optimization_barrier(jnp.mean(values, axis=-1, keepdims=True))
    spread = lax.optimization_barrier(jnp.mean(centred * centred, axis=-1, keepdims=True))
    return centred * lax.rsqrt(spread + 1e-05) * gain.astype(jnp.float32)

def reference(points, gain_attn, w_qkv, w_out, gain_mlp, w_fc1, w_fc2, contact_route, contact_patch, counts):
    per_group = HEADS // N_HEAD
    row_blocks = points.reshape(PATCHES, PATCH, D)

    def project(row_block):
        normed = layer_norm(row_block, gain_attn).astype(jnp.bfloat16)
        return jnp.dot(normed, w_qkv, preferred_element_type=jnp.float32).astype(jnp.bfloat16)
    projected = lax.map(project, row_blocks).reshape(PATCHES, PATCH, HEADS, 3, HEAD_DIM)
    queries = projected[:, :, :, 0]
    key_values = projected[:, :, :, 1:]
    positions = jnp.arange(TOKENS, dtype=jnp.int32)
    valid_all = (positions % TOK_DEV < counts[positions // TOK_DEV]).reshape(PATCHES, PATCH)
    route_ids = contact_route.reshape(N_HEAD, PATCHES, CB)
    offset = route_ids - REACH + (route_ids >= REACH).astype(jnp.int32)
    shard_ids = jnp.arange(PATCHES, dtype=jnp.int32) // NPL
    target = ((shard_ids[None, :, None] + offset) % N_SEQ * NPL + contact_patch.reshape(N_HEAD, PATCHES, CB)).astype(jnp.int32)
    head_ids = jnp.arange(HEADS, dtype=jnp.int32)
    score_scale = HEAD_DIM ** (-0.5)

    def attend(patch_index):
        far_ids = jnp.repeat(target[:, patch_index], per_group, axis=0)
        far_kv = key_values[far_ids, :, head_ids[:, None]]
        own_kv = jnp.transpose(key_values[patch_index], (1, 0, 2, 3))[:, None]
        keys_all = jnp.concatenate([own_kv, far_kv], axis=1).reshape(HEADS, -1, 2, HEAD_DIM)
        own_valid = jnp.broadcast_to(valid_all[patch_index], (HEADS, 1, PATCH))
        key_valid = jnp.concatenate([own_valid, valid_all[far_ids]], axis=1).reshape(HEADS, -1)
        scores = jnp.einsum('qhd,hkd->hqk', queries[patch_index].astype(jnp.float32), keys_all[:, :, 0].astype(jnp.float32)) * score_scale
        masked = jnp.where(key_valid[:, None, :], scores, -jnp.inf)
        row_max = lax.optimization_barrier(jnp.max(masked, axis=-1, keepdims=True))
        weights = jnp.exp(masked - row_max)
        denominator = lax.optimization_barrier(jnp.sum(weights, axis=-1))
        rounded = weights.astype(jnp.bfloat16)
        attended = jnp.einsum('hqk,hkd->qhd', rounded.astype(jnp.float32), keys_all[:, :, 1].astype(jnp.float32))
        attended = attended / jnp.transpose(denominator)[:, :, None]
        return attended.astype(jnp.bfloat16).reshape(PATCH, D)
    attn_rows = lax.map(attend, jnp.arange(PATCHES, dtype=jnp.int32))

    def finish(packed):
        row_block, attn_block = packed
        updated = (row_block.astype(jnp.float32) + jnp.dot(attn_block, w_out, preferred_element_type=jnp.float32)).astype(jnp.bfloat16)
        normed_mlp = layer_norm(updated, gain_mlp).astype(jnp.bfloat16)
        hidden = jax.nn.gelu(jnp.dot(normed_mlp, w_fc1, preferred_element_type=jnp.float32), approximate=False).astype(jnp.bfloat16)
        partials = jnp.einsum('tjf,jfd->jtd', hidden.reshape(PATCH, N_HEAD, -1).astype(jnp.float32), w_fc2.reshape(N_HEAD, -1, D).astype(jnp.float32))
        partials = lax.optimization_barrier(partials.astype(jnp.bfloat16)).astype(jnp.float32)
        return (updated.astype(jnp.float32) + lax.optimization_barrier(jnp.sum(partials, axis=0))).astype(jnp.bfloat16)
    return lax.map(finish, (row_blocks, attn_rows)).reshape(TOKENS, D)
```

```python
import functools
import math

import jax
import jax.numpy as jnp
import numpy as np
from jax import lax
from jax.experimental import pallas as pl
from jax.experimental.pallas import tpu as pltpu
from jax.sharding import PartitionSpec as P

D = 512
HEADS = 32
HEAD_DIM = 16
PATCH = 1024
CB = 2
NPL = 2
REACH = 4
TOK = 256
GROUPS = 8
LANES = 128
CHUNK = 256
F32 = jnp.float32
BF16 = jnp.bfloat16
MASKED = -3.3e38
ROWS = 8 * LANES


def placing():
    kv = np.zeros((384, 256), np.float32)
    low = np.zeros((384, 256), np.float32)
    high = np.zeros((384, 256), np.float32)
    for group in range(2):
        for head in range(4):
            for dim in range(HEAD_DIM):
                source = group * 192 + head * 48 + dim
                lane = group * 128 + head * 16 + dim
                low[source, lane] = 1
                high[source, lane + 64] = 1
                kv[source + 16, lane] = 1
                kv[source + 32, lane + 64] = 1
    return np.concatenate([kv, low, high], axis=1)


def lane_of(shape):
    return lax.broadcasted_iota(jnp.int32, shape, len(shape) - 1)


def normalise(values, gain):
    centred = values - jnp.mean(values, axis=-1, keepdims=True)
    spread = jnp.mean(centred * centred, axis=-1, keepdims=True)
    return centred * lax.rsqrt(spread + 1e-05) * gain


def project_kernel(points_ref, gain_ref, w_ref, scale_ref, place_ref, kv_ref, q_ref):
    normed = normalise(points_ref[...].astype(F32), gain_ref[...]).astype(BF16)
    for pair in range(GROUPS // 2):
        columns = slice(384 * pair, 384 * pair + 384)
        projected = jnp.dot(normed, w_ref[:, columns], preferred_element_type=F32)
        projected = (projected * scale_ref[:, columns]).astype(BF16)
        kv = jnp.dot(projected, place_ref[:, :256], preferred_element_type=F32).astype(BF16)
        q = jnp.dot(projected[:128], place_ref[:, 256:512], preferred_element_type=F32)
        q = q + jnp.dot(projected[128:], place_ref[:, 512:], preferred_element_type=F32)
        q = q.astype(BF16)
        for side in range(2):
            kv_ref[2 * pair + side] = kv[:, 128 * side:128 * side + 128]
            q_ref[2 * pair + side] = q[:, 128 * side:128 * side + 128]


def project(points, gain, w_qkv):
    scale = np.ones((1, 1536), np.float32)
    scale[0, np.arange(1536) % 48 < 16] = HEAD_DIM ** -0.5 * math.log2(math.e)
    return pl.pallas_call(
        project_kernel,
        out_shape=(
            jax.ShapeDtypeStruct((GROUPS, TOK, LANES), BF16),
            jax.ShapeDtypeStruct((GROUPS, LANES, LANES), BF16),
        ),
        name="project",
    )(points, gain.reshape(1, D), w_qkv, jnp.asarray(scale), jnp.asarray(placing(), BF16))


def attend_kernel(
    slot_of, sides, routes_ref, local_ref, counts_ref, place_ref, q_ref, kv_ref, out_ref,
    raw, keys, vals, lhs, acc, top, sems,
):
    seq = place_ref[0]
    core = place_ref[1]
    own_slot = slot_of(0, core) * NPL

    def source(patch, which):
        if which == 0:
            return own_slot + patch, seq * GROUPS + patch * 4
        row = seq * NPL * CB + patch * CB + which - 1
        route = routes_ref[row]
        offset = jnp.where(route < REACH, route - REACH, route - REACH + 1)
        local = local_ref[row]
        owner = lax.rem(seq + offset + 32, 32)
        return slot_of(offset, core) * NPL + local, owner * GROUPS + local * 4

    for patch in range(NPL):
        for which in range(CB + 1):
            slot, _ = source(patch, which)
            pltpu.make_async_copy(kv_ref.at[slot], raw.at[patch * 3 + which], sems.at[patch * 3 + which]).start()

    lane_kv = lane_of((TOK, LANES))
    row_kv = lax.broadcasted_iota(jnp.int32, (TOK, LANES), 0)
    lane_q = lane_of((LANES, LANES))
    one = jnp.ones((TOK, LANES), BF16)
    zero = jnp.zeros((TOK, LANES), BF16)
    low_lane = lane_kv < 64
    sum_of = ((lane_of((LANES, LANES)) == (lax.broadcasted_iota(jnp.int32, (LANES, LANES), 0) // 16))).astype(BF16)
    sum_of = jnp.where(lane_q < 4, sum_of, jnp.zeros_like(sum_of))

    def patch_body(patch, _):
        for which in range(CB + 1):
            pltpu.make_async_copy(kv_ref.at[0], raw.at[patch * 3 + which], sems.at[patch * 3 + which]).wait()

        first = jnp.int32(0)
        key_top = jnp.zeros((1, LANES), F32)
        val_top = jnp.zeros((1, LANES), F32)
        for which in range(CB + 1):
            row = seq * NPL * CB + patch * CB + max(which - 1, 0)
            if which == 0:
                shard = seq * GROUPS + patch * 4
            else:
                route = routes_ref[row]
                offset = jnp.where(route < REACH, route - REACH, route - REACH + 1)
                shard = lax.rem(seq + offset + 32, 32) * GROUPS + local_ref[row] * 4
            for part in range(4):
                count = counts_ref[shard + part]
                block = raw[patch * 3 + which, TOK * part:TOK * part + TOK, :]
                valid = row_kv < count
                flag = jnp.where(valid, zero, jnp.where(lane_kv < 66, jnp.full_like(zero, MASKED), zero))
                keyed = jnp.where(low_lane & valid, block, zero)
                at = pl.ds(pl.multiple_of(first, 16), TOK)
                keys[at, :] = jnp.where(low_lane, keyed, flag)
                vals[at, :] = jnp.where(low_lane, one, block)
                squares = jnp.dot(keyed * keyed, sum_of, preferred_element_type=F32)
                key_top = jnp.maximum(key_top, jnp.max(squares, axis=0, keepdims=True))
                size = jnp.max(jnp.where(low_lane, zero, jnp.abs(block)).astype(F32), axis=0, keepdims=True)
                val_top = jnp.maximum(val_top, size)
                first = first + (count + 15) // 16 * 16
        tail = pl.ds(pl.multiple_of(first, 16), TOK)
        keys[tail, :] = jnp.where(low_lane | (lane_kv >= 66), zero, jnp.full_like(zero, MASKED))
        vals[tail, :] = jnp.where(low_lane, one, zero)
        chunks = (first + CHUNK - 1) // CHUNK

        query_top = jnp.zeros((1, LANES), F32)
        for part in range(4):
            packed = q_ref[patch * 4 + part]
            for half in range(2):
                q = packed if half == 0 else pltpu.roll(packed.astype(F32), 64, 1).astype(BF16)
                q = jnp.where(lane_q < 64, q, jnp.zeros_like(q))
                squares = jnp.dot(q * q, sum_of, preferred_element_type=F32)
                query_top = jnp.maximum(query_top, jnp.max(squares, axis=0, keepdims=True))
        bound = jnp.max(query_top * key_top)
        small = (bound < 3000.0) & (jnp.max(val_top) < 1e9)

        def shard_body(part, _):
            packed = q_ref[patch * 4 + part]
            for half in range(2):
                q = packed if half == 0 else pltpu.roll(packed.astype(F32), 64, 1).astype(BF16)
                for head in range(4):
                    mine = (lane_q >= 16 * head) & (lane_q < 16 * head + 16)
                    flags = jnp.where((lane_q >= 64) & (lane_q < 66), jnp.ones_like(q), jnp.zeros_like(q))
                    lhs[pl.ds((half * 4 + head) * LANES, LANES), :] = jnp.where(mine, q, flags)
            acc[...] = jnp.zeros_like(acc)

            def scores_of(chunk):
                at = pl.ds(pl.multiple_of(chunk * CHUNK, CHUNK), CHUNK)
                return at, lax.dot_general(
                    lhs[...], keys[at, :], (((1,), (1,)), ((), ())), preferred_element_type=F32
                )

            @pl.when(small)
            def _():
                def chunk_body(chunk, _):
                    at, scores = scores_of(chunk)
                    weights = jnp.exp2(scores).astype(BF16)
                    acc[...] += jnp.dot(weights, vals[at, :], preferred_element_type=F32)
                    return 0

                lax.fori_loop(0, chunks, chunk_body, 0)

            @pl.when(jnp.logical_not(small))
            def _():
                top[...] = jnp.full_like(top, -jnp.inf)

                def top_body(chunk, _):
                    _, scores = scores_of(chunk)
                    top[...] = jnp.maximum(top[...], jnp.max(scores, axis=1, keepdims=True))
                    return 0

                lax.fori_loop(0, chunks, top_body, 0)

                def chunk_body(chunk, _):
                    at, scores = scores_of(chunk)
                    weights = jnp.exp2(scores - top[:, :1]).astype(BF16)
                    acc[...] += jnp.dot(weights, vals[at, :], preferred_element_type=F32)
                    return 0

                lax.fori_loop(0, chunks, chunk_body, 0)

            halves = []
            for half in range(2):
                joined = jnp.zeros((LANES, LANES), F32)
                for head in range(4):
                    part_acc = acc[pl.ds((half * 4 + head) * LANES, LANES), :]
                    mine = (lane_q >= 64 + 16 * head) & (lane_q < 80 + 16 * head)
                    joined = jnp.where(mine, part_acc / pltpu.roll(part_acc, 64, 1), joined)
                halves.append(joined)
            out_ref[patch * 4 + part] = (pltpu.roll(halves[0], 64, 1) + halves[1]).astype(BF16)
            return 0

        lax.fori_loop(0, 4, shard_body, 0)
        return 0

    lax.fori_loop(0, NPL, patch_body, 0)


def attend(slot_of, place, routes, local, counts, q, kv):
    smem = pl.BlockSpec(memory_space=pltpu.SMEM)
    vmem = pl.BlockSpec(memory_space=pltpu.VMEM)
    return pl.pallas_call(
        functools.partial(attend_kernel, slot_of, 0),
        out_shape=jax.ShapeDtypeStruct((GROUPS, LANES, LANES), BF16),
        in_specs=[smem, smem, smem, smem, vmem, pl.BlockSpec(memory_space=pl.ANY)],
        out_specs=vmem,
        scratch_shapes=[
            pltpu.VMEM((6, PATCH, LANES), BF16),
            pltpu.VMEM((3 * PATCH + TOK, LANES), BF16),
            pltpu.VMEM((3 * PATCH + TOK, LANES), BF16),
            pltpu.VMEM((ROWS, LANES), BF16),
            pltpu.VMEM((ROWS, LANES), F32),
            pltpu.VMEM((ROWS, LANES), F32),
            pltpu.SemaphoreType.DMA((6,)),
        ],
        compiler_params=pltpu.CompilerParams(vmem_limit_bytes=40 << 20),
        name="attend",
    )(routes, local, counts, place, q, kv)


def finish_kernel(points_ref, packed_ref, w_out_ref, gain_ref, w1_ref, w2_ref, out_ref):
    lane = lane_of((LANES, LANES))
    low, high = [], []
    for pair in range(GROUPS // 2):
        first, second = packed_ref[2 * pair].astype(F32), packed_ref[2 * pair + 1].astype(F32)
        low.append(jnp.where(lane < 64, first, pltpu.roll(second, 64, 1)))
        high.append(jnp.where(lane < 64, pltpu.roll(first, 64, 1), second))
    attended = jnp.concatenate([jnp.concatenate(low, axis=1), jnp.concatenate(high, axis=1)], axis=0)
    updated = points_ref[...].astype(F32) + jnp.dot(
        attended.astype(BF16), w_out_ref[...], preferred_element_type=F32
    )
    updated = updated.astype(BF16).astype(F32)
    normed = normalise(updated, gain_ref[...]).astype(BF16)
    total = updated
    for part in range(GROUPS):
        hidden = jnp.dot(normed, w1_ref[part], preferred_element_type=F32)
        hidden = hidden * (0.5 * (1.0 + lax.erf(hidden * (2.0 ** -0.5))))
        total = total + jnp.dot(hidden.astype(BF16), w2_ref[part], preferred_element_type=F32)
    out_ref[...] = total.astype(BF16)


def finish(points, packed, w_out, gain, w1, w2):
    return pl.pallas_call(
        finish_kernel,
        out_shape=jax.ShapeDtypeStruct((TOK, D), BF16),
        compiler_params=pltpu.CompilerParams(vmem_limit_bytes=40 << 20),
        name="finish",
    )(points, packed, w_out, gain.reshape(1, D), w1, w2)


def passed_along(value, axis, steps):
    count = lax.axis_size(axis)
    return lax.ppermute(value, axis, [(source, (source + steps) % count) for source in range(count)])


def per_device(
    points, gain_attn, w_qkv, w_out, gain_mlp, w_fc1, w_fc2, contact_route, contact_patch, counts
):
    w1 = lax.all_gather(w_fc1, "head", axis=0)
    w2 = lax.all_gather(w_fc2, "head", axis=0)
    kv, q = project(points, gain_attn, w_qkv)
    kv = lax.all_to_all(kv, "head", split_axis=0, concat_axis=0, tiled=True)
    q = lax.all_to_all(q, "head", split_axis=0, concat_axis=0, tiled=True)
    own = kv.reshape(NPL, PATCH, LANES)
    slots = [own if offset == 0 else passed_along(own, "seq", -offset) for offset in range(-REACH, REACH + 1)]
    slots = jnp.concatenate(slots, axis=0)
    place = jnp.stack([lax.axis_index("seq"), jnp.int32(0)])
    packed = attend(
        lambda offset, core: offset + REACH, place, contact_route.reshape(-1), contact_patch.reshape(-1), counts, q, slots
    )
    packed = lax.all_to_all(packed, "head", split_axis=0, concat_axis=0, tiled=True)
    return finish(points, packed, w_out, gain_mlp, w1, w2)


def solution(mesh):
    return jax.shard_map(
        per_device,
        mesh=mesh,
        in_specs=(
            P(("seq", "head"), None), P(), P(), P(), P(), P(None, "head"), P("head", None),
            P("head", None, None), P("head", None), P(),
        ),
        out_specs=P(("seq", "head"), None),
        check_vma=False,
    )
```

```python
import functools
import math

import jax
import jax.numpy as jnp
import numpy as np
from jax import lax
from jax.experimental import pallas as pl
from jax.experimental.pallas import tpu as pltpu
from jax.sharding import PartitionSpec as P

D = 512
HEADS = 32
HEAD_DIM = 16
PATCH = 1024
CB = 2
NPL = 2
REACH = 4
TOK = 256
GROUPS = 8
LANES = 128
CHUNK = 256
F32 = jnp.float32
BF16 = jnp.bfloat16
MASKED = -3.3e38
ROWS = 8 * LANES
MESH = pl.DeviceIdType.MESH


def placing():
    kv = np.zeros((384, 256), np.float32)
    low = np.zeros((384, 256), np.float32)
    high = np.zeros((384, 256), np.float32)
    for group in range(2):
        for head in range(4):
            for dim in range(HEAD_DIM):
                source = group * 192 + head * 48 + dim
                lane = group * 128 + head * 16 + dim
                low[source, lane] = 1
                high[source, lane + 64] = 1
                kv[source + 16, lane] = 1
                kv[source + 32, lane + 64] = 1
    return np.concatenate([kv, low, high], axis=1)


def lane_of(shape):
    return lax.broadcasted_iota(jnp.int32, shape, len(shape) - 1)


def normalise(values, gain):
    centred = values - jnp.mean(values, axis=-1, keepdims=True)
    spread = jnp.mean(centred * centred, axis=-1, keepdims=True)
    return centred * lax.rsqrt(spread + 1e-05) * gain


def project_kernel(points_ref, gain_ref, w_ref, scale_ref, place_ref, kv_ref, q_ref):
    normed = normalise(points_ref[...].astype(F32), gain_ref[...]).astype(BF16)
    for pair in range(GROUPS // 2):
        columns = slice(384 * pair, 384 * pair + 384)
        projected = jnp.dot(normed, w_ref[:, columns], preferred_element_type=F32)
        projected = (projected * scale_ref[:, columns]).astype(BF16)
        kv = jnp.dot(projected, place_ref[:, :256], preferred_element_type=F32).astype(BF16)
        q = jnp.dot(projected[:128], place_ref[:, 256:512], preferred_element_type=F32)
        q = q + jnp.dot(projected[128:], place_ref[:, 512:], preferred_element_type=F32)
        q = q.astype(BF16)
        for side in range(2):
            kv_ref[2 * pair + side] = kv[:, 128 * side:128 * side + 128]
            q_ref[2 * pair + side] = q[:, 128 * side:128 * side + 128]


def project(points, gain, w_qkv):
    scale = np.ones((1, 1536), np.float32)
    scale[0, np.arange(1536) % 48 < 16] = HEAD_DIM ** -0.5 * math.log2(math.e)
    return pl.pallas_call(
        project_kernel,
        out_shape=(
            jax.ShapeDtypeStruct((GROUPS, TOK, LANES), BF16),
            jax.ShapeDtypeStruct((GROUPS, LANES, LANES), BF16),
        ),
        name="project",
    )(points, gain.reshape(1, D), w_qkv, jnp.asarray(scale), jnp.asarray(placing(), BF16))


def attend_kernel(
    slot_of, routes_ref, counts_ref, q_ref, kv_ref, out_ref,
    raw, keys, vals, lhs, acc, top, sems,
):
    column, _, head_index = swap_ids()
    seq = column * 8 + head_index
    core = lax.rem(head_index, 2)
    own_slot = slot_of(0, core) * NPL

    def source(patch, which):
        if which == 0:
            return own_slot + patch, seq * GROUPS + patch * 4
        row = seq * NPL * CB + patch * CB + which - 1
        route = routes_ref[0, row]
        offset = jnp.where(route < REACH, route - REACH, route - REACH + 1)
        local = routes_ref[1, row]
        owner = lax.rem(seq + offset + 32, 32)
        return slot_of(offset, core) * NPL + local, owner * GROUPS + local * 4

    for patch in range(NPL):
        for which in range(CB + 1):
            slot, _ = source(patch, which)
            pltpu.make_async_copy(kv_ref.at[slot], raw.at[patch * 3 + which], sems.at[patch * 3 + which]).start()

    lane_kv = lane_of((TOK, LANES))
    row_kv = lax.broadcasted_iota(jnp.int32, (TOK, LANES), 0)
    lane_q = lane_of((LANES, LANES))
    one = jnp.ones((TOK, LANES), BF16)
    zero = jnp.zeros((TOK, LANES), BF16)
    low_lane = lane_kv < 64
    sum_of = ((lane_of((LANES, LANES)) == (lax.broadcasted_iota(jnp.int32, (LANES, LANES), 0) // 16))).astype(BF16)
    sum_of = jnp.where(lane_q < 4, sum_of, jnp.zeros_like(sum_of))

    def patch_body(patch, _):
        for which in range(CB + 1):
            pltpu.make_async_copy(kv_ref.at[0], raw.at[patch * 3 + which], sems.at[patch * 3 + which]).wait()

        first = jnp.int32(0)
        key_top = jnp.zeros((1, LANES), F32)
        val_top = jnp.zeros((1, LANES), F32)
        for which in range(CB + 1):
            row = seq * NPL * CB + patch * CB + max(which - 1, 0)
            if which == 0:
                shard = seq * GROUPS + patch * 4
            else:
                route = routes_ref[0, row]
                offset = jnp.where(route < REACH, route - REACH, route - REACH + 1)
                shard = lax.rem(seq + offset + 32, 32) * GROUPS + routes_ref[1, row] * 4
            for part in range(4):
                count = counts_ref[shard + part]
                block = raw[patch * 3 + which, TOK * part:TOK * part + TOK, :]
                valid = row_kv < count
                flag = jnp.where(valid, zero, jnp.where(lane_kv < 66, jnp.full_like(zero, MASKED), zero))
                keyed = jnp.where(low_lane & valid, block, zero)
                at = pl.ds(pl.multiple_of(first, 16), TOK)
                keys[at, :] = jnp.where(low_lane, keyed, flag)
                vals[at, :] = jnp.where(low_lane, one, block)
                squares = jnp.dot(keyed * keyed, sum_of, preferred_element_type=F32)
                key_top = jnp.maximum(key_top, jnp.max(squares, axis=0, keepdims=True))
                size = jnp.max(jnp.where(low_lane, zero, jnp.abs(block)).astype(F32), axis=0, keepdims=True)
                val_top = jnp.maximum(val_top, size)
                first = first + (count + 15) // 16 * 16
        tail = pl.ds(pl.multiple_of(first, 16), TOK)
        keys[tail, :] = jnp.where(low_lane | (lane_kv >= 66), zero, jnp.full_like(zero, MASKED))
        vals[tail, :] = jnp.where(low_lane, one, zero)
        chunks = (first + CHUNK - 1) // CHUNK

        query_top = jnp.zeros((1, LANES), F32)
        for part in range(4):
            packed = q_ref[patch * 4 + part]
            for half in range(2):
                q = packed if half == 0 else pltpu.roll(packed.astype(F32), 64, 1).astype(BF16)
                q = jnp.where(lane_q < 64, q, jnp.zeros_like(q))
                squares = jnp.dot(q * q, sum_of, preferred_element_type=F32)
                query_top = jnp.maximum(query_top, jnp.max(squares, axis=0, keepdims=True))
        bound = jnp.max(query_top * key_top)
        small = (bound < 3000.0) & (jnp.max(val_top) < 1e9)

        def shard_body(part, _):
            packed = q_ref[patch * 4 + part]
            for half in range(2):
                q = packed if half == 0 else pltpu.roll(packed.astype(F32), 64, 1).astype(BF16)
                for head in range(4):
                    mine = (lane_q >= 16 * head) & (lane_q < 16 * head + 16)
                    flags = jnp.where((lane_q >= 64) & (lane_q < 66), jnp.ones_like(q), jnp.zeros_like(q))
                    lhs[pl.ds((half * 4 + head) * LANES, LANES), :] = jnp.where(mine, q, flags)
            acc[...] = jnp.zeros_like(acc)

            def scores_of(chunk):
                at = pl.ds(pl.multiple_of(chunk * CHUNK, CHUNK), CHUNK)
                return at, lax.dot_general(
                    lhs[...], keys[at, :], (((1,), (1,)), ((), ())), preferred_element_type=F32
                )

            @pl.when(small)
            def _():
                def chunk_body(chunk, _):
                    at, scores = scores_of(chunk)
                    weights = jnp.exp2(scores).astype(BF16)
                    acc[...] += jnp.dot(weights, vals[at, :], preferred_element_type=F32)
                    return 0

                lax.fori_loop(0, chunks, chunk_body, 0)

            @pl.when(jnp.logical_not(small))
            def _():
                top[...] = jnp.full_like(top, -jnp.inf)

                def top_body(chunk, _):
                    _, scores = scores_of(chunk)
                    top[...] = jnp.maximum(top[...], jnp.max(scores, axis=1, keepdims=True))
                    return 0

                lax.fori_loop(0, chunks, top_body, 0)

                def chunk_body(chunk, _):
                    at, scores = scores_of(chunk)
                    weights = jnp.exp2(scores - top[:, :1]).astype(BF16)
                    acc[...] += jnp.dot(weights, vals[at, :], preferred_element_type=F32)
                    return 0

                lax.fori_loop(0, chunks, chunk_body, 0)

            halves = []
            for half in range(2):
                joined = jnp.zeros((LANES, LANES), F32)
                for head in range(4):
                    part_acc = acc[pl.ds((half * 4 + head) * LANES, LANES), :]
                    mine = (lane_q >= 64 + 16 * head) & (lane_q < 80 + 16 * head)
                    joined = jnp.where(mine, part_acc / pltpu.roll(part_acc, 64, 1), joined)
                halves.append(joined)
            out_ref[patch * 4 + part] = (pltpu.roll(halves[0], 64, 1) + halves[1]).astype(BF16)
            return 0

        lax.fori_loop(0, 4, shard_body, 0)
        return 0

    lax.fori_loop(0, NPL, patch_body, 0)


def attend(slot_of, routes, counts, q, kv):
    smem = pl.BlockSpec(memory_space=pltpu.SMEM)
    vmem = pl.BlockSpec(memory_space=pltpu.VMEM)
    return pl.pallas_call(
        functools.partial(attend_kernel, slot_of),
        out_shape=jax.ShapeDtypeStruct((GROUPS, LANES, LANES), BF16),
        in_specs=[smem, smem, vmem, pl.BlockSpec(memory_space=pl.ANY)],
        out_specs=vmem,
        scratch_shapes=[
            pltpu.VMEM((6, PATCH, LANES), BF16),
            pltpu.VMEM((3 * PATCH + TOK, LANES), BF16),
            pltpu.VMEM((3 * PATCH + TOK, LANES), BF16),
            pltpu.VMEM((ROWS, LANES), BF16),
            pltpu.VMEM((ROWS, LANES), F32),
            pltpu.VMEM((ROWS, LANES), F32),
            pltpu.SemaphoreType.DMA((6,)),
        ],
        compiler_params=pltpu.CompilerParams(vmem_limit_bytes=40 << 20),
        name="attend",
    )(routes, counts, q, kv)


def finish_kernel(points_ref, packed_ref, w_out_ref, gain_ref, w1_ref, w2_ref, out_ref):
    lane = lane_of((LANES, LANES))
    low, high = [], []
    for pair in range(GROUPS // 2):
        first, second = packed_ref[2 * pair].astype(F32), packed_ref[2 * pair + 1].astype(F32)
        low.append(jnp.where(lane < 64, first, pltpu.roll(second, 64, 1)))
        high.append(jnp.where(lane < 64, pltpu.roll(first, 64, 1), second))
    attended = jnp.concatenate([jnp.concatenate(low, axis=1), jnp.concatenate(high, axis=1)], axis=0)
    updated = points_ref[...].astype(F32) + jnp.dot(
        attended.astype(BF16), w_out_ref[...], preferred_element_type=F32
    )
    updated = updated.astype(BF16).astype(F32)
    normed = normalise(updated, gain_ref[...]).astype(BF16)
    total = updated
    for part in range(GROUPS):
        hidden = jnp.dot(normed, w1_ref[part], preferred_element_type=F32)
        hidden = hidden * (0.5 * (1.0 + lax.erf(hidden * (2.0 ** -0.5))))
        total = total + jnp.dot(hidden.astype(BF16), w2_ref[part], preferred_element_type=F32)
    out_ref[...] = total.astype(BF16)


def finish(points, packed, w_out, gain, w1, w2):
    return pl.pallas_call(
        finish_kernel,
        out_shape=jax.ShapeDtypeStruct((TOK, D), BF16),
        compiler_params=pltpu.CompilerParams(vmem_limit_bytes=40 << 20),
        name="finish",
    )(points, packed, w_out, gain.reshape(1, D), w1, w2)


def swap_ids():
    seq, head = lax.axis_index("seq"), lax.axis_index("head")
    column = seq // 8
    return column, seq - column * 8, head


def exchange_kernel(
    kv_ref, q_ref, route_ref, kv_out, q_out, route_out,
    all_send, all_recv, ring_send, ring_recv, pair_send, pair_recv, route_sem, local_sem,
):
    column, plane, head = swap_ids()
    core = lax.rem(head, 2)
    spot = column * 4 + head // 2
    after, before = lax.rem(spot + 1, 16), lax.rem(spot + 15, 16)
    right = ((after // 4) * 8 + plane, lax.rem(after, 4) * 2 + core)
    left = ((before // 4) * 8 + plane, lax.rem(before, 4) * 2 + core)
    pair = (column * 8 + plane, head + 1 - 2 * core)
    partner = (column * 8 + head, plane)
    diagonal = plane == head
    across = jnp.logical_not(diagonal)

    barrier = pltpu.get_barrier_semaphore()

    def greet(index, _):
        @pl.when(across | (index != head))
        def _():
            pl.semaphore_signal(barrier, inc=1, device_id=(column * 8 + head, index), device_id_type=MESH)
        return 0

    lax.fori_loop(0, 8, greet, 0)
    for other in (right, left, pair):
        pl.semaphore_signal(barrier, inc=1, device_id=other, device_id_type=MESH)

    @pl.when(diagonal)
    def _():
        pl.semaphore_wait(barrier, 10)

    @pl.when(across)
    def _():
        pl.semaphore_wait(barrier, 11)

    def rows(half):
        return pl.ds(half * LANES, LANES)

    def spread(group, half, shard):
        return pltpu.make_async_remote_copy(
            src_ref=kv_ref.at[group, rows(half)],
            dst_ref=kv_out.at[4 + lax.rem(plane, 2), shard, rows(half)],
            send_sem=all_send.at[half, group],
            recv_sem=all_recv.at[half, shard],
            device_id=(column * 8 + group, plane),
            device_id_type=MESH,
        )

    def landed(half, shard):
        return pltpu.make_async_remote_copy(
            src_ref=kv_ref.at[0, rows(half)],
            dst_ref=kv_out.at[4 + core, shard, rows(half)],
            send_sem=all_send.at[half, 0],
            recv_sem=all_recv.at[half, shard],
            device_id=pair,
            device_id_type=MESH,
        )

    def spread_q(group, shard):
        return pltpu.make_async_remote_copy(
            src_ref=q_ref.at[group],
            dst_ref=q_out.at[shard],
            send_sem=all_send.at[2, group],
            recv_sem=all_recv.at[2, shard],
            device_id=(column * 8 + group, plane),
            device_id_type=MESH,
        )

    def at_home(half):
        return pltpu.make_async_copy(
            kv_ref.at[plane, rows(half)], kv_out.at[4 + core, head, rows(half)], local_sem.at[half]
        )

    q_at_home = pltpu.make_async_copy(q_ref.at[plane], q_out.at[head], local_sem.at[2])
    route_at_home = pltpu.make_async_copy(route_ref, route_out, local_sem.at[3])
    route_sent = pltpu.make_async_remote_copy(
        src_ref=route_ref, dst_ref=route_out, send_sem=route_sem.at[0], recv_sem=route_sem.at[1],
        device_id=partner, device_id_type=MESH,
    )

    def each(body):
        def step(index, _):
            body(index)
            return 0

        lax.fori_loop(0, 8, step, 0)

    for half in range(2):
        def start(group):
            @pl.when(across | (group != plane))
            def _():
                spread(group, half, head).start()

        each(start)

    def start_q(group):
        @pl.when(across | (group != plane))
        def _():
            spread_q(group, head).start()

    each(start_q)

    @pl.when(diagonal)
    def _():
        at_home(0).start()
        at_home(1).start()
        q_at_home.start()
        route_at_home.start()

    @pl.when(across)
    def _():
        route_sent.start()

    def moved(source, target, half, send, recv, to):
        return pltpu.make_async_remote_copy(
            src_ref=kv_out.at[source, :, rows(half)], dst_ref=kv_out.at[target, :, rows(half)],
            send_sem=send, recv_sem=recv, device_id=to, device_id_type=MESH,
        )

    def hop(way, step, half):
        if way == 0:
            source, to = 4 - 2 * step + core, right
            target = 2 - 2 * step + core
        else:
            source, to = 4 + 2 * step + core, left
            target = 6 + 2 * step + core
        return moved(source, target, half, ring_send.at[way, step, half], ring_recv.at[way, step, half], to)

    def shared(place, half):
        return moved(2 * place + core, 2 * place + core, half, pair_send.at[place, half], pair_recv.at[place, half], pair)

    def taken(place, half):
        return moved(2 * place + 1 - core, 2 * place + 1 - core, half, pair_send.at[place, half], pair_recv.at[place, half], pair)

    for half in range(2):
        def wait(shard):
            @pl.when(across | (shard != head))
            def _():
                landed(half, shard).wait_recv()

        each(wait)

        @pl.when(diagonal)
        def _():
            at_home(half).wait()

        hop(0, 0, half).start()
        hop(1, 0, half).start()
        shared(2, half).start()
    for half in range(2):
        hop(0, 0, half).wait_recv()
        hop(0, 1, half).start()
        hop(1, 0, half).wait_recv()
        hop(1, 1, half).start()
        shared(1, half).start()
        shared(3, half).start()
    for half in range(2):
        hop(0, 1, half).wait_recv()
        shared(0, half).start()
        hop(1, 1, half).wait_recv()
        shared(4, half).start()

    def wait_q(shard):
        @pl.when(across | (shard != head))
        def _():
            spread_q(0, shard).wait_recv()

    each(wait_q)

    def sent(group):
        @pl.when(across | (group != plane))
        def _():
            spread(group, 0, head).wait_send()
            spread(group, 1, head).wait_send()
            spread_q(group, head).wait_send()

    each(sent)

    @pl.when(diagonal)
    def _():
        q_at_home.wait()
        route_at_home.wait()

    @pl.when(across)
    def _():
        route_sent.wait()

    for half in range(2):
        for way in range(2):
            for step in range(2):
                hop(way, step, half).wait_send()
        for place in range(5):
            shared(place, half).wait_send()
            taken(place, half).wait_recv()


def exchange(kv, q, routes):
    anywhere = pl.BlockSpec(memory_space=pl.ANY)
    return pl.pallas_call(
        exchange_kernel,
        out_shape=(
            jax.ShapeDtypeStruct((10, GROUPS, TOK, LANES), BF16),
            jax.ShapeDtypeStruct((GROUPS, LANES, LANES), BF16),
            jax.ShapeDtypeStruct((8, LANES), jnp.int32),
        ),
        in_specs=[anywhere] * 3,
        out_specs=(anywhere,) * 3,
        scratch_shapes=[
            pltpu.SemaphoreType.DMA((3, 8)),
            pltpu.SemaphoreType.DMA((3, 8)),
            pltpu.SemaphoreType.DMA((2, 2, 2)),
            pltpu.SemaphoreType.DMA((2, 2, 2)),
            pltpu.SemaphoreType.DMA((5, 2)),
            pltpu.SemaphoreType.DMA((5, 2)),
            pltpu.SemaphoreType.DMA((2,)),
            pltpu.SemaphoreType.DMA((4,)),
        ],
        compiler_params=pltpu.CompilerParams(collective_id=0, has_side_effects=True),
        name="exchange",
    )(kv, q, routes)


def give_back_kernel(packed_ref, out_ref, send, recv, local_sem):
    column, plane, head = swap_ids()
    diagonal = plane == head
    across = jnp.logical_not(diagonal)
    barrier = pltpu.get_barrier_semaphore()

    def each(body):
        def step(index, _):
            body(index)
            return 0

        lax.fori_loop(0, 8, step, 0)

    def greet(group):
        @pl.when(across | (group != plane))
        def _():
            pl.semaphore_signal(barrier, inc=1, device_id=(column * 8 + group, plane), device_id_type=MESH)

    each(greet)

    @pl.when(diagonal)
    def _():
        pl.semaphore_wait(barrier, 7)

    @pl.when(across)
    def _():
        pl.semaphore_wait(barrier, 8)

    def copy(shard, group):
        return pltpu.make_async_remote_copy(
            src_ref=packed_ref.at[shard], dst_ref=out_ref.at[group],
            send_sem=send.at[shard], recv_sem=recv.at[group],
            device_id=(column * 8 + head, shard), device_id_type=MESH,
        )

    at_home = pltpu.make_async_copy(packed_ref.at[head], out_ref.at[plane], local_sem.at[0])

    def start(shard):
        @pl.when(across | (shard != head))
        def _():
            copy(shard, plane).start()

    each(start)

    @pl.when(diagonal)
    def _():
        at_home.start()
        at_home.wait()

    def wait(index):
        @pl.when(across | (index != plane))
        def _():
            copy(0, index).wait_recv()

        @pl.when(across | (index != head))
        def _():
            copy(index, plane).wait_send()

    each(wait)


def give_back(packed):
    vmem = pl.BlockSpec(memory_space=pltpu.VMEM)
    return pl.pallas_call(
        give_back_kernel,
        out_shape=jax.ShapeDtypeStruct((GROUPS, LANES, LANES), BF16),
        in_specs=[vmem],
        out_specs=vmem,
        scratch_shapes=[
            pltpu.SemaphoreType.DMA((8,)), pltpu.SemaphoreType.DMA((8,)), pltpu.SemaphoreType.DMA((1,)),
        ],
        compiler_params=pltpu.CompilerParams(collective_id=1, has_side_effects=True),
        name="give_back",
    )(packed)


def per_device(
    points, gain_attn, w_qkv, w_out, gain_mlp, w_fc1, w_fc2, contact_route, contact_patch, counts
):
    w1 = lax.all_gather(w_fc1, "head", axis=0)
    w2 = lax.all_gather(w_fc2, "head", axis=0)
    routes = jnp.concatenate([contact_route.reshape(1, -1), contact_patch, jnp.zeros((6, LANES), jnp.int32)])
    kv, q = project(points, gain_attn, w_qkv)
    slots, q, routes = exchange(kv, q, routes)
    packed = attend(
        lambda offset, core: offset + REACH + core, routes, counts, q, slots.reshape(20, PATCH, LANES)
    )
    packed = give_back(packed)
    return finish(points, packed, w_out, gain_mlp, w1, w2)


def solution(mesh):
    return jax.shard_map(
        per_device,
        mesh=mesh,
        in_specs=(
            P(("seq", "head"), None), P(), P(), P(), P(), P(None, "head"), P("head", None),
            P("head", None, None), P("head", None), P(),
        ),
        out_specs=P(("seq", "head"), None),
        check_vma=False,
    )
```

```python
import functools
import math

import jax
import jax.numpy as jnp
import numpy as np
from jax import lax
from jax.experimental import pallas as pl
from jax.experimental.pallas import tpu as pltpu
from jax.sharding import PartitionSpec as P

D = 512
HEADS = 32
HEAD_DIM = 16
PATCH = 1024
CB = 2
NPL = 2
REACH = 4
TOK = 256
GROUPS = 8
LANES = 128
CHUNK = 512
F32 = jnp.float32
BF16 = jnp.bfloat16
MASKED = -3.3e38
ROWS = 8 * LANES
MESH = pl.DeviceIdType.MESH


def placing():
    kv = np.zeros((384, 256), np.float32)
    low = np.zeros((384, 256), np.float32)
    high = np.zeros((384, 256), np.float32)
    for group in range(2):
        for head in range(4):
            for dim in range(HEAD_DIM):
                source = group * 192 + head * 48 + dim
                lane = group * 128 + head * 16 + dim
                low[source, lane] = 1
                high[source, lane + 64] = 1
                kv[source + 16, lane] = 1
                kv[source + 32, lane + 64] = 1
    return np.concatenate([kv, low, high], axis=1)


def lane_of(shape):
    return lax.broadcasted_iota(jnp.int32, shape, len(shape) - 1)


def normalise(values, gain):
    centred = values - jnp.mean(values, axis=-1, keepdims=True)
    spread = jnp.mean(centred * centred, axis=-1, keepdims=True)
    return centred * lax.rsqrt(spread + 1e-05) * gain


def project_kernel(points_ref, gain_ref, w_ref, scale_ref, place_ref, kv_ref, q_ref):
    normed = normalise(points_ref[...].astype(F32), gain_ref[...]).astype(BF16)
    for pair in range(GROUPS // 2):
        columns = slice(384 * pair, 384 * pair + 384)
        projected = jnp.dot(normed, w_ref[:, columns], preferred_element_type=F32)
        projected = (projected * scale_ref[:, columns]).astype(BF16)
        kv = jnp.dot(projected, place_ref[:, :256], preferred_element_type=F32).astype(BF16)
        q = jnp.dot(projected[:128], place_ref[:, 256:512], preferred_element_type=F32)
        q = q + jnp.dot(projected[128:], place_ref[:, 512:], preferred_element_type=F32)
        q = q.astype(BF16)
        for side in range(2):
            kv_ref[2 * pair + side] = kv[:, 128 * side:128 * side + 128]
            q_ref[2 * pair + side] = q[:, 128 * side:128 * side + 128]


def project(points, gain, w_qkv):
    scale = np.ones((1, 1536), np.float32)
    scale[0, np.arange(1536) % 48 < 16] = HEAD_DIM ** -0.5 * math.log2(math.e)
    return pl.pallas_call(
        project_kernel,
        out_shape=(
            jax.ShapeDtypeStruct((GROUPS, TOK, LANES), BF16),
            jax.ShapeDtypeStruct((GROUPS, LANES, LANES), BF16),
        ),
        name="project",
    )(points, gain.reshape(1, D), w_qkv, jnp.asarray(scale), jnp.asarray(placing(), BF16))


def swap_ids():
    seq, head = lax.axis_index("seq"), lax.axis_index("head")
    column = seq // 8
    return column, seq - column * 8, head


def attend_kernel(
    routes_hbm, local_hbm, counts_hbm, q_hbm, kv_ref, out_ref,
    routes_ref, local_ref, counts_ref, q_ref, raw, keys, vals, turned, lhs, acc, top, done, sems, small_sems, out_sems,
):
    column, _, head_index = swap_ids()
    seq = column * 8 + head_index
    core = lax.rem(head_index, 2)
    loads = [
        pltpu.make_async_copy(routes_hbm, routes_ref, small_sems.at[0]),
        pltpu.make_async_copy(local_hbm, local_ref, small_sems.at[1]),
        pltpu.make_async_copy(counts_hbm, counts_ref, small_sems.at[2]),
        pltpu.make_async_copy(q_hbm, q_ref, small_sems.at[3]),
    ]
    for load in loads:
        load.start()
    for load in loads[:3]:
        load.wait()

    def source(patch, which):
        if which == 0:
            return (REACH + core) * NPL + patch, seq * GROUPS + patch * 4
        row = seq * NPL * CB + patch * CB + which - 1
        route = routes_ref[0, row]
        offset = jnp.where(route < REACH, route - REACH, route - REACH + 1)
        local = local_ref[0, row]
        owner = lax.rem(seq + offset + 32, 32)
        return (offset + REACH + core) * NPL + local, owner * GROUPS + local * 4

    for patch in range(NPL):
        for which in range(CB + 1):
            slot, _ = source(patch, which)
            pltpu.make_async_copy(kv_ref.at[slot], raw.at[patch * 3 + which], sems.at[patch * 3 + which]).start()
    loads[3].wait()

    lane_kv = lane_of((TOK, LANES))
    row_kv = lax.broadcasted_iota(jnp.int32, (TOK, LANES), 0)
    lane_q = lane_of((LANES, LANES))
    row_q = lax.broadcasted_iota(jnp.int32, (LANES, LANES), 0)
    zero = jnp.zeros((TOK, LANES), BF16)
    low_lane = lane_kv < 64
    sum_of = ((lane_q == row_q // 16) & (lane_q < 4)).astype(F32).astype(BF16)
    value_of = ((row_q % 32 < 16) & (lane_q == 64 + row_q // 32 * 16 + row_q % 32)).astype(F32).astype(BF16)
    ones_row = lax.broadcasted_iota(jnp.int32, (LANES, CHUNK), 0) % 32 >= 16

    def patch_body(patch, _):
        for which in range(CB + 1):
            pltpu.make_async_copy(kv_ref.at[0], raw.at[patch * 3 + which], sems.at[patch * 3 + which]).wait()

        first = jnp.int32(0)
        key_top = jnp.zeros((1, LANES), F32)
        val_top = jnp.zeros((1, LANES), F32)
        for which in range(CB + 1):
            _, shard = source(patch, which)
            for part in range(4):
                count = counts_ref[shard + part]
                block = raw[patch * 3 + which, TOK * part:TOK * part + TOK, :]
                valid = row_kv < count
                flag = jnp.where(valid, zero, jnp.where(lane_kv < 66, jnp.full_like(zero, MASKED), zero))
                keyed = jnp.where(low_lane & valid, block, zero)
                at = pl.ds(pl.multiple_of(first, 16), TOK)
                keys[at, :] = jnp.where(low_lane, keyed, flag)
                vals[at, :] = block
                squares = jnp.dot(keyed * keyed, sum_of, preferred_element_type=F32)
                key_top = jnp.maximum(key_top, jnp.max(squares, axis=0, keepdims=True))
                size = jnp.max(jnp.where(low_lane, zero, jnp.abs(block)).astype(F32), axis=0, keepdims=True)
                val_top = jnp.maximum(val_top, size)
                first = first + (count + 15) // 16 * 16
        for more in range(CHUNK // TOK):
            tail = pl.ds(pl.multiple_of(first + more * TOK, 16), TOK)
            keys[tail, :] = jnp.where(low_lane | (lane_kv >= 66), zero, jnp.full_like(zero, MASKED))
            vals[tail, :] = zero
        chunks = (first + CHUNK - 1) // CHUNK

        def turn(chunk, _):
            at = pl.ds(pl.multiple_of(chunk * CHUNK, CHUNK), CHUNK)
            picked = lax.dot_general(value_of, vals[at, :], (((1,), (1,)), ((), ())), preferred_element_type=F32)
            turned[:, at] = jnp.where(ones_row, 1.0, picked).astype(BF16)
            return 0

        lax.fori_loop(0, chunks, turn, 0)

        query_top = jnp.zeros((1, LANES), F32)
        for part in range(4):
            packed = q_ref[patch * 4 + part]
            for half in range(2):
                q = packed if half == 0 else pltpu.roll(packed.astype(F32), 64, 1).astype(BF16)
                q = jnp.where(lane_q < 64, q, jnp.zeros_like(q))
                squares = jnp.dot(q * q, sum_of, preferred_element_type=F32)
                query_top = jnp.maximum(query_top, jnp.max(squares, axis=0, keepdims=True))
        bound = jnp.max(query_top * key_top)
        small = (bound < 3000.0) & (jnp.max(val_top) < 1e9)

        def shard_body(part, _):
            packed = q_ref[patch * 4 + part]
            flags = jnp.where((lane_q >= 64) & (lane_q < 66), jnp.ones_like(packed), jnp.zeros_like(packed))
            for half in range(2):
                q = packed if half == 0 else pltpu.roll(packed.astype(F32), 64, 1).astype(BF16)
                for head in range(4):
                    mine = (lane_q >= 16 * head) & (lane_q < 16 * head + 16)
                    lhs[pl.ds((head * 2 + half) * LANES, LANES), :] = jnp.where(mine, q, flags)
            acc[...] = jnp.zeros_like(acc)

            def scores_of(chunk):
                at = pl.ds(pl.multiple_of(chunk * CHUNK, CHUNK), CHUNK)
                return at, lax.dot_general(
                    keys[at, :], lhs[...], (((1,), (1,)), ((), ())), preferred_element_type=F32
                )

            def gather(at, weights):
                for head in range(4):
                    rows = slice(32 * head, 32 * head + 32)
                    acc[rows] += jnp.dot(
                        turned[rows, at], weights[:, TOK * head:TOK * head + TOK], preferred_element_type=F32
                    )

            @pl.when(small)
            def _():
                def chunk_body(chunk, _):
                    at, scores = scores_of(chunk)
                    gather(at, jnp.exp2(scores).astype(BF16))
                    return 0

                lax.fori_loop(0, chunks, chunk_body, 0)

            @pl.when(jnp.logical_not(small))
            def _():
                top[...] = jnp.full_like(top, -jnp.inf)

                def top_body(chunk, _):
                    _, scores = scores_of(chunk)
                    top[...] = jnp.maximum(top[...], jnp.max(scores, axis=0, keepdims=True))
                    return 0

                lax.fori_loop(0, chunks, top_body, 0)

                def chunk_body(chunk, _):
                    at, scores = scores_of(chunk)
                    gather(at, jnp.exp2(scores - top[...]).astype(BF16))
                    return 0

                lax.fori_loop(0, chunks, chunk_body, 0)

            joined = [acc[32 * head:32 * head + 16] / acc[32 * head + 16:32 * head + 32] for head in range(4)]
            done[patch * 4 + part] = jnp.concatenate(joined, axis=0).astype(BF16)
            pltpu.make_async_copy(
                done.at[patch * 4 + part], out_ref.at[patch * 4 + part], out_sems.at[patch * 4 + part]
            ).start()
            return 0

        lax.fori_loop(0, 4, shard_body, 0)
        return 0

    lax.fori_loop(0, NPL, patch_body, 0)
    for shard in range(GROUPS):
        pltpu.make_async_copy(done.at[shard], out_ref.at[shard], out_sems.at[shard]).wait()


def attend(routes, local, counts, q, kv):
    hbm = pl.BlockSpec(memory_space=pltpu.HBM)
    return pl.pallas_call(
        attend_kernel,
        out_shape=jax.ShapeDtypeStruct((GROUPS, 64, TOK), BF16),
        in_specs=[hbm] * 5,
        out_specs=hbm,
        scratch_shapes=[
            pltpu.SMEM((1, LANES), jnp.int32),
            pltpu.SMEM((1, LANES), jnp.int32),
            pltpu.SMEM((256,), jnp.int32),
            pltpu.VMEM((GROUPS, LANES, LANES), BF16),
            pltpu.VMEM((6, PATCH, LANES), BF16),
            pltpu.VMEM((3 * PATCH + CHUNK, LANES), BF16),
            pltpu.VMEM((3 * PATCH + CHUNK, LANES), BF16),
            pltpu.VMEM((LANES, 3 * PATCH + CHUNK), BF16),
            pltpu.VMEM((ROWS, LANES), BF16),
            pltpu.VMEM((LANES, TOK), F32),
            pltpu.VMEM((1, ROWS), F32),
            pltpu.VMEM((GROUPS, 64, TOK), BF16),
            pltpu.SemaphoreType.DMA((6,)),
            pltpu.SemaphoreType.DMA((4,)),
            pltpu.SemaphoreType.DMA((8,)),
        ],
        compiler_params=pltpu.CompilerParams(vmem_limit_bytes=40 << 20),
        name="attend",
    )(routes, local, counts, q, kv)


def each(body):
    def step(index, _):
        body(index)
        return 0

    lax.fori_loop(0, 8, step, 0)


def finish_kernel(
    points_ref, packed_ref, w_out_ref, gain_ref, w1_ref, w2_ref, out_ref,
    points, w_out, gain, w1, w2, back, send, recv, local_sem, load_sem, weight_sem,
):
    column, plane, head = swap_ids()
    diagonal = plane == head
    across = jnp.logical_not(diagonal)
    barrier = pltpu.get_barrier_semaphore()

    def greet(group):
        @pl.when(across | (group != plane))
        def _():
            pl.semaphore_signal(barrier, inc=1, device_id=(column * 8 + group, plane), device_id_type=MESH)

    each(greet)
    loads = [
        pltpu.make_async_copy(points_ref, points, load_sem.at[0]),
        pltpu.make_async_copy(w_out_ref, w_out, load_sem.at[1]),
        pltpu.make_async_copy(gain_ref, gain, load_sem.at[2]),
    ]
    for load in loads:
        load.start()

    def weights(part):
        return (
            pltpu.make_async_copy(w1_ref.at[part], w1.at[part], weight_sem.at[0, part]),
            pltpu.make_async_copy(w2_ref.at[part], w2.at[part], weight_sem.at[1, part]),
        )

    for part in range(GROUPS):
        for copy in weights(part):
            copy.start()

    @pl.when(diagonal)
    def _():
        pl.semaphore_wait(barrier, 7)

    @pl.when(across)
    def _():
        pl.semaphore_wait(barrier, 8)

    def copy(shard, group):
        return pltpu.make_async_remote_copy(
            src_ref=packed_ref.at[shard], dst_ref=back.at[group],
            send_sem=send.at[shard], recv_sem=recv.at[group],
            device_id=(column * 8 + head, shard), device_id_type=MESH,
        )

    at_home = pltpu.make_async_copy(packed_ref.at[head], back.at[plane], local_sem.at[0])

    def start(shard):
        @pl.when(across | (shard != head))
        def _():
            copy(shard, plane).start()

    each(start)

    @pl.when(diagonal)
    def _():
        at_home.start()
        at_home.wait()

    for load in loads:
        load.wait()

    def wait(index):
        @pl.when(across | (index != plane))
        def _():
            copy(0, index).wait_recv()

    each(wait)

    attended = back[...].reshape(D, TOK)
    updated = points[...].astype(F32) + lax.dot_general(
        attended, w_out[...], (((0,), (0,)), ((), ())), preferred_element_type=F32
    )
    updated = updated.astype(BF16).astype(F32)
    normed = normalise(updated, gain[...]).astype(BF16)
    total = updated
    for part in range(GROUPS):
        for load in weights(part):
            load.wait()
        hidden = jnp.dot(normed, w1[part], preferred_element_type=F32)
        hidden = hidden * (0.5 * (1.0 + lax.erf(hidden * (2.0 ** -0.5))))
        total = total + jnp.dot(hidden.astype(BF16), w2[part], preferred_element_type=F32)
    out_ref[...] = total.astype(BF16)

    def sent(index):
        @pl.when(across | (index != head))
        def _():
            copy(index, plane).wait_send()

    each(sent)


def finish(points, packed, w_out, gain, w1, w2):
    hbm = pl.BlockSpec(memory_space=pltpu.HBM)
    return pl.pallas_call(
        finish_kernel,
        out_shape=jax.ShapeDtypeStruct((TOK, D), BF16),
        in_specs=[hbm] * 6,
        out_specs=pl.BlockSpec(memory_space=pltpu.VMEM),
        scratch_shapes=[
            pltpu.VMEM((TOK, D), BF16),
            pltpu.VMEM((D, D), BF16),
            pltpu.VMEM((1, D), F32),
            pltpu.VMEM((GROUPS, D, 256), BF16),
            pltpu.VMEM((GROUPS, 256, D), BF16),
            pltpu.VMEM((GROUPS, 64, TOK), BF16),
            pltpu.SemaphoreType.DMA((8,)),
            pltpu.SemaphoreType.DMA((8,)),
            pltpu.SemaphoreType.DMA((1,)),
            pltpu.SemaphoreType.DMA((3,)),
            pltpu.SemaphoreType.DMA((2, 8)),
        ],
        compiler_params=pltpu.CompilerParams(
            collective_id=1, has_side_effects=True, vmem_limit_bytes=40 << 20
        ),
        name="finish",
    )(points, packed, w_out, gain.reshape(1, D), w1, w2)


def exchange_kernel(
    kv_ref, q_ref, route_ref, local_ref, w1_ref, w2_ref, kv_out, q_out, route_out, local_out, w1_out, w2_out,
    all_send, all_recv, ring_send, ring_recv, pair_send, pair_recv, route_sem, local_sem,
    down_send, down_recv, over_send, over_recv, share_send, share_recv,
):
    column, plane, head = swap_ids()
    core = lax.rem(head, 2)
    spot = column * 4 + head // 2
    after, before = lax.rem(spot + 1, 16), lax.rem(spot + 15, 16)
    right = ((after // 4) * 8 + plane, lax.rem(after, 4) * 2 + core)
    left = ((before // 4) * 8 + plane, lax.rem(before, 4) * 2 + core)
    pair = (column * 8 + plane, head + 1 - 2 * core)
    partner = (column * 8 + head, plane)
    diagonal = plane == head
    across = jnp.logical_not(diagonal)

    barrier = pltpu.get_barrier_semaphore()

    def greet(index, _):
        @pl.when(across | (index != head))
        def _():
            pl.semaphore_signal(barrier, inc=1, device_id=(column * 8 + head, index), device_id_type=MESH)
        return 0

    lax.fori_loop(0, 8, greet, 0)
    level = head // 2
    downs = [(column * 8 + plane, lax.rem(level + step, 4) * 2 + core) for step in range(1, 4)]
    overs = [(lax.rem(column + step, 4) * 8 + plane, head) for step in range(1, 4)]
    for other in (right, left, pair, *downs, *overs):
        pl.semaphore_signal(barrier, inc=1, device_id=other, device_id_type=MESH)

    @pl.when(diagonal)
    def _():
        pl.semaphore_wait(barrier, 16)

    @pl.when(across)
    def _():
        pl.semaphore_wait(barrier, 17)

    def rows(half):
        return pl.ds(half * LANES, LANES)

    def spread(group, half, shard):
        return pltpu.make_async_remote_copy(
            src_ref=kv_ref.at[group, rows(half)],
            dst_ref=kv_out.at[4 + lax.rem(plane, 2), shard, rows(half)],
            send_sem=all_send.at[half, group],
            recv_sem=all_recv.at[half, shard],
            device_id=(column * 8 + group, plane),
            device_id_type=MESH,
        )

    def landed(half, shard):
        return pltpu.make_async_remote_copy(
            src_ref=kv_ref.at[0, rows(half)],
            dst_ref=kv_out.at[4 + core, shard, rows(half)],
            send_sem=all_send.at[half, 0],
            recv_sem=all_recv.at[half, shard],
            device_id=pair,
            device_id_type=MESH,
        )

    def spread_q(group, shard):
        return pltpu.make_async_remote_copy(
            src_ref=q_ref.at[group],
            dst_ref=q_out.at[shard],
            send_sem=all_send.at[2, group],
            recv_sem=all_recv.at[2, shard],
            device_id=(column * 8 + group, plane),
            device_id_type=MESH,
        )

    def at_home(half):
        return pltpu.make_async_copy(
            kv_ref.at[plane, rows(half)], kv_out.at[4 + core, head, rows(half)], local_sem.at[half]
        )

    q_at_home = pltpu.make_async_copy(q_ref.at[plane], q_out.at[head], local_sem.at[2])
    routes_at_home = [
        pltpu.make_async_copy(route_ref, route_out, local_sem.at[3]),
        pltpu.make_async_copy(local_ref, local_out, local_sem.at[4]),
    ]
    routes_sent = [
        pltpu.make_async_remote_copy(
            src_ref=source, dst_ref=target, send_sem=route_sem.at[0, index], recv_sem=route_sem.at[1, index],
            device_id=partner, device_id_type=MESH,
        )
        for index, (source, target) in enumerate(((route_ref, route_out), (local_ref, local_out)))
    ]

    slabs = (
        (w1_ref, w1_out, pl.ds(column * LANES, LANES)),
        (w2_ref, w2_out, pl.ds(column * 64, 64)),
    )
    weights_at_home = [
        pltpu.make_async_copy(source, target.at[core, level], local_sem.at[5 + index])
        for index, (source, target, _) in enumerate(slabs)
    ]

    def down(index, step):
        source, target, quarter = slabs[index]
        return pltpu.make_async_remote_copy(
            src_ref=source.at[quarter], dst_ref=target.at[core, level, quarter],
            send_sem=down_send.at[index, step - 1], recv_sem=down_recv.at[index, step - 1],
            device_id=downs[step - 1], device_id_type=MESH,
        )

    def over(index, rise, step):
        _, target, quarter = slabs[index]
        spot_of = target.at[core, lax.rem(level + 4 - rise, 4), quarter]
        return pltpu.make_async_remote_copy(
            src_ref=spot_of, dst_ref=spot_of,
            send_sem=over_send.at[index, rise - 1, step - 1], recv_sem=over_recv.at[index, rise - 1, step - 1],
            device_id=overs[step - 1], device_id_type=MESH,
        )

    def share(index):
        _, target, _ = slabs[index]
        return pltpu.make_async_remote_copy(
            src_ref=target.at[core], dst_ref=target.at[core],
            send_sem=share_send.at[index], recv_sem=share_recv.at[index], device_id=pair, device_id_type=MESH,
        )

    for index in range(2):
        weights_at_home[index].start()
        for step in range(1, 4):
            down(index, step).start()

    for half in range(2):
        def start(group):
            @pl.when(across | (group != plane))
            def _():
                spread(group, half, head).start()

        each(start)

    def start_q(group):
        @pl.when(across | (group != plane))
        def _():
            spread_q(group, head).start()

    each(start_q)

    @pl.when(diagonal)
    def _():
        at_home(0).start()
        at_home(1).start()
        q_at_home.start()
        for copy in routes_at_home:
            copy.start()

    @pl.when(across)
    def _():
        for copy in routes_sent:
            copy.start()

    for rise in range(1, 4):
        for index in range(2):
            down(index, rise).wait_recv()
            for step in range(1, 4):
                over(index, rise, step).start()

    def moved(source, target, half, send, recv, to):
        return pltpu.make_async_remote_copy(
            src_ref=kv_out.at[source, :, rows(half)], dst_ref=kv_out.at[target, :, rows(half)],
            send_sem=send, recv_sem=recv, device_id=to, device_id_type=MESH,
        )

    def hop(way, step, half):
        if way == 0:
            source, to = 4 - 2 * step + core, right
            target = 2 - 2 * step + core
        else:
            source, to = 4 + 2 * step + core, left
            target = 6 + 2 * step + core
        return moved(source, target, half, ring_send.at[way, step, half], ring_recv.at[way, step, half], to)

    def shared(place, half):
        return moved(2 * place + core, 2 * place + core, half, pair_send.at[place, half], pair_recv.at[place, half], pair)

    def taken(place, half):
        return moved(2 * place + 1 - core, 2 * place + 1 - core, half, pair_send.at[place, half], pair_recv.at[place, half], pair)

    for half in range(2):
        def wait(shard):
            @pl.when(across | (shard != head))
            def _():
                landed(half, shard).wait_recv()

        each(wait)

        @pl.when(diagonal)
        def _():
            at_home(half).wait()

        hop(0, 0, half).start()
        hop(1, 0, half).start()
        shared(2, half).start()
    for half in range(2):
        hop(0, 0, half).wait_recv()
        hop(0, 1, half).start()
        hop(1, 0, half).wait_recv()
        hop(1, 1, half).start()
        shared(1, half).start()
        shared(3, half).start()
    for half in range(2):
        hop(0, 1, half).wait_recv()
        shared(0, half).start()
        hop(1, 1, half).wait_recv()
        shared(4, half).start()

    def wait_q(shard):
        @pl.when(across | (shard != head))
        def _():
            spread_q(0, shard).wait_recv()

    each(wait_q)

    def sent(group):
        @pl.when(across | (group != plane))
        def _():
            spread(group, 0, head).wait_send()
            spread(group, 1, head).wait_send()
            spread_q(group, head).wait_send()

    each(sent)

    @pl.when(diagonal)
    def _():
        q_at_home.wait()
        for copy in routes_at_home:
            copy.wait()

    @pl.when(across)
    def _():
        for copy in routes_sent:
            copy.wait()

    for index in range(2):
        weights_at_home[index].wait()
        for rise in range(1, 4):
            for step in range(1, 4):
                over(index, rise, step).wait_recv()
        share(index).start()

    for half in range(2):
        for way in range(2):
            for step in range(2):
                hop(way, step, half).wait_send()
        for place in range(5):
            shared(place, half).wait_send()
            taken(place, half).wait_recv()
    for index in range(2):
        for rise in range(1, 4):
            down(index, rise).wait_send()
            for step in range(1, 4):
                over(index, rise, step).wait_send()
        share(index).wait()


def exchange(kv, q, routes, local, w1, w2):
    anywhere = pl.BlockSpec(memory_space=pltpu.HBM)
    return pl.pallas_call(
        exchange_kernel,
        out_shape=(
            jax.ShapeDtypeStruct((10, GROUPS, TOK, LANES), BF16),
            jax.ShapeDtypeStruct((GROUPS, LANES, LANES), BF16),
            jax.ShapeDtypeStruct((1, LANES), jnp.int32),
            jax.ShapeDtypeStruct((1, LANES), jnp.int32),
            jax.ShapeDtypeStruct((2, 4, D, 256), BF16),
            jax.ShapeDtypeStruct((2, 4, 256, D), BF16),
        ),
        in_specs=[anywhere] * 6,
        out_specs=(anywhere,) * 6,
        scratch_shapes=[
            pltpu.SemaphoreType.DMA((3, 8)),
            pltpu.SemaphoreType.DMA((3, 8)),
            pltpu.SemaphoreType.DMA((2, 2, 2)),
            pltpu.SemaphoreType.DMA((2, 2, 2)),
            pltpu.SemaphoreType.DMA((5, 2)),
            pltpu.SemaphoreType.DMA((5, 2)),
            pltpu.SemaphoreType.DMA((2, 2)),
            pltpu.SemaphoreType.DMA((7,)),
            pltpu.SemaphoreType.DMA((2, 3)),
            pltpu.SemaphoreType.DMA((2, 3)),
            pltpu.SemaphoreType.DMA((2, 3, 3)),
            pltpu.SemaphoreType.DMA((2, 3, 3)),
            pltpu.SemaphoreType.DMA((2,)),
            pltpu.SemaphoreType.DMA((2,)),
        ],
        compiler_params=pltpu.CompilerParams(collective_id=0, has_side_effects=True),
        name="exchange",
    )(kv, q, routes, local, w1, w2)


def per_device(
    points, gain_attn, w_qkv, w_out, gain_mlp, w_fc1, w_fc2, contact_route, contact_patch, counts
):
    kv, q = project(points, gain_attn, w_qkv)
    slots, q, routes, local, w1, w2 = exchange(kv, q, contact_route.reshape(1, -1), contact_patch, w_fc1, w_fc2)
    packed = attend(routes, local, counts, q, slots.reshape(20, PATCH, LANES))
    w1 = w1.reshape(GROUPS, D, 256)
    return finish(points, packed, w_out, gain_mlp, w1, w2.reshape(GROUPS, 256, D))


def solution(mesh):
    return jax.shard_map(
        per_device,
        mesh=mesh,
        in_specs=(
            P(("seq", "head"), None), P(), P(), P(), P(), P(None, "head"), P("head", None),
            P("head", None, None), P("head", None), P(),
        ),
        out_specs=P(("seq", "head"), None),
        check_vma=False,
    )
```

```python
import functools
import math

import jax
import jax.numpy as jnp
import numpy as np
from jax import lax
from jax.experimental import pallas as pl
from jax.experimental.pallas import tpu as pltpu
from jax.sharding import PartitionSpec as P

D = 512
HEADS = 32
HEAD_DIM = 16
PATCH = 1024
CB = 2
NPL = 2
REACH = 4
TOK = 256
GROUPS = 8
LANES = 128
CHUNK = 512
F32 = jnp.float32
BF16 = jnp.bfloat16
MASKED = -3.3e38
ROWS = 8 * LANES
MESH = pl.DeviceIdType.MESH


def placing():
    kv = np.zeros((384, 256), np.float32)
    low = np.zeros((384, 256), np.float32)
    high = np.zeros((384, 256), np.float32)
    for group in range(2):
        for head in range(4):
            for dim in range(HEAD_DIM):
                source = group * 192 + head * 48 + dim
                lane = group * 128 + head * 16 + dim
                low[source, lane] = 1
                high[source, lane + 64] = 1
                kv[source + 16, lane] = 1
                kv[source + 32, lane + 64] = 1
    return np.concatenate([kv, low, high], axis=1)


def lane_of(shape):
    return lax.broadcasted_iota(jnp.int32, shape, len(shape) - 1)


def normalise(values, gain):
    centred = values - jnp.mean(values, axis=-1, keepdims=True)
    spread = jnp.mean(centred * centred, axis=-1, keepdims=True)
    return centred * lax.rsqrt(spread + 1e-05) * gain


def swap_ids():
    seq, head = lax.axis_index("seq"), lax.axis_index("head")
    column = seq // 8
    return column, seq - column * 8, head


def attend_kernel(
    routes_hbm, local_hbm, counts_hbm, q_hbm, kv_ref, out_ref,
    routes_ref, local_ref, counts_ref, q_ref, raw, keys, vals, turned, lhs, acc, top, done, sems, small_sems, out_sems,
):
    column, _, head_index = swap_ids()
    seq = column * 8 + head_index
    core = lax.rem(head_index, 2)
    loads = [
        pltpu.make_async_copy(routes_hbm, routes_ref, small_sems.at[0]),
        pltpu.make_async_copy(local_hbm, local_ref, small_sems.at[1]),
        pltpu.make_async_copy(counts_hbm, counts_ref, small_sems.at[2]),
        pltpu.make_async_copy(q_hbm, q_ref, small_sems.at[3]),
    ]
    for load in loads:
        load.start()
    for load in loads[:3]:
        load.wait()

    def source(patch, which):
        if which == 0:
            return (REACH + core) * NPL + patch, seq * GROUPS + patch * 4
        row = seq * NPL * CB + patch * CB + which - 1
        route = routes_ref[0, row]
        offset = jnp.where(route < REACH, route - REACH, route - REACH + 1)
        local = local_ref[0, row]
        owner = lax.rem(seq + offset + 32, 32)
        return (offset + REACH + core) * NPL + local, owner * GROUPS + local * 4

    for patch in range(NPL):
        for which in range(CB + 1):
            slot, _ = source(patch, which)
            pltpu.make_async_copy(kv_ref.at[slot], raw.at[patch * 3 + which], sems.at[patch * 3 + which]).start()
    loads[3].wait()

    lane_kv = lane_of((TOK, LANES))
    row_kv = lax.broadcasted_iota(jnp.int32, (TOK, LANES), 0)
    lane_q = lane_of((LANES, LANES))
    row_q = lax.broadcasted_iota(jnp.int32, (LANES, LANES), 0)
    zero = jnp.zeros((TOK, LANES), BF16)
    low_lane = lane_kv < 64
    sum_of = ((lane_q == row_q // 16) & (lane_q < 4)).astype(F32).astype(BF16)
    value_of = ((row_q % 32 < 16) & (lane_q == 64 + row_q // 32 * 16 + row_q % 32)).astype(F32).astype(BF16)
    ones_row = lax.broadcasted_iota(jnp.int32, (LANES, CHUNK), 0) % 32 >= 16

    def patch_body(patch, _):
        for which in range(CB + 1):
            pltpu.make_async_copy(kv_ref.at[0], raw.at[patch * 3 + which], sems.at[patch * 3 + which]).wait()

        first = jnp.int32(0)
        key_top = jnp.zeros((1, LANES), F32)
        val_top = jnp.zeros((1, LANES), F32)
        for which in range(CB + 1):
            _, shard = source(patch, which)
            for part in range(4):
                count = counts_ref[shard + part]
                block = raw[patch * 3 + which, TOK * part:TOK * part + TOK, :]
                valid = row_kv < count
                flag = jnp.where(valid, zero, jnp.where(lane_kv < 66, jnp.full_like(zero, MASKED), zero))
                keyed = jnp.where(low_lane & valid, block, zero)
                at = pl.ds(pl.multiple_of(first, 16), TOK)
                keys[at, :] = jnp.where(low_lane, keyed, flag)
                vals[at, :] = block
                squares = jnp.dot(keyed * keyed, sum_of, preferred_element_type=F32)
                key_top = jnp.maximum(key_top, jnp.max(squares, axis=0, keepdims=True))
                size = jnp.max(jnp.where(low_lane, zero, jnp.abs(block)).astype(F32), axis=0, keepdims=True)
                val_top = jnp.maximum(val_top, size)
                first = first + (count + 15) // 16 * 16
        for more in range(CHUNK // TOK):
            tail = pl.ds(pl.multiple_of(first + more * TOK, 16), TOK)
            keys[tail, :] = jnp.where(low_lane | (lane_kv >= 66), zero, jnp.full_like(zero, MASKED))
            vals[tail, :] = zero
        chunks = (first + CHUNK - 1) // CHUNK

        def turn(chunk, _):
            at = pl.ds(pl.multiple_of(chunk * CHUNK, CHUNK), CHUNK)
            picked = lax.dot_general(value_of, vals[at, :], (((1,), (1,)), ((), ())), preferred_element_type=F32)
            turned[:, at] = jnp.where(ones_row, 1.0, picked).astype(BF16)
            return 0

        lax.fori_loop(0, chunks, turn, 0)

        query_top = jnp.zeros((1, LANES), F32)
        for part in range(4):
            packed = q_ref[patch * 4 + part]
            for half in range(2):
                q = packed if half == 0 else pltpu.roll(packed.astype(F32), 64, 1).astype(BF16)
                q = jnp.where(lane_q < 64, q, jnp.zeros_like(q))
                squares = jnp.dot(q * q, sum_of, preferred_element_type=F32)
                query_top = jnp.maximum(query_top, jnp.max(squares, axis=0, keepdims=True))
        bound = jnp.max(query_top * key_top)
        small = (bound < 3000.0) & (jnp.max(val_top) < 1e9)

        def shard_body(part, _):
            packed = q_ref[patch * 4 + part]
            flags = jnp.where((lane_q >= 64) & (lane_q < 66), jnp.ones_like(packed), jnp.zeros_like(packed))
            for half in range(2):
                q = packed if half == 0 else pltpu.roll(packed.astype(F32), 64, 1).astype(BF16)
                for head in range(4):
                    mine = (lane_q >= 16 * head) & (lane_q < 16 * head + 16)
                    lhs[pl.ds((head * 2 + half) * LANES, LANES), :] = jnp.where(mine, q, flags)
            acc[...] = jnp.zeros_like(acc)

            def scores_of(chunk):
                at = pl.ds(pl.multiple_of(chunk * CHUNK, CHUNK), CHUNK)
                return at, lax.dot_general(
                    keys[at, :], lhs[...], (((1,), (1,)), ((), ())), preferred_element_type=F32
                )

            def gather(at, weights):
                for head in range(4):
                    rows = slice(32 * head, 32 * head + 32)
                    acc[rows] += jnp.dot(
                        turned[rows, at], weights[:, TOK * head:TOK * head + TOK], preferred_element_type=F32
                    )

            @pl.when(small)
            def _():
                def chunk_body(chunk, _):
                    at, scores = scores_of(chunk)
                    gather(at, jnp.exp2(scores).astype(BF16))
                    return 0

                lax.fori_loop(0, chunks, chunk_body, 0)

            @pl.when(jnp.logical_not(small))
            def _():
                top[...] = jnp.full_like(top, -jnp.inf)

                def top_body(chunk, _):
                    _, scores = scores_of(chunk)
                    top[...] = jnp.maximum(top[...], jnp.max(scores, axis=0, keepdims=True))
                    return 0

                lax.fori_loop(0, chunks, top_body, 0)

                def chunk_body(chunk, _):
                    at, scores = scores_of(chunk)
                    gather(at, jnp.exp2(scores - top[...]).astype(BF16))
                    return 0

                lax.fori_loop(0, chunks, chunk_body, 0)

            joined = [acc[32 * head:32 * head + 16] / acc[32 * head + 16:32 * head + 32] for head in range(4)]
            done[patch * 4 + part] = jnp.concatenate(joined, axis=0).astype(BF16)
            pltpu.make_async_copy(
                done.at[patch * 4 + part], out_ref.at[patch * 4 + part], out_sems.at[patch * 4 + part]
            ).start()
            return 0

        lax.fori_loop(0, 4, shard_body, 0)
        return 0

    lax.fori_loop(0, NPL, patch_body, 0)
    for shard in range(GROUPS):
        pltpu.make_async_copy(done.at[shard], out_ref.at[shard], out_sems.at[shard]).wait()


def attend(routes, local, counts, q, kv):
    hbm = pl.BlockSpec(memory_space=pltpu.HBM)
    return pl.pallas_call(
        attend_kernel,
        out_shape=jax.ShapeDtypeStruct((GROUPS, 64, TOK), BF16),
        in_specs=[hbm] * 5,
        out_specs=hbm,
        scratch_shapes=[
            pltpu.SMEM((1, LANES), jnp.int32),
            pltpu.SMEM((1, LANES), jnp.int32),
            pltpu.SMEM((256,), jnp.int32),
            pltpu.VMEM((GROUPS, LANES, LANES), BF16),
            pltpu.VMEM((6, PATCH, LANES), BF16),
            pltpu.VMEM((3 * PATCH + CHUNK, LANES), BF16),
            pltpu.VMEM((3 * PATCH + CHUNK, LANES), BF16),
            pltpu.VMEM((LANES, 3 * PATCH + CHUNK), BF16),
            pltpu.VMEM((ROWS, LANES), BF16),
            pltpu.VMEM((LANES, TOK), F32),
            pltpu.VMEM((1, ROWS), F32),
            pltpu.VMEM((GROUPS, 64, TOK), BF16),
            pltpu.SemaphoreType.DMA((6,)),
            pltpu.SemaphoreType.DMA((4,)),
            pltpu.SemaphoreType.DMA((8,)),
        ],
        compiler_params=pltpu.CompilerParams(vmem_limit_bytes=60 << 20),
        cost_estimate=pl.CostEstimate(flops=30_000_000_000, bytes_accessed=8_000_000, transcendentals=25_000_000),
        name="attend",
    )(routes, local, counts, q, kv)


def each(body):
    def step(index, _):
        body(index)
        return 0

    lax.fori_loop(0, 8, step, 0)


def finish_kernel(
    points_ref, packed_ref, w_out_ref, gain_ref, w0_ref, w1_ref, w2_ref, w3_ref, out_ref,
    points, w_out, gain, slabs, back, send, recv, local_sem, load_sem, weight_sem, pair_send, pair_recv,
):
    column, plane, head = swap_ids()
    diagonal = plane == head
    across = jnp.logical_not(diagonal)
    barrier = pltpu.get_barrier_semaphore()

    def greet(group):
        @pl.when(across | (group != plane))
        def _():
            pl.semaphore_signal(barrier, inc=1, device_id=(column * 8 + group, plane), device_id_type=MESH)

    each(greet)
    pair = (column * 8 + plane, head + 1 - 2 * lax.rem(head, 2))
    pl.semaphore_signal(barrier, inc=1, device_id=pair, device_id_type=MESH)
    loads = [
        pltpu.make_async_copy(points_ref, points, load_sem.at[0]),
        pltpu.make_async_copy(w_out_ref, w_out, load_sem.at[1]),
        pltpu.make_async_copy(gain_ref, gain, load_sem.at[2]),
    ]
    for load in loads:
        load.start()

    shards = (w0_ref, w1_ref, w2_ref, w3_ref)
    own = [pltpu.make_async_copy(shard, slabs.at[part], weight_sem.at[part]) for part, shard in enumerate(shards)]
    lent = [
        pltpu.make_async_remote_copy(
            src_ref=shard, dst_ref=slabs.at[4 + part], send_sem=pair_send.at[part], recv_sem=pair_recv.at[part],
            device_id=pair, device_id_type=MESH,
        )
        for part, shard in enumerate(shards)
    ]
    for load in own:
        load.start()

    @pl.when(diagonal)
    def _():
        pl.semaphore_wait(barrier, 8)

    @pl.when(across)
    def _():
        pl.semaphore_wait(barrier, 9)

    def copy(shard, group):
        return pltpu.make_async_remote_copy(
            src_ref=packed_ref.at[shard], dst_ref=back.at[group],
            send_sem=send.at[shard], recv_sem=recv.at[group],
            device_id=(column * 8 + head, shard), device_id_type=MESH,
        )

    at_home = pltpu.make_async_copy(packed_ref.at[head], back.at[plane], local_sem.at[0])

    def start(shard):
        @pl.when(across | (shard != head))
        def _():
            copy(shard, plane).start()

    each(start)
    for load in lent:
        load.start()

    @pl.when(diagonal)
    def _():
        at_home.start()
        at_home.wait()

    for load in loads:
        load.wait()

    def wait(index):
        @pl.when(across | (index != plane))
        def _():
            copy(0, index).wait_recv()

    each(wait)

    attended = back[...].reshape(D, TOK)
    updated = points[...].astype(F32) + lax.dot_general(
        attended, w_out[...], (((0,), (0,)), ((), ())), preferred_element_type=F32
    )
    updated = updated.astype(BF16).astype(F32)
    normed = normalise(updated, gain[...]).astype(BF16)
    low, high = updated[:, :256], updated[:, 256:]
    for part in range(GROUPS):
        if part < 4:
            own[part].wait()
        else:
            lent[part - 4].wait_recv()
        hidden = jnp.dot(normed, slabs[part, :D], preferred_element_type=F32)
        hidden = (hidden * (0.5 * (1.0 + lax.erf(hidden * (2.0 ** -0.5))))).astype(BF16)
        low = low + jnp.dot(hidden, slabs[part, D:D + 256], preferred_element_type=F32)
        high = high + jnp.dot(hidden, slabs[part, D + 256:], preferred_element_type=F32)
    out_ref[:, :256] = low.astype(BF16)
    out_ref[:, 256:] = high.astype(BF16)

    def sent(index):
        @pl.when(across | (index != head))
        def _():
            copy(index, plane).wait_send()

    each(sent)
    for load in lent:
        load.wait_send()


def finish(points, packed, w_out, gain, weights):
    hbm = pl.BlockSpec(memory_space=pltpu.HBM)
    return pl.pallas_call(
        finish_kernel,
        out_shape=jax.ShapeDtypeStruct((TOK, D), BF16),
        in_specs=[hbm] * 8,
        out_specs=pl.BlockSpec(memory_space=pltpu.VMEM),
        scratch_shapes=[
            pltpu.VMEM((TOK, D), BF16),
            pltpu.VMEM((D, D), BF16),
            pltpu.VMEM((1, D), F32),
            pltpu.VMEM((GROUPS, 2 * D, 256), BF16),
            pltpu.VMEM((GROUPS, 64, TOK), BF16),
            pltpu.SemaphoreType.DMA((8,)),
            pltpu.SemaphoreType.DMA((8,)),
            pltpu.SemaphoreType.DMA((1,)),
            pltpu.SemaphoreType.DMA((3,)),
            pltpu.SemaphoreType.DMA((4,)),
            pltpu.SemaphoreType.DMA((4,)),
            pltpu.SemaphoreType.DMA((4,)),
        ],
        compiler_params=pltpu.CompilerParams(
            collective_id=1, has_side_effects=True, vmem_limit_bytes=40 << 20
        ),
        name="finish",
    )(points, packed, w_out, gain.reshape(1, D), *weights)


def exchange_kernel(
    points_ref, gain_ref, w_ref, scale_ref, place_ref, route_ref, local_ref, kv_out, q_out, route_out, local_out,
    kv_ref, q_ref,
    all_send, all_recv, ring_send, ring_recv, pair_send, pair_recv, route_sem, local_sem,
):
    column, plane, head = swap_ids()
    core = lax.rem(head, 2)
    spot = column * 4 + head // 2
    after, before = lax.rem(spot + 1, 16), lax.rem(spot + 15, 16)
    right = ((after // 4) * 8 + plane, lax.rem(after, 4) * 2 + core)
    left = ((before // 4) * 8 + plane, lax.rem(before, 4) * 2 + core)
    pair = (column * 8 + plane, head + 1 - 2 * core)
    partner = (column * 8 + head, plane)
    diagonal = plane == head
    across = jnp.logical_not(diagonal)

    barrier = pltpu.get_barrier_semaphore()

    def greet(index, _):
        @pl.when(across | (index != head))
        def _():
            pl.semaphore_signal(barrier, inc=1, device_id=(column * 8 + head, index), device_id_type=MESH)
        return 0

    lax.fori_loop(0, 8, greet, 0)
    for other in (right, left, pair):
        pl.semaphore_signal(barrier, inc=1, device_id=other, device_id_type=MESH)

    def enter():
        @pl.when(diagonal)
        def _():
            pl.semaphore_wait(barrier, 10)

        @pl.when(across)
        def _():
            pl.semaphore_wait(barrier, 11)

    def rows(half):
        return pl.ds(half * LANES, LANES)

    def spread(group, half, shard):
        return pltpu.make_async_remote_copy(
            src_ref=kv_ref.at[group, rows(half)],
            dst_ref=kv_out.at[4 + lax.rem(plane, 2), shard, rows(half)],
            send_sem=all_send.at[half, group],
            recv_sem=all_recv.at[half, shard],
            device_id=(column * 8 + group, plane),
            device_id_type=MESH,
        )

    def landed(half, shard):
        return pltpu.make_async_remote_copy(
            src_ref=kv_ref.at[0, rows(half)],
            dst_ref=kv_out.at[4 + core, shard, rows(half)],
            send_sem=all_send.at[half, 0],
            recv_sem=all_recv.at[half, shard],
            device_id=pair,
            device_id_type=MESH,
        )

    def spread_q(group, shard):
        return pltpu.make_async_remote_copy(
            src_ref=q_ref.at[group],
            dst_ref=q_out.at[shard],
            send_sem=all_send.at[2, group],
            recv_sem=all_recv.at[2, shard],
            device_id=(column * 8 + group, plane),
            device_id_type=MESH,
        )

    def at_home(half):
        return pltpu.make_async_copy(
            kv_ref.at[plane, rows(half)], kv_out.at[4 + core, head, rows(half)], local_sem.at[half]
        )

    q_at_home = pltpu.make_async_copy(q_ref.at[plane], q_out.at[head], local_sem.at[2])
    routes_at_home = [
        pltpu.make_async_copy(route_ref, route_out, local_sem.at[3]),
        pltpu.make_async_copy(local_ref, local_out, local_sem.at[4]),
    ]
    routes_sent = [
        pltpu.make_async_remote_copy(
            src_ref=source, dst_ref=target, send_sem=route_sem.at[0, index], recv_sem=route_sem.at[1, index],
            device_id=partner, device_id_type=MESH,
        )
        for index, (source, target) in enumerate(((route_ref, route_out), (local_ref, local_out)))
    ]

    def start(group):
        @pl.when(across | (group != plane))
        def _():
            spread(group, 0, head).start()
            spread(group, 1, head).start()

    def start_q(group):
        @pl.when(across | (group != plane))
        def _():
            spread_q(group, head).start()

    normed = normalise(points_ref[...].astype(F32), gain_ref[...]).astype(BF16)
    for couple in range(GROUPS // 2):
        columns = slice(384 * couple, 384 * couple + 384)
        projected = jnp.dot(normed, w_ref[:, columns], preferred_element_type=F32)
        projected = (projected * scale_ref[:, columns]).astype(BF16)
        kv = jnp.dot(projected, place_ref[:, :256], preferred_element_type=F32).astype(BF16)
        q = jnp.dot(projected[:128], place_ref[:, 256:512], preferred_element_type=F32)
        q = (q + jnp.dot(projected[128:], place_ref[:, 512:], preferred_element_type=F32)).astype(BF16)
        for side in range(2):
            kv_ref[2 * couple + side] = kv[:, 128 * side:128 * side + 128]
            q_ref[2 * couple + side] = q[:, 128 * side:128 * side + 128]
        if couple == 0:
            enter()
        start(2 * couple)
        start(2 * couple + 1)
    each(start_q)

    @pl.when(diagonal)
    def _():
        at_home(0).start()
        at_home(1).start()
        q_at_home.start()
        for copy in routes_at_home:
            copy.start()

    @pl.when(across)
    def _():
        for copy in routes_sent:
            copy.start()


    def moved(source, target, half, send, recv, to):
        return pltpu.make_async_remote_copy(
            src_ref=kv_out.at[source, :, rows(half)], dst_ref=kv_out.at[target, :, rows(half)],
            send_sem=send, recv_sem=recv, device_id=to, device_id_type=MESH,
        )

    def hop(way, step, half):
        if way == 0:
            source, to = 4 - 2 * step + core, right
            target = 2 - 2 * step + core
        else:
            source, to = 4 + 2 * step + core, left
            target = 6 + 2 * step + core
        return moved(source, target, half, ring_send.at[way, step, half], ring_recv.at[way, step, half], to)

    def shared(place, half):
        return moved(2 * place + core, 2 * place + core, half, pair_send.at[place, half], pair_recv.at[place, half], pair)

    def taken(place, half):
        return moved(2 * place + 1 - core, 2 * place + 1 - core, half, pair_send.at[place, half], pair_recv.at[place, half], pair)

    for half in range(2):
        def wait(shard):
            @pl.when(across | (shard != head))
            def _():
                landed(half, shard).wait_recv()

        each(wait)

        @pl.when(diagonal)
        def _():
            at_home(half).wait()

        hop(0, 0, half).start()
        hop(1, 0, half).start()
        shared(2, half).start()
    for half in range(2):
        hop(0, 0, half).wait_recv()
        hop(0, 1, half).start()
        hop(1, 0, half).wait_recv()
        hop(1, 1, half).start()
        shared(1, half).start()
        shared(3, half).start()
    for half in range(2):
        hop(0, 1, half).wait_recv()
        shared(0, half).start()
        hop(1, 1, half).wait_recv()
        shared(4, half).start()

    def wait_q(shard):
        @pl.when(across | (shard != head))
        def _():
            spread_q(0, shard).wait_recv()

    each(wait_q)

    def sent(group):
        @pl.when(across | (group != plane))
        def _():
            spread(group, 0, head).wait_send()
            spread(group, 1, head).wait_send()
            spread_q(group, head).wait_send()

    each(sent)

    @pl.when(diagonal)
    def _():
        q_at_home.wait()
        for copy in routes_at_home:
            copy.wait()

    @pl.when(across)
    def _():
        for copy in routes_sent:
            copy.wait()


    for half in range(2):
        for way in range(2):
            for step in range(2):
                hop(way, step, half).wait_send()
        for place in range(5):
            shared(place, half).wait_send()
            taken(place, half).wait_recv()


def exchange(points, gain, w_qkv, routes, local):
    scale = np.ones((1, 1536), np.float32)
    scale[0, np.arange(1536) % 48 < 16] = HEAD_DIM ** -0.5 * math.log2(math.e)
    vmem = pl.BlockSpec(memory_space=pltpu.VMEM)
    anywhere = pl.BlockSpec(memory_space=pltpu.HBM)
    return pl.pallas_call(
        exchange_kernel,
        out_shape=(
            jax.ShapeDtypeStruct((10, GROUPS, TOK, LANES), BF16),
            jax.ShapeDtypeStruct((GROUPS, LANES, LANES), BF16),
            jax.ShapeDtypeStruct((1, LANES), jnp.int32),
            jax.ShapeDtypeStruct((1, LANES), jnp.int32),
        ),
        in_specs=[vmem] * 5 + [anywhere] * 2,
        out_specs=(anywhere,) * 4,
        scratch_shapes=[
            pltpu.VMEM((GROUPS, TOK, LANES), BF16),
            pltpu.VMEM((GROUPS, LANES, LANES), BF16),
            pltpu.SemaphoreType.DMA((3, 8)),
            pltpu.SemaphoreType.DMA((3, 8)),
            pltpu.SemaphoreType.DMA((2, 2, 2)),
            pltpu.SemaphoreType.DMA((2, 2, 2)),
            pltpu.SemaphoreType.DMA((5, 2)),
            pltpu.SemaphoreType.DMA((5, 2)),
            pltpu.SemaphoreType.DMA((2, 2)),
            pltpu.SemaphoreType.DMA((7,)),
        ],
        compiler_params=pltpu.CompilerParams(collective_id=0, has_side_effects=True, vmem_limit_bytes=60 << 20),
        name="exchange",
    )(
        points, gain.reshape(1, D), w_qkv, jnp.asarray(scale), jnp.asarray(placing(), BF16), routes, local,
    )


def per_device(
    points, gain_attn, w_qkv, w_out, gain_mlp, w_fc1, w_fc2, contact_route, contact_patch, counts
):
    slots, q, routes, local = exchange(points, gain_attn, w_qkv, contact_route.reshape(1, -1), contact_patch)
    own = jnp.concatenate([w_fc1, w_fc2[:, :256], w_fc2[:, 256:]], axis=0)
    own, routes = lax.optimization_barrier((own, routes))
    weights = [own]
    for step in range(1, 4):
        pairs = [(head, (head + 2 * step) % GROUPS) for head in range(GROUPS)]
        weights.append(lax.ppermute(own, "head", pairs))
    packed = attend(routes, local, counts, q, slots.reshape(20, PATCH, LANES))
    return finish(points, packed, w_out, gain_mlp, weights)


def solution(mesh):
    return jax.shard_map(
        per_device,
        mesh=mesh,
        in_specs=(
            P(("seq", "head"), None), P(), P(), P(), P(), P(None, "head"), P("head", None),
            P("head", None, None), P("head", None), P(),
        ),
        out_specs=P(("seq", "head"), None),
        check_vma=False,
    )
```

```python
import functools
import math

import jax
import jax.numpy as jnp
import numpy as np
from jax import lax
from jax.experimental import pallas as pl
from jax.experimental.pallas import tpu as pltpu
from jax.sharding import PartitionSpec as P

D = 512
HEADS = 32
HEAD_DIM = 16
PATCH = 1024
CB = 2
NPL = 2
REACH = 4
TOK = 256
GROUPS = 8
LANES = 128
CHUNK = 512
F32 = jnp.float32
BF16 = jnp.bfloat16
MASKED = -3.3e38
ROWS = 8 * LANES
MESH = pl.DeviceIdType.MESH


def placing():
    kv = np.zeros((384, 256), np.float32)
    low = np.zeros((384, 256), np.float32)
    high = np.zeros((384, 256), np.float32)
    for group in range(2):
        for head in range(4):
            for dim in range(HEAD_DIM):
                source = group * 192 + head * 48 + dim
                lane = group * 128 + head * 16 + dim
                low[source, lane] = 1
                high[source, lane + 64] = 1
                kv[source + 16, lane] = 1
                kv[source + 32, lane + 64] = 1
    return np.concatenate([kv, low, high], axis=1)


def lane_of(shape):
    return lax.broadcasted_iota(jnp.int32, shape, len(shape) - 1)


def normalise(values, gain):
    centred = values - jnp.mean(values, axis=-1, keepdims=True)
    spread = jnp.mean(centred * centred, axis=-1, keepdims=True)
    return centred * lax.rsqrt(spread + 1e-05) * gain


def swap_ids():
    seq, head = lax.axis_index("seq"), lax.axis_index("head")
    column = seq // 8
    return column, seq - column * 8, head


def iotas(rows):
    shape = (rows, LANES)
    return lax.broadcasted_iota(jnp.int32, shape, 0), lax.broadcasted_iota(jnp.int32, shape, 1)


def value_picker():
    row, lane = iotas(LANES)
    return ((row % 32 < 16) & (lane == 64 + row // 32 * 16 + row % 32)).astype(F32).astype(BF16)


def keyed_rows(block, count):
    row, lane = iotas(TOK)
    zero = jnp.zeros((TOK, LANES), BF16)
    valid = row < count
    flag = jnp.where(valid, zero, jnp.where(lane < 66, jnp.full_like(zero, MASKED), zero))
    keyed = jnp.where((lane < 64) & valid, block, zero)
    return keyed, jnp.where(lane < 64, keyed, flag)


def turn_values(vals, turned, at, size):
    ones_row = lax.broadcasted_iota(jnp.int32, (LANES, size), 0) % 32 >= 16
    picked = lax.dot_general(value_picker(), vals, (((1,), (1,)), ((), ())), preferred_element_type=F32)
    turned[:, at] = jnp.where(ones_row, 1.0, picked).astype(BF16)


def half_of(packed, half):
    return packed if half == 0 else pltpu.roll(packed.astype(F32), 64, 1).astype(BF16)


def spread_heads(packed, lhs):
    _, lane = iotas(LANES)
    flags = jnp.where((lane >= 64) & (lane < 66), jnp.ones_like(packed), jnp.zeros_like(packed))
    for half in range(2):
        q = half_of(packed, half)
        for head in range(4):
            mine = (lane >= 16 * head) & (lane < 16 * head + 16)
            lhs[pl.ds((head * 2 + half) * LANES, LANES), :] = jnp.where(mine, q, flags)


def scores_of(keys, lhs):
    return lax.dot_general(keys, lhs[...], (((1,), (1,)), ((), ())), preferred_element_type=F32)


def head_columns(values, head):
    return values[:, TOK * head:TOK * head + TOK]


def attend_kernel(
    routes_hbm, local_hbm, counts_hbm, q_hbm, kv_ref, own_hbm, own_top_hbm, out_ref,
    routes_ref, local_ref, counts_ref, q_ref, own_ref, own_top_ref,
    raw, keys, vals, turned, lhs, acc, top, done, sems, small_sems, out_sems,
):
    column, _, head_index = swap_ids()
    seq = column * 8 + head_index
    core = lax.rem(head_index, 2)
    loads = [
        pltpu.make_async_copy(source, target, small_sems.at[index])
        for index, (source, target) in enumerate((
            (routes_hbm, routes_ref), (local_hbm, local_ref), (counts_hbm, counts_ref),
            (q_hbm, q_ref), (own_hbm, own_ref), (own_top_hbm, own_top_ref),
        ))
    ]
    for load in loads:
        load.start()
    for load in loads[:3]:
        load.wait()

    def source(patch, which):
        row = seq * NPL * CB + patch * CB + which
        route = routes_ref[0, row]
        offset = jnp.where(route < REACH, route - REACH, route - REACH + 1)
        local = local_ref[0, row]
        owner = lax.rem(seq + offset + 32, 32)
        return (offset + REACH + core) * NPL + local, owner * GROUPS + local * 4

    for patch in range(NPL):
        for which in range(CB):
            slot, _ = source(patch, which)
            pltpu.make_async_copy(kv_ref.at[slot], raw.at[patch * CB + which], sems.at[patch * CB + which]).start()
    for load in loads[3:]:
        load.wait()

    row_q, lane_q = iotas(LANES)
    _, lane_kv = iotas(TOK)
    zero = jnp.zeros((TOK, LANES), BF16)
    sum_of = ((lane_q == row_q // 16) & (lane_q < 4)).astype(F32).astype(BF16)

    def patch_body(patch, _):
        for which in range(CB):
            pltpu.make_async_copy(kv_ref.at[0], raw.at[patch * CB + which], sems.at[patch * CB + which]).wait()

        first = jnp.int32(0)
        key_top = jnp.zeros((1, LANES), F32)
        val_top = jnp.zeros((1, LANES), F32)
        for which in range(CB):
            _, shard = source(patch, which)
            for part in range(4):
                count = counts_ref[shard + part]
                block = raw[patch * CB + which, TOK * part:TOK * part + TOK, :]
                keyed, marked = keyed_rows(block, count)
                at = pl.ds(pl.multiple_of(first, 16), TOK)
                keys[at, :] = marked
                vals[at, :] = block
                squares = jnp.dot(keyed * keyed, sum_of, preferred_element_type=F32)
                key_top = jnp.maximum(key_top, jnp.max(squares, axis=0, keepdims=True))
                size = jnp.max(jnp.where(lane_kv < 64, zero, jnp.abs(block)).astype(F32), axis=0, keepdims=True)
                val_top = jnp.maximum(val_top, size)
                first = first + (count + 15) // 16 * 16
        tail = pl.ds(pl.multiple_of(first, 16), TOK)
        keys[tail, :] = keyed_rows(zero, 0)[1]
        vals[tail, :] = zero
        pieces = (first + TOK - 1) // TOK
        chunks = pieces // 2
        odd = pieces % 2 == 1

        def turn(piece, _):
            at = pl.ds(pl.multiple_of(piece * TOK, TOK), TOK)
            turn_values(vals[at, :], turned, at, TOK)
            return 0

        lax.fori_loop(0, pieces, turn, 0)

        query_top = jnp.zeros((1, LANES), F32)
        for part in range(4):
            packed = q_ref[patch * 4 + part]
            for half in range(2):
                q = half_of(packed, half)
                q = jnp.where(lane_q < 64, q, jnp.zeros_like(q))
                squares = jnp.dot(q * q, sum_of, preferred_element_type=F32)
                query_top = jnp.maximum(query_top, jnp.max(squares, axis=0, keepdims=True))
        small = (jnp.max(query_top * key_top) < 3000.0) & (jnp.max(val_top) < 1e9)

        def shard_body(part, _):
            shard = patch * 4 + part
            spread_heads(q_ref[shard], lhs)
            own_top = own_top_ref[shard]

            def over_chunks(body):
                def chunk_body(chunk, _):
                    body(pl.ds(pl.multiple_of(chunk * CHUNK, CHUNK), CHUNK))
                    return 0

                lax.fori_loop(0, chunks, chunk_body, 0)

                @pl.when(odd)
                def _():
                    body(pl.ds(pl.multiple_of(chunks * CHUNK, CHUNK), TOK))

            def begin(scale):
                for head in range(4):
                    rows = slice(32 * head, 32 * head + 32)
                    acc[rows] = own_ref[shard, rows] * head_columns(scale, head)

            def gather(at, weights):
                for head in range(4):
                    rows = slice(32 * head, 32 * head + 32)
                    acc[rows] += jnp.dot(turned[rows, at], head_columns(weights, head), preferred_element_type=F32)

            fits = small & (jnp.max(jnp.abs(own_top)) < 55.0) & (jnp.max(jnp.abs(own_ref[shard])) < 1e12)

            @pl.when(fits)
            def _():
                begin(jnp.exp2(own_top))
                over_chunks(lambda at: gather(at, jnp.exp2(scores_of(keys[at, :], lhs)).astype(BF16)))

            @pl.when(jnp.logical_not(fits))
            def _():
                top[...] = own_top

                def raise_top(at):
                    top[...] = jnp.maximum(top[...], jnp.max(scores_of(keys[at, :], lhs), axis=0, keepdims=True))

                over_chunks(raise_top)
                begin(jnp.exp2(own_top - top[...]))
                over_chunks(lambda at: gather(at, jnp.exp2(scores_of(keys[at, :], lhs) - top[...]).astype(BF16)))

            joined = [acc[32 * head:32 * head + 16] / acc[32 * head + 16:32 * head + 32] for head in range(4)]
            done[shard] = jnp.concatenate(joined, axis=0).astype(BF16)
            pltpu.make_async_copy(done.at[shard], out_ref.at[shard], out_sems.at[shard]).start()
            return 0

        lax.fori_loop(0, 4, shard_body, 0)
        return 0

    lax.fori_loop(0, NPL, patch_body, 0)
    for shard in range(GROUPS):
        pltpu.make_async_copy(done.at[shard], out_ref.at[shard], out_sems.at[shard]).wait()


def attend(routes, local, counts, q, kv, own, own_top):
    hbm = pl.BlockSpec(memory_space=pltpu.HBM)
    most = CB * PATCH + TOK
    return pl.pallas_call(
        attend_kernel,
        out_shape=jax.ShapeDtypeStruct((GROUPS, 64, TOK), BF16),
        in_specs=[hbm] * 7,
        out_specs=hbm,
        scratch_shapes=[
            pltpu.SMEM((1, LANES), jnp.int32),
            pltpu.SMEM((1, LANES), jnp.int32),
            pltpu.SMEM((256,), jnp.int32),
            pltpu.VMEM((GROUPS, LANES, LANES), BF16),
            pltpu.VMEM((GROUPS, LANES, TOK), F32),
            pltpu.VMEM((GROUPS, 1, ROWS), F32),
            pltpu.VMEM((NPL * CB, PATCH, LANES), BF16),
            pltpu.VMEM((most, LANES), BF16),
            pltpu.VMEM((most, LANES), BF16),
            pltpu.VMEM((LANES, most), BF16),
            pltpu.VMEM((ROWS, LANES), BF16),
            pltpu.VMEM((LANES, TOK), F32),
            pltpu.VMEM((1, ROWS), F32),
            pltpu.VMEM((GROUPS, 64, TOK), BF16),
            pltpu.SemaphoreType.DMA((NPL * CB,)),
            pltpu.SemaphoreType.DMA((6,)),
            pltpu.SemaphoreType.DMA((8,)),
        ],
        compiler_params=pltpu.CompilerParams(vmem_limit_bytes=60 << 20),
        cost_estimate=pl.CostEstimate(flops=20_000_000_000, bytes_accessed=6_000_000, transcendentals=17_000_000),
        name="attend",
    )(routes, local, counts, q, kv, own, own_top)


def each(body):
    def step(index, _):
        body(index)
        return 0

    lax.fori_loop(0, 8, step, 0)


def finish_kernel(
    points_ref, packed_ref, w_out_ref, gain_ref, w0_ref, w1_ref, w2_ref, w3_ref, out_ref,
    points, w_out, gain, slabs, back, send, recv, local_sem, load_sem, weight_sem, pair_send, pair_recv,
):
    column, plane, head = swap_ids()
    diagonal = plane == head
    across = jnp.logical_not(diagonal)
    barrier = pltpu.get_barrier_semaphore()

    def greet(group):
        @pl.when(across | (group != plane))
        def _():
            pl.semaphore_signal(barrier, inc=1, device_id=(column * 8 + group, plane), device_id_type=MESH)

    each(greet)
    pair = (column * 8 + plane, head + 1 - 2 * lax.rem(head, 2))
    pl.semaphore_signal(barrier, inc=1, device_id=pair, device_id_type=MESH)
    loads = [
        pltpu.make_async_copy(points_ref, points, load_sem.at[0]),
        pltpu.make_async_copy(w_out_ref, w_out, load_sem.at[1]),
        pltpu.make_async_copy(gain_ref, gain, load_sem.at[2]),
    ]
    for load in loads:
        load.start()

    shards = (w0_ref, w1_ref, w2_ref, w3_ref)
    own = [pltpu.make_async_copy(shard, slabs.at[part], weight_sem.at[part]) for part, shard in enumerate(shards)]
    lent = [
        pltpu.make_async_remote_copy(
            src_ref=shard, dst_ref=slabs.at[4 + part], send_sem=pair_send.at[part], recv_sem=pair_recv.at[part],
            device_id=pair, device_id_type=MESH,
        )
        for part, shard in enumerate(shards)
    ]
    for load in own:
        load.start()

    @pl.when(diagonal)
    def _():
        pl.semaphore_wait(barrier, 8)

    @pl.when(across)
    def _():
        pl.semaphore_wait(barrier, 9)

    def copy(shard, group):
        return pltpu.make_async_remote_copy(
            src_ref=packed_ref.at[shard], dst_ref=back.at[group],
            send_sem=send.at[shard], recv_sem=recv.at[group],
            device_id=(column * 8 + head, shard), device_id_type=MESH,
        )

    at_home = pltpu.make_async_copy(packed_ref.at[head], back.at[plane], local_sem.at[0])

    def start(shard):
        @pl.when(across | (shard != head))
        def _():
            copy(shard, plane).start()

    each(start)
    for load in lent:
        load.start()

    @pl.when(diagonal)
    def _():
        at_home.start()
        at_home.wait()

    for load in loads:
        load.wait()

    def wait(index):
        @pl.when(across | (index != plane))
        def _():
            copy(0, index).wait_recv()

    each(wait)

    attended = back[...].reshape(D, TOK)
    updated = points[...].astype(F32) + lax.dot_general(
        attended, w_out[...], (((0,), (0,)), ((), ())), preferred_element_type=F32
    )
    updated = updated.astype(BF16).astype(F32)
    normed = normalise(updated, gain[...]).astype(BF16)
    low, high = updated[:, :256], updated[:, 256:]
    for part in range(GROUPS):
        if part < 4:
            own[part].wait()
        else:
            lent[part - 4].wait_recv()
        hidden = jnp.dot(normed, slabs[part, :D], preferred_element_type=F32)
        hidden = (hidden * (0.5 * (1.0 + lax.erf(hidden * (2.0 ** -0.5))))).astype(BF16)
        low = low + jnp.dot(hidden, slabs[part, D:D + 256], preferred_element_type=F32)
        high = high + jnp.dot(hidden, slabs[part, D + 256:], preferred_element_type=F32)
    out_ref[:, :256] = low.astype(BF16)
    out_ref[:, 256:] = high.astype(BF16)

    def sent(index):
        @pl.when(across | (index != head))
        def _():
            copy(index, plane).wait_send()

    each(sent)
    for load in lent:
        load.wait_send()


def finish(points, packed, w_out, gain, weights):
    hbm = pl.BlockSpec(memory_space=pltpu.HBM)
    return pl.pallas_call(
        finish_kernel,
        out_shape=jax.ShapeDtypeStruct((TOK, D), BF16),
        in_specs=[hbm] * 8,
        out_specs=pl.BlockSpec(memory_space=pltpu.VMEM),
        scratch_shapes=[
            pltpu.VMEM((TOK, D), BF16),
            pltpu.VMEM((D, D), BF16),
            pltpu.VMEM((1, D), F32),
            pltpu.VMEM((GROUPS, 2 * D, 256), BF16),
            pltpu.VMEM((GROUPS, 64, TOK), BF16),
            pltpu.SemaphoreType.DMA((8,)),
            pltpu.SemaphoreType.DMA((8,)),
            pltpu.SemaphoreType.DMA((1,)),
            pltpu.SemaphoreType.DMA((3,)),
            pltpu.SemaphoreType.DMA((4,)),
            pltpu.SemaphoreType.DMA((4,)),
            pltpu.SemaphoreType.DMA((4,)),
        ],
        compiler_params=pltpu.CompilerParams(
            collective_id=1, has_side_effects=True, vmem_limit_bytes=40 << 20
        ),
        name="finish",
    )(points, packed, w_out, gain.reshape(1, D), *weights)


def exchange_kernel(
    points_ref, gain_ref, w_ref, scale_ref, place_ref, counts_ref, route_ref, local_ref, w1_ref, w2_ref,
    kv_out, q_out, route_out, local_out, own_out, own_top_out, weights_out,
    kv_ref, q_ref, raw, queries, keys, turned, lhs, scores, own, own_top,
    all_send, all_recv, ring_send, ring_recv, pair_send, pair_recv, route_sem, local_sem, load_sem, own_sem,
):
    column, plane, head = swap_ids()
    core = lax.rem(head, 2)
    spot = column * 4 + head // 2
    after, before = lax.rem(spot + 1, 16), lax.rem(spot + 15, 16)
    right = ((after // 4) * 8 + plane, lax.rem(after, 4) * 2 + core)
    left = ((before // 4) * 8 + plane, lax.rem(before, 4) * 2 + core)
    pair = (column * 8 + plane, head + 1 - 2 * core)
    partner = (column * 8 + head, plane)
    diagonal = plane == head
    across = jnp.logical_not(diagonal)

    barrier = pltpu.get_barrier_semaphore()

    def greet(index, _):
        @pl.when(across | (index != head))
        def _():
            pl.semaphore_signal(barrier, inc=1, device_id=(column * 8 + head, index), device_id_type=MESH)
        return 0

    lax.fori_loop(0, 8, greet, 0)
    for other in (right, left, pair):
        pl.semaphore_signal(barrier, inc=1, device_id=other, device_id_type=MESH)

    def enter():
        @pl.when(diagonal)
        def _():
            pl.semaphore_wait(barrier, 10)

        @pl.when(across)
        def _():
            pl.semaphore_wait(barrier, 11)

    def rows(half):
        return pl.ds(half * LANES, LANES)

    def spread(group, half, shard):
        return pltpu.make_async_remote_copy(
            src_ref=kv_ref.at[group, rows(half)],
            dst_ref=kv_out.at[4 + lax.rem(plane, 2), shard, rows(half)],
            send_sem=all_send.at[half, group],
            recv_sem=all_recv.at[half, shard],
            device_id=(column * 8 + group, plane),
            device_id_type=MESH,
        )

    def landed(half, shard):
        return pltpu.make_async_remote_copy(
            src_ref=kv_ref.at[0, rows(half)],
            dst_ref=kv_out.at[4 + core, shard, rows(half)],
            send_sem=all_send.at[half, 0],
            recv_sem=all_recv.at[half, shard],
            device_id=pair,
            device_id_type=MESH,
        )

    def spread_q(group, shard):
        return pltpu.make_async_remote_copy(
            src_ref=q_ref.at[group],
            dst_ref=q_out.at[shard],
            send_sem=all_send.at[2, group],
            recv_sem=all_recv.at[2, shard],
            device_id=(column * 8 + group, plane),
            device_id_type=MESH,
        )

    def at_home(half):
        return pltpu.make_async_copy(
            kv_ref.at[plane, rows(half)], kv_out.at[4 + core, head, rows(half)], local_sem.at[half]
        )

    q_at_home = pltpu.make_async_copy(q_ref.at[plane], q_out.at[head], local_sem.at[2])
    routes_at_home = [
        pltpu.make_async_copy(route_ref, route_out, local_sem.at[3]),
        pltpu.make_async_copy(local_ref, local_out, local_sem.at[4]),
    ]
    routes_sent = [
        pltpu.make_async_remote_copy(
            src_ref=source, dst_ref=target, send_sem=route_sem.at[0, index], recv_sem=route_sem.at[1, index],
            device_id=partner, device_id_type=MESH,
        )
        for index, (source, target) in enumerate(((route_ref, route_out), (local_ref, local_out)))
    ]

    def start(group):
        @pl.when(across | (group != plane))
        def _():
            spread(group, 0, head).start()
            spread(group, 1, head).start()

    def start_q(group):
        @pl.when(across | (group != plane))
        def _():
            spread_q(group, head).start()

    joins = [
        pltpu.make_async_copy(source, weights_out.at[rows_at], load_sem.at[2 + index])
        for index, (source, rows_at) in enumerate((
            (w1_ref, pl.ds(0, D)), (w2_ref.at[:, pl.ds(0, 256)], pl.ds(D, 256)), (w2_ref.at[:, pl.ds(256, 256)], pl.ds(D + 256, 256)),
        ))
    ]
    for join in joins:
        join.start()

    normed = normalise(points_ref[...].astype(F32), gain_ref[...]).astype(BF16)
    for couple in range(GROUPS // 2):
        columns = slice(384 * couple, 384 * couple + 384)
        projected = jnp.dot(normed, w_ref[:, columns], preferred_element_type=F32)
        projected = (projected * scale_ref[:, columns]).astype(BF16)
        kv = jnp.dot(projected, place_ref[:, :256], preferred_element_type=F32).astype(BF16)
        q = jnp.dot(projected[:128], place_ref[:, 256:512], preferred_element_type=F32)
        q = (q + jnp.dot(projected[128:], place_ref[:, 512:], preferred_element_type=F32)).astype(BF16)
        for side in range(2):
            kv_ref[2 * couple + side] = kv[:, 128 * side:128 * side + 128]
            q_ref[2 * couple + side] = q[:, 128 * side:128 * side + 128]
        if couple == 0:
            enter()
        start(2 * couple)
        start(2 * couple + 1)
    each(start_q)

    @pl.when(diagonal)
    def _():
        at_home(0).start()
        at_home(1).start()
        q_at_home.start()
        for copy in routes_at_home:
            copy.start()

    @pl.when(across)
    def _():
        for copy in routes_sent:
            copy.start()


    def moved(source, target, half, send, recv, to):
        return pltpu.make_async_remote_copy(
            src_ref=kv_out.at[source, :, rows(half)], dst_ref=kv_out.at[target, :, rows(half)],
            send_sem=send, recv_sem=recv, device_id=to, device_id_type=MESH,
        )

    def hop(way, step, half):
        if way == 0:
            source, to = 4 - 2 * step + core, right
            target = 2 - 2 * step + core
        else:
            source, to = 4 + 2 * step + core, left
            target = 6 + 2 * step + core
        return moved(source, target, half, ring_send.at[way, step, half], ring_recv.at[way, step, half], to)

    def shared(place, half):
        return moved(2 * place + core, 2 * place + core, half, pair_send.at[place, half], pair_recv.at[place, half], pair)

    def taken(place, half):
        return moved(2 * place + 1 - core, 2 * place + 1 - core, half, pair_send.at[place, half], pair_recv.at[place, half], pair)

    for half in range(2):
        def wait(shard):
            @pl.when(across | (shard != head))
            def _():
                landed(half, shard).wait_recv()

        each(wait)

        @pl.when(diagonal)
        def _():
            at_home(half).wait()

        hop(0, 0, half).start()
        hop(1, 0, half).start()
        shared(2, half).start()
    def wait_q(shard):
        @pl.when(across | (shard != head))
        def _():
            spread_q(0, shard).wait_recv()

    each(wait_q)

    @pl.when(diagonal)
    def _():
        q_at_home.wait()

    loads = [
        pltpu.make_async_copy(kv_out.at[4 + core], raw, load_sem.at[0]),
        pltpu.make_async_copy(q_out, queries, load_sem.at[1]),
    ]
    for load in loads:
        load.start()
    for load in loads:
        load.wait()

    def own_keys(shard):
        at = pl.ds(pl.multiple_of(shard * TOK, TOK), TOK)
        keys[at, :] = keyed_rows(raw[shard], counts_ref[(column * 8 + head) * GROUPS + shard])[1]
        turn_values(raw[shard], turned, at, TOK)

    each(own_keys)

    def own_saved(shard):
        return (
            pltpu.make_async_copy(own.at[shard], own_out.at[shard], own_sem.at[0, shard]),
            pltpu.make_async_copy(own_top.at[shard], own_top_out.at[shard], own_sem.at[1, shard]),
        )

    def own_patch(patch):
        def own_shard(part, _):
            shard = patch * 4 + part
            spread_heads(queries[shard], lhs)
            most = None
            for piece in range(2):
                at = slice(patch * PATCH + piece * CHUNK, patch * PATCH + piece * CHUNK + CHUNK)
                found = scores_of(keys[at, :], lhs)
                scores[piece] = found
                found = jnp.max(found, axis=0, keepdims=True)
                most = found if piece == 0 else jnp.maximum(most, found)
            own_top[shard] = most
            total = [None] * 4
            for piece in range(2):
                at = slice(patch * PATCH + piece * CHUNK, patch * PATCH + piece * CHUNK + CHUNK)
                weights = jnp.exp2(scores[piece] - most).astype(BF16)
                for index in range(4):
                    rows_of = slice(32 * index, 32 * index + 32)
                    term = jnp.dot(turned[rows_of, at], head_columns(weights, index), preferred_element_type=F32)
                    total[index] = term if piece == 0 else total[index] + term
            for index in range(4):
                own[shard, 32 * index:32 * index + 32] = total[index]
            for save in own_saved(shard):
                save.start()
            return 0

        lax.fori_loop(0, 4, own_shard, 0)

    for half in range(2):
        own_patch(half)
        hop(0, 0, half).wait_recv()
        hop(0, 1, half).start()
        hop(1, 0, half).wait_recv()
        hop(1, 1, half).start()
        shared(1, half).start()
        shared(3, half).start()
    for half in range(2):
        hop(0, 1, half).wait_recv()
        shared(0, half).start()
        hop(1, 1, half).wait_recv()
        shared(4, half).start()

    def sent(group):
        @pl.when(across | (group != plane))
        def _():
            spread(group, 0, head).wait_send()
            spread(group, 1, head).wait_send()
            spread_q(group, head).wait_send()

    each(sent)

    @pl.when(diagonal)
    def _():
        for copy in routes_at_home:
            copy.wait()

    @pl.when(across)
    def _():
        for copy in routes_sent:
            copy.wait()


    for half in range(2):
        for way in range(2):
            for step in range(2):
                hop(way, step, half).wait_send()
        for place in range(5):
            shared(place, half).wait_send()
            taken(place, half).wait_recv()
    for join in joins:
        join.wait()

    def saved(shard):
        for save in own_saved(shard):
            save.wait()

    each(saved)


def exchange(points, gain, w_qkv, counts, routes, local, w1, w2):
    scale = np.ones((1, 1536), np.float32)
    scale[0, np.arange(1536) % 48 < 16] = HEAD_DIM ** -0.5 * math.log2(math.e)
    vmem = pl.BlockSpec(memory_space=pltpu.VMEM)
    anywhere = pl.BlockSpec(memory_space=pltpu.HBM)
    return pl.pallas_call(
        exchange_kernel,
        out_shape=(
            jax.ShapeDtypeStruct((10, GROUPS, TOK, LANES), BF16),
            jax.ShapeDtypeStruct((GROUPS, LANES, LANES), BF16),
            jax.ShapeDtypeStruct((1, LANES), jnp.int32),
            jax.ShapeDtypeStruct((1, LANES), jnp.int32),
            jax.ShapeDtypeStruct((GROUPS, LANES, TOK), F32),
            jax.ShapeDtypeStruct((GROUPS, 1, ROWS), F32),
            jax.ShapeDtypeStruct((2 * D, 256), BF16),
        ),
        in_specs=[vmem] * 5 + [pl.BlockSpec(memory_space=pltpu.SMEM)] + [anywhere] * 4,
        out_specs=(anywhere,) * 7,
        scratch_shapes=[
            pltpu.VMEM((GROUPS, TOK, LANES), BF16),
            pltpu.VMEM((GROUPS, LANES, LANES), BF16),
            pltpu.VMEM((GROUPS, TOK, LANES), BF16),
            pltpu.VMEM((GROUPS, LANES, LANES), BF16),
            pltpu.VMEM((NPL * PATCH, LANES), BF16),
            pltpu.VMEM((LANES, NPL * PATCH), BF16),
            pltpu.VMEM((ROWS, LANES), BF16),
            pltpu.VMEM((2, CHUNK, ROWS), F32),
            pltpu.VMEM((GROUPS, LANES, TOK), F32),
            pltpu.VMEM((GROUPS, 1, ROWS), F32),
            pltpu.SemaphoreType.DMA((3, 8)),
            pltpu.SemaphoreType.DMA((3, 8)),
            pltpu.SemaphoreType.DMA((2, 2, 2)),
            pltpu.SemaphoreType.DMA((2, 2, 2)),
            pltpu.SemaphoreType.DMA((5, 2)),
            pltpu.SemaphoreType.DMA((5, 2)),
            pltpu.SemaphoreType.DMA((2, 2)),
            pltpu.SemaphoreType.DMA((5,)),
            pltpu.SemaphoreType.DMA((5,)),
            pltpu.SemaphoreType.DMA((2, 8)),
        ],
        compiler_params=pltpu.CompilerParams(collective_id=0, has_side_effects=True, vmem_limit_bytes=60 << 20),
        name="exchange",
    )(
        points, gain.reshape(1, D), w_qkv, jnp.asarray(scale), jnp.asarray(placing(), BF16),
        counts, routes, local, w1, w2,
    )


def per_device(
    points, gain_attn, w_qkv, w_out, gain_mlp, w_fc1, w_fc2, contact_route, contact_patch, counts
):
    slots, q, routes, local, sums, tops, joined = exchange(
        points, gain_attn, w_qkv, counts, contact_route.reshape(1, -1), contact_patch, w_fc1, w_fc2
    )
    weights = [joined]
    for step in range(1, 4):
        pairs = [(head, (head + 2 * step) % GROUPS) for head in range(GROUPS)]
        weights.append(lax.ppermute(joined, "head", pairs))
    packed = attend(routes, local, counts, q, slots.reshape(20, PATCH, LANES), sums, tops)
    return finish(points, packed, w_out, gain_mlp, weights)


def solution(mesh):
    return jax.shard_map(
        per_device,
        mesh=mesh,
        in_specs=(
            P(("seq", "head"), None), P(), P(), P(), P(), P(None, "head"), P("head", None),
            P("head", None, None), P("head", None), P(),
        ),
        out_specs=P(("seq", "head"), None),
        check_vma=False,
    )
```

```python
import functools
import math

import jax
import jax.numpy as jnp
import numpy as np
from jax import lax
from jax.experimental import pallas as pl
from jax.experimental.pallas import tpu as pltpu
from jax.sharding import PartitionSpec as P

D = 512
HEADS = 32
HEAD_DIM = 16
PATCH = 1024
CB = 2
NPL = 2
REACH = 4
TOK = 256
GROUPS = 8
LANES = 128
CHUNK = 512
F32 = jnp.float32
BF16 = jnp.bfloat16
MASKED = -3.3e38
ROWS = 8 * LANES
MESH = pl.DeviceIdType.MESH


def placing():
    kv = np.zeros((384, 256), np.float32)
    low = np.zeros((384, 256), np.float32)
    high = np.zeros((384, 256), np.float32)
    for group in range(2):
        for head in range(4):
            for dim in range(HEAD_DIM):
                source = group * 192 + head * 48 + dim
                lane = group * 128 + head * 16 + dim
                low[source, lane] = 1
                high[source, lane + 64] = 1
                kv[source + 16, lane] = 1
                kv[source + 32, lane + 64] = 1
    return np.concatenate([kv, low, high], axis=1)


def lane_of(shape):
    return lax.broadcasted_iota(jnp.int32, shape, len(shape) - 1)


def normalise(values, gain):
    centred = values - jnp.mean(values, axis=-1, keepdims=True)
    spread = jnp.mean(centred * centred, axis=-1, keepdims=True)
    return centred * lax.rsqrt(spread + 1e-05) * gain


def swap_ids():
    seq, head = lax.axis_index("seq"), lax.axis_index("head")
    column = seq // 8
    return column, seq - column * 8, head


def iotas(rows):
    shape = (rows, LANES)
    return lax.broadcasted_iota(jnp.int32, shape, 0), lax.broadcasted_iota(jnp.int32, shape, 1)


def value_picker():
    row, lane = iotas(LANES)
    return ((row % 32 < 16) & (lane == 64 + row // 32 * 16 + row % 32)).astype(F32).astype(BF16)


def keyed_rows(block, count):
    row, lane = iotas(TOK)
    zero = jnp.zeros((TOK, LANES), BF16)
    valid = row < count
    flag = jnp.where(valid, zero, jnp.where(lane < 66, jnp.full_like(zero, MASKED), zero))
    keyed = jnp.where((lane < 64) & valid, block, zero)
    return keyed, jnp.where(lane < 64, keyed, flag)


def norms(values):
    row, lane = iotas(LANES)
    sum_of = ((lane == row // 16) & (lane < 4)).astype(F32).astype(BF16)
    size = jnp.minimum(jnp.abs(values), jnp.full_like(values, 1e15))
    size = jnp.where(lax.broadcasted_iota(jnp.int32, values.shape, 1) < 64, size, jnp.zeros_like(size))
    return jnp.max(jnp.dot(size * size, sum_of, preferred_element_type=F32), axis=0, keepdims=True)


def turn_values(vals, turned, at, size):
    ones_row = lax.broadcasted_iota(jnp.int32, (LANES, size), 0) % 32 >= 16
    picked = lax.dot_general(value_picker(), vals, (((1,), (1,)), ((), ())), preferred_element_type=F32)
    turned[:, at] = jnp.where(ones_row, 1.0, picked).astype(BF16)


def half_of(packed, half):
    return packed if half == 0 else pltpu.roll(packed.astype(F32), 64, 1).astype(BF16)


def spread_heads(packed, lhs):
    _, lane = iotas(LANES)
    flags = jnp.where((lane >= 64) & (lane < 66), jnp.ones_like(packed), jnp.zeros_like(packed))
    for half in range(2):
        q = half_of(packed, half)
        for head in range(4):
            mine = (lane >= 16 * head) & (lane < 16 * head + 16)
            lhs[pl.ds((head * 2 + half) * LANES, LANES), :] = jnp.where(mine, q, flags)


def scores_of(keys, lhs):
    return lax.dot_general(keys, lhs[...], (((1,), (1,)), ((), ())), preferred_element_type=F32)


def head_columns(values, head):
    return values[:, TOK * head:TOK * head + TOK]


def attend_kernel(
    routes_hbm, local_hbm, counts_hbm, q_hbm, kv_ref, own_hbm, own_top_hbm, own_size_hbm, own_query_hbm, out_ref,
    routes_ref, local_ref, counts_ref, q_ref, own_ref, own_top_ref, own_size_ref, own_query_ref,
    raw, keys, vals, turned, lhs, acc, top, done, sems, small_sems, out_sems,
):
    column, _, head_index = swap_ids()
    seq = column * 8 + head_index
    core = lax.rem(head_index, 2)
    loads = [
        pltpu.make_async_copy(source, target, small_sems.at[index])
        for index, (source, target) in enumerate((
            (routes_hbm, routes_ref), (local_hbm, local_ref), (counts_hbm, counts_ref),
            (q_hbm, q_ref), (own_hbm, own_ref), (own_top_hbm, own_top_ref),
            (own_size_hbm, own_size_ref), (own_query_hbm, own_query_ref),
        ))
    ]
    for load in loads:
        load.start()
    for load in loads[:3]:
        load.wait()

    def source(patch, which):
        row = seq * NPL * CB + patch * CB + which
        route = routes_ref[0, row]
        offset = jnp.where(route < REACH, route - REACH, route - REACH + 1)
        local = local_ref[0, row]
        owner = lax.rem(seq + offset + 32, 32)
        return (offset + REACH + core) * NPL + local, owner * GROUPS + local * 4

    for patch in range(NPL):
        for which in range(CB):
            slot, _ = source(patch, which)
            pltpu.make_async_copy(kv_ref.at[slot], raw.at[patch * CB + which], sems.at[patch * CB + which]).start()
    for load in loads[3:]:
        load.wait()

    _, lane_kv = iotas(TOK)
    zero = jnp.zeros((TOK, LANES), BF16)

    def patch_body(patch, _):
        for which in range(CB):
            pltpu.make_async_copy(kv_ref.at[0], raw.at[patch * CB + which], sems.at[patch * CB + which]).wait()

        first = jnp.int32(0)
        key_top = jnp.zeros((1, LANES), F32)
        val_top = jnp.zeros((1, LANES), F32)
        for which in range(CB):
            _, shard = source(patch, which)
            for part in range(4):
                count = counts_ref[shard + part]
                block = raw[patch * CB + which, TOK * part:TOK * part + TOK, :]
                keyed, marked = keyed_rows(block, count)
                at = pl.ds(pl.multiple_of(first, 16), TOK)
                keys[at, :] = marked
                vals[at, :] = block
                key_top = jnp.maximum(key_top, norms(keyed))
                size = jnp.max(jnp.where(lane_kv < 64, zero, jnp.abs(block)).astype(F32), axis=0, keepdims=True)
                val_top = jnp.maximum(val_top, size)
                first = first + (count + 15) // 16 * 16
        tail = pl.ds(pl.multiple_of(first, 16), TOK)
        keys[tail, :] = keyed_rows(zero, 0)[1]
        vals[tail, :] = zero
        pieces = (first + TOK - 1) // TOK
        chunks = pieces // 2
        odd = pieces % 2 == 1

        def turn(piece, _):
            at = pl.ds(pl.multiple_of(piece * TOK, TOK), TOK)
            turn_values(vals[at, :], turned, at, TOK)
            return 0

        lax.fori_loop(0, pieces, turn, 0)

        query_top, own_size = own_query_ref[patch * 4], own_size_ref[patch * 4]
        for part in range(1, 4):
            query_top = jnp.maximum(query_top, own_query_ref[patch * 4 + part])
            own_size = jnp.maximum(own_size, own_size_ref[patch * 4 + part])
        sizes = jnp.maximum(query_top * key_top * (1.0 / 3000.0), val_top * 1e-9)
        fits = jnp.maximum(jnp.max(sizes), jnp.max(own_size)) < 1.0

        def shards_body(couple, _):
            shards = [patch * 4 + couple * 2 + side for side in range(2)]
            for side in range(2):
                spread_heads(q_ref[shards[side]], lhs.at[pl.ds(side * ROWS, ROWS)])

            def over_chunks(body):
                def chunk_body(chunk, _):
                    body(pl.ds(pl.multiple_of(chunk * CHUNK, CHUNK), CHUNK))
                    return 0

                lax.fori_loop(0, chunks, chunk_body, 0)

                @pl.when(odd)
                def _():
                    body(pl.ds(pl.multiple_of(chunks * CHUNK, CHUNK), TOK))

            def begin(side, scale):
                for head in range(4):
                    rows = slice(32 * head, 32 * head + 32)
                    acc[side, rows] = own_ref[shards[side], rows] * head_columns(scale, head)

            def gather(at, weights):
                for side in range(2):
                    for head in range(4):
                        rows = slice(32 * head, 32 * head + 32)
                        acc[side, rows] += jnp.dot(
                            turned[rows, at], head_columns(weights, side * 4 + head), preferred_element_type=F32
                        )

            @pl.when(fits)
            def _():
                for side in range(2):
                    begin(side, jnp.exp2(own_top_ref[shards[side]]))
                over_chunks(lambda at: gather(at, jnp.exp2(scores_of(keys[at, :], lhs)).astype(BF16)))

            @pl.when(jnp.logical_not(fits))
            def _():
                for side in range(2):
                    top[:, pl.ds(side * ROWS, ROWS)] = own_top_ref[shards[side]]

                def raise_top(at):
                    top[...] = jnp.maximum(top[...], jnp.max(scores_of(keys[at, :], lhs), axis=0, keepdims=True))

                over_chunks(raise_top)
                for side in range(2):
                    begin(side, jnp.exp2(own_top_ref[shards[side]] - top[:, pl.ds(side * ROWS, ROWS)]))
                over_chunks(lambda at: gather(at, jnp.exp2(scores_of(keys[at, :], lhs) - top[...]).astype(BF16)))

            for side in range(2):
                joined = [
                    acc[side, 32 * head:32 * head + 16] / acc[side, 32 * head + 16:32 * head + 32] for head in range(4)
                ]
                shard = shards[side]
                done[shard] = jnp.concatenate(joined, axis=0).astype(BF16)
                pltpu.make_async_copy(done.at[shard], out_ref.at[shard], out_sems.at[shard]).start()
            return 0

        lax.fori_loop(0, 2, shards_body, 0)
        return 0

    lax.fori_loop(0, NPL, patch_body, 0)
    for shard in range(GROUPS):
        pltpu.make_async_copy(done.at[shard], out_ref.at[shard], out_sems.at[shard]).wait()


def attend(routes, local, counts, q, kv, own, own_top, own_size, own_query):
    hbm = pl.BlockSpec(memory_space=pltpu.HBM)
    most = CB * PATCH + TOK
    return pl.pallas_call(
        attend_kernel,
        out_shape=jax.ShapeDtypeStruct((GROUPS, 64, TOK), BF16),
        in_specs=[hbm] * 9,
        out_specs=hbm,
        scratch_shapes=[
            pltpu.SMEM((1, LANES), jnp.int32),
            pltpu.SMEM((1, LANES), jnp.int32),
            pltpu.SMEM((256,), jnp.int32),
            pltpu.VMEM((GROUPS, LANES, LANES), BF16),
            pltpu.VMEM((GROUPS, LANES, TOK), F32),
            pltpu.VMEM((GROUPS, 1, ROWS), F32),
            pltpu.VMEM((GROUPS, 1, ROWS), F32),
            pltpu.VMEM((GROUPS, 1, LANES), F32),
            pltpu.VMEM((NPL * CB, PATCH, LANES), BF16),
            pltpu.VMEM((most, LANES), BF16),
            pltpu.VMEM((most, LANES), BF16),
            pltpu.VMEM((LANES, most), BF16),
            pltpu.VMEM((2 * ROWS, LANES), BF16),
            pltpu.VMEM((2, LANES, TOK), F32),
            pltpu.VMEM((1, 2 * ROWS), F32),
            pltpu.VMEM((GROUPS, 64, TOK), BF16),
            pltpu.SemaphoreType.DMA((NPL * CB,)),
            pltpu.SemaphoreType.DMA((8,)),
            pltpu.SemaphoreType.DMA((8,)),
        ],
        compiler_params=pltpu.CompilerParams(vmem_limit_bytes=60 << 20),
        cost_estimate=pl.CostEstimate(flops=20_000_000_000, bytes_accessed=6_000_000, transcendentals=17_000_000),
        name="attend",
    )(routes, local, counts, q, kv, own, own_top, own_size, own_query)


def each(body):
    def step(index, _):
        body(index)
        return 0

    lax.fori_loop(0, 8, step, 0)


def finish_kernel(
    points_ref, packed_ref, w_out_ref, gain_ref, w0_ref, w1_ref, w2_ref, w3_ref, out_ref,
    points, w_out, gain, slabs, back, send, recv, local_sem, load_sem, weight_sem, pair_send, pair_recv,
):
    column, plane, head = swap_ids()
    diagonal = plane == head
    across = jnp.logical_not(diagonal)
    barrier = pltpu.get_barrier_semaphore()

    def greet(group):
        @pl.when(across | (group != plane))
        def _():
            pl.semaphore_signal(barrier, inc=1, device_id=(column * 8 + group, plane), device_id_type=MESH)

    each(greet)
    pair = (column * 8 + plane, head + 1 - 2 * lax.rem(head, 2))
    pl.semaphore_signal(barrier, inc=1, device_id=pair, device_id_type=MESH)
    loads = [
        pltpu.make_async_copy(points_ref, points, load_sem.at[0]),
        pltpu.make_async_copy(w_out_ref, w_out, load_sem.at[1]),
        pltpu.make_async_copy(gain_ref, gain, load_sem.at[2]),
    ]
    for load in loads:
        load.start()

    shards = (w0_ref, w1_ref, w2_ref, w3_ref)
    own = [pltpu.make_async_copy(shard, slabs.at[part], weight_sem.at[part]) for part, shard in enumerate(shards)]
    lent = [
        pltpu.make_async_remote_copy(
            src_ref=shard, dst_ref=slabs.at[4 + part], send_sem=pair_send.at[part], recv_sem=pair_recv.at[part],
            device_id=pair, device_id_type=MESH,
        )
        for part, shard in enumerate(shards)
    ]
    for load in own:
        load.start()

    @pl.when(diagonal)
    def _():
        pl.semaphore_wait(barrier, 8)

    @pl.when(across)
    def _():
        pl.semaphore_wait(barrier, 9)

    def copy(shard, group):
        return pltpu.make_async_remote_copy(
            src_ref=packed_ref.at[shard], dst_ref=back.at[group],
            send_sem=send.at[shard], recv_sem=recv.at[group],
            device_id=(column * 8 + head, shard), device_id_type=MESH,
        )

    at_home = pltpu.make_async_copy(packed_ref.at[head], back.at[plane], local_sem.at[0])

    def start(shard):
        @pl.when(across | (shard != head))
        def _():
            copy(shard, plane).start()

    each(start)
    for load in lent:
        load.start()

    @pl.when(diagonal)
    def _():
        at_home.start()
        at_home.wait()

    for load in loads:
        load.wait()

    def wait(index):
        @pl.when(across | (index != plane))
        def _():
            copy(0, index).wait_recv()

    each(wait)

    attended = back[...].reshape(D, TOK)
    updated = points[...].astype(F32) + lax.dot_general(
        attended, w_out[...], (((0,), (0,)), ((), ())), preferred_element_type=F32
    )
    updated = updated.astype(BF16).astype(F32)
    normed = normalise(updated, gain[...]).astype(BF16)
    low, high = updated[:, :256], updated[:, 256:]
    for part in range(GROUPS):
        if part < 4:
            own[part].wait()
        else:
            lent[part - 4].wait_recv()
        hidden = jnp.dot(normed, slabs[part, :D], preferred_element_type=F32)
        hidden = (hidden * (0.5 * (1.0 + lax.erf(hidden * (2.0 ** -0.5))))).astype(BF16)
        low = low + jnp.dot(hidden, slabs[part, D:D + 256], preferred_element_type=F32)
        high = high + jnp.dot(hidden, slabs[part, D + 256:], preferred_element_type=F32)
    out_ref[:, :256] = low.astype(BF16)
    out_ref[:, 256:] = high.astype(BF16)

    def sent(index):
        @pl.when(across | (index != head))
        def _():
            copy(index, plane).wait_send()

    each(sent)
    for load in lent:
        load.wait_send()


def finish(points, packed, w_out, gain, weights):
    hbm = pl.BlockSpec(memory_space=pltpu.HBM)
    return pl.pallas_call(
        finish_kernel,
        out_shape=jax.ShapeDtypeStruct((TOK, D), BF16),
        in_specs=[hbm] * 8,
        out_specs=pl.BlockSpec(memory_space=pltpu.VMEM),
        scratch_shapes=[
            pltpu.VMEM((TOK, D), BF16),
            pltpu.VMEM((D, D), BF16),
            pltpu.VMEM((1, D), F32),
            pltpu.VMEM((GROUPS, 2 * D, 256), BF16),
            pltpu.VMEM((GROUPS, 64, TOK), BF16),
            pltpu.SemaphoreType.DMA((8,)),
            pltpu.SemaphoreType.DMA((8,)),
            pltpu.SemaphoreType.DMA((1,)),
            pltpu.SemaphoreType.DMA((3,)),
            pltpu.SemaphoreType.DMA((4,)),
            pltpu.SemaphoreType.DMA((4,)),
            pltpu.SemaphoreType.DMA((4,)),
        ],
        compiler_params=pltpu.CompilerParams(
            collective_id=1, has_side_effects=True, vmem_limit_bytes=40 << 20
        ),
        name="finish",
    )(points, packed, w_out, gain.reshape(1, D), *weights)


def exchange_kernel(
    points_ref, gain_ref, w_ref, scale_ref, place_ref, counts_ref, route_ref, local_ref, w1_ref, w2_ref,
    kv_out, q_out, route_out, local_out, own_out, own_top_out, own_size_out, own_query_out, weights_out,
    kv_ref, q_ref, raw, queries, keys, turned, lhs, scores, own, own_top, own_size, own_query,
    all_send, all_recv, ring_send, ring_recv, pair_send, pair_recv, route_sem, local_sem, load_sem, own_sem, over_send, over_recv,
):
    column, plane, head = swap_ids()
    core = lax.rem(head, 2)
    spot = column * 4 + head // 2
    after, before = lax.rem(spot + 1, 16), lax.rem(spot + 15, 16)
    right = ((after // 4) * 8 + plane, lax.rem(after, 4) * 2 + core)
    left = ((before // 4) * 8 + plane, lax.rem(before, 4) * 2 + core)
    pair = (column * 8 + plane, head + 1 - 2 * core)
    partner = (column * 8 + head, plane)
    diagonal = plane == head
    across = jnp.logical_not(diagonal)

    barrier = pltpu.get_barrier_semaphore()

    def greet(index, _):
        @pl.when(across | (index != head))
        def _():
            pl.semaphore_signal(barrier, inc=1, device_id=(column * 8 + head, index), device_id_type=MESH)
        return 0

    lax.fori_loop(0, 8, greet, 0)
    over_right = (lax.rem(column + 1, 4) * 8 + plane, head)
    over_left = (lax.rem(column + 3, 4) * 8 + plane, head)
    for other in (right, left, pair, over_right, over_left):
        pl.semaphore_signal(barrier, inc=1, device_id=other, device_id_type=MESH)

    def enter():
        @pl.when(diagonal)
        def _():
            pl.semaphore_wait(barrier, 12)

        @pl.when(across)
        def _():
            pl.semaphore_wait(barrier, 13)

    def rows(half):
        return pl.ds(half * LANES, LANES)

    def spread(group, half, shard):
        return pltpu.make_async_remote_copy(
            src_ref=kv_ref.at[group, rows(half)],
            dst_ref=kv_out.at[4 + lax.rem(plane, 2), shard, rows(half)],
            send_sem=all_send.at[half, group],
            recv_sem=all_recv.at[half, shard],
            device_id=(column * 8 + group, plane),
            device_id_type=MESH,
        )

    def landed(half, shard):
        return pltpu.make_async_remote_copy(
            src_ref=kv_ref.at[0, rows(half)],
            dst_ref=kv_out.at[4 + core, shard, rows(half)],
            send_sem=all_send.at[half, 0],
            recv_sem=all_recv.at[half, shard],
            device_id=pair,
            device_id_type=MESH,
        )

    def spread_q(group, shard):
        return pltpu.make_async_remote_copy(
            src_ref=q_ref.at[group],
            dst_ref=q_out.at[shard],
            send_sem=all_send.at[2, group],
            recv_sem=all_recv.at[2, shard],
            device_id=(column * 8 + group, plane),
            device_id_type=MESH,
        )

    def at_home(half):
        return pltpu.make_async_copy(
            kv_ref.at[plane, rows(half)], kv_out.at[4 + core, head, rows(half)], local_sem.at[half]
        )

    q_at_home = pltpu.make_async_copy(q_ref.at[plane], q_out.at[head], local_sem.at[2])
    routes_at_home = [
        pltpu.make_async_copy(route_ref, route_out, local_sem.at[3]),
        pltpu.make_async_copy(local_ref, local_out, local_sem.at[4]),
    ]
    routes_sent = [
        pltpu.make_async_remote_copy(
            src_ref=source, dst_ref=target, send_sem=route_sem.at[0, index], recv_sem=route_sem.at[1, index],
            device_id=partner, device_id_type=MESH,
        )
        for index, (source, target) in enumerate(((route_ref, route_out), (local_ref, local_out)))
    ]

    def start(group):
        @pl.when(across | (group != plane))
        def _():
            spread(group, 0, head).start()
            spread(group, 1, head).start()

    def start_q(group):
        @pl.when(across | (group != plane))
        def _():
            spread_q(group, head).start()

    joins = [
        pltpu.make_async_copy(source, weights_out.at[rows_at], load_sem.at[2 + index])
        for index, (source, rows_at) in enumerate((
            (w1_ref, pl.ds(0, D)), (w2_ref.at[:, pl.ds(0, 256)], pl.ds(D, 256)), (w2_ref.at[:, pl.ds(256, 256)], pl.ds(D + 256, 256)),
        ))
    ]
    for join in joins:
        join.start()

    normed = normalise(points_ref[...].astype(F32), gain_ref[...]).astype(BF16)
    for couple in range(GROUPS // 2):
        columns = slice(384 * couple, 384 * couple + 384)
        projected = jnp.dot(normed, w_ref[:, columns], preferred_element_type=F32)
        projected = (projected * scale_ref[:, columns]).astype(BF16)
        kv = jnp.dot(projected, place_ref[:, :256], preferred_element_type=F32).astype(BF16)
        q = jnp.dot(projected[:128], place_ref[:, 256:512], preferred_element_type=F32)
        q = (q + jnp.dot(projected[128:], place_ref[:, 512:], preferred_element_type=F32)).astype(BF16)
        for side in range(2):
            kv_ref[2 * couple + side] = kv[:, 128 * side:128 * side + 128]
            q_ref[2 * couple + side] = q[:, 128 * side:128 * side + 128]
        if couple == 0:
            enter()
        start(2 * couple)
        start(2 * couple + 1)
    each(start_q)

    @pl.when(diagonal)
    def _():
        at_home(0).start()
        at_home(1).start()
        q_at_home.start()
        for copy in routes_at_home:
            copy.start()

    @pl.when(across)
    def _():
        for copy in routes_sent:
            copy.start()


    def moved(source, target, half, send, recv, to):
        return pltpu.make_async_remote_copy(
            src_ref=kv_out.at[source, :, rows(half)], dst_ref=kv_out.at[target, :, rows(half)],
            send_sem=send, recv_sem=recv, device_id=to, device_id_type=MESH,
        )

    def hop(way, step, half):
        if way == 0:
            source, to = 4 - 2 * step + core, right
            target = 2 - 2 * step + core
        else:
            source, to = 4 + 2 * step + core, left
            target = 6 + 2 * step + core
        return moved(source, target, half, ring_send.at[way, step, half], ring_recv.at[way, step, half], to)

    def shared(place, half):
        return moved(2 * place + core, 2 * place + core, half, pair_send.at[place, half], pair_recv.at[place, half], pair)

    def taken(place, half):
        return moved(2 * place + 1 - core, 2 * place + 1 - core, half, pair_send.at[place, half], pair_recv.at[place, half], pair)

    for half in range(2):
        def wait(shard):
            @pl.when(across | (shard != head))
            def _():
                landed(half, shard).wait_recv()

        each(wait)

        @pl.when(diagonal)
        def _():
            at_home(half).wait()

        hop(0, 0, half).start()
        hop(1, 0, half).start()
        shared(2, half).start()
    def wait_q(shard):
        @pl.when(across | (shard != head))
        def _():
            spread_q(0, shard).wait_recv()

    each(wait_q)

    @pl.when(diagonal)
    def _():
        q_at_home.wait()

    loads = [
        pltpu.make_async_copy(kv_out.at[4 + core], raw, load_sem.at[0]),
        pltpu.make_async_copy(q_out, queries, load_sem.at[1]),
    ]
    for load in loads:
        load.start()
    for load in loads:
        load.wait()

    def own_keys(shard):
        at = pl.ds(pl.multiple_of(shard * TOK, TOK), TOK)
        keys[at, :] = keyed_rows(raw[shard], counts_ref[(column * 8 + head) * GROUPS + shard])[1]
        turn_values(raw[shard], turned, at, TOK)

    each(own_keys)

    def own_saved(shard):
        return (
            pltpu.make_async_copy(own.at[shard], own_out.at[shard], own_sem.at[0, shard]),
            pltpu.make_async_copy(own_top.at[shard], own_top_out.at[shard], own_sem.at[1, shard]),
            pltpu.make_async_copy(own_size.at[shard], own_size_out.at[shard], own_sem.at[2, shard]),
            pltpu.make_async_copy(own_query.at[shard], own_query_out.at[shard], own_sem.at[3, shard]),
        )

    def own_run(begin, end):
        def own_shard(shard, _):
            patch = shard // 4
            packed = queries[shard]
            spread_heads(packed, lhs)
            most = None
            spots = [pl.ds(pl.multiple_of(patch * PATCH + piece * CHUNK, CHUNK), CHUNK) for piece in range(2)]
            for piece in range(2):
                found = scores_of(keys[spots[piece], :], lhs)
                scores[piece] = found
                found = jnp.max(found, axis=0, keepdims=True)
                most = found if piece == 0 else jnp.maximum(most, found)
            own_top[shard] = most
            total = [None] * 4
            for piece in range(2):
                weights = jnp.exp2(scores[piece] - most).astype(BF16)
                for index in range(4):
                    rows_of = slice(32 * index, 32 * index + 32)
                    term = jnp.dot(
                        turned[rows_of, spots[piece]], head_columns(weights, index), preferred_element_type=F32
                    )
                    total[index] = term if piece == 0 else total[index] + term
            for index in range(4):
                own[shard, 32 * index:32 * index + 32] = total[index]
                columns = slice(TOK * index, TOK * index + TOK)
                size = jnp.max(jnp.abs(total[index]), axis=0, keepdims=True) * 1e-12
                own_size[shard, :, columns] = jnp.maximum(size, jnp.abs(most[:, columns]) * (1.0 / 55.0))
            own_query[shard] = jnp.maximum(norms(half_of(packed, 0)), norms(half_of(packed, 1)))
            for save in own_saved(shard):
                save.start()
            return 0

        lax.fori_loop(begin, end, own_shard, 0)

    def swapped(way):
        if way == 0:
            source, target, half, to = 8 + core, core, 1, over_right
        else:
            source, target, half, to = core, 8 + core, 0, over_left
        return moved(source, target, half, over_send.at[way], over_recv.at[way], to)

    own_run(0, 5)
    hop(0, 0, 0).wait_recv()
    hop(0, 1, 0).start()
    hop(1, 0, 1).wait_recv()
    hop(1, 1, 1).start()
    shared(1, 0).start()
    shared(3, 1).start()
    hop(0, 0, 1).wait_recv()
    shared(1, 1).start()
    hop(1, 0, 0).wait_recv()
    shared(3, 0).start()
    own_run(5, 8)
    hop(0, 1, 0).wait_recv()
    swapped(1).start()
    hop(1, 1, 1).wait_recv()
    swapped(0).start()
    shared(0, 0).start()
    shared(4, 1).start()
    swapped(0).wait_recv()
    shared(0, 1).start()
    swapped(1).wait_recv()
    shared(4, 0).start()

    def sent(group):
        @pl.when(across | (group != plane))
        def _():
            spread(group, 0, head).wait_send()
            spread(group, 1, head).wait_send()
            spread_q(group, head).wait_send()

    each(sent)

    @pl.when(diagonal)
    def _():
        for copy in routes_at_home:
            copy.wait()

    @pl.when(across)
    def _():
        for copy in routes_sent:
            copy.wait()


    for half in range(2):
        for way in range(2):
            hop(way, 0, half).wait_send()
        for place in range(5):
            shared(place, half).wait_send()
            taken(place, half).wait_recv()
    hop(0, 1, 0).wait_send()
    hop(1, 1, 1).wait_send()
    swapped(0).wait_send()
    swapped(1).wait_send()
    for join in joins:
        join.wait()

    def saved(shard):
        for save in own_saved(shard):
            save.wait()

    each(saved)


def exchange(points, gain, w_qkv, counts, routes, local, w1, w2):
    scale = np.ones((1, 1536), np.float32)
    scale[0, np.arange(1536) % 48 < 16] = HEAD_DIM ** -0.5 * math.log2(math.e)
    vmem = pl.BlockSpec(memory_space=pltpu.VMEM)
    anywhere = pl.BlockSpec(memory_space=pltpu.HBM)
    return pl.pallas_call(
        exchange_kernel,
        out_shape=(
            jax.ShapeDtypeStruct((10, GROUPS, TOK, LANES), BF16),
            jax.ShapeDtypeStruct((GROUPS, LANES, LANES), BF16),
            jax.ShapeDtypeStruct((1, LANES), jnp.int32),
            jax.ShapeDtypeStruct((1, LANES), jnp.int32),
            jax.ShapeDtypeStruct((GROUPS, LANES, TOK), F32),
            jax.ShapeDtypeStruct((GROUPS, 1, ROWS), F32),
            jax.ShapeDtypeStruct((GROUPS, 1, ROWS), F32),
            jax.ShapeDtypeStruct((GROUPS, 1, LANES), F32),
            jax.ShapeDtypeStruct((2 * D, 256), BF16),
        ),
        in_specs=[vmem] * 5 + [pl.BlockSpec(memory_space=pltpu.SMEM)] + [anywhere] * 4,
        out_specs=(anywhere,) * 9,
        scratch_shapes=[
            pltpu.VMEM((GROUPS, TOK, LANES), BF16),
            pltpu.VMEM((GROUPS, LANES, LANES), BF16),
            pltpu.VMEM((GROUPS, TOK, LANES), BF16),
            pltpu.VMEM((GROUPS, LANES, LANES), BF16),
            pltpu.VMEM((NPL * PATCH, LANES), BF16),
            pltpu.VMEM((LANES, NPL * PATCH), BF16),
            pltpu.VMEM((ROWS, LANES), BF16),
            pltpu.VMEM((2, CHUNK, ROWS), F32),
            pltpu.VMEM((GROUPS, LANES, TOK), F32),
            pltpu.VMEM((GROUPS, 1, ROWS), F32),
            pltpu.VMEM((GROUPS, 1, ROWS), F32),
            pltpu.VMEM((GROUPS, 1, LANES), F32),
            pltpu.SemaphoreType.DMA((3, 8)),
            pltpu.SemaphoreType.DMA((3, 8)),
            pltpu.SemaphoreType.DMA((2, 2, 2)),
            pltpu.SemaphoreType.DMA((2, 2, 2)),
            pltpu.SemaphoreType.DMA((5, 2)),
            pltpu.SemaphoreType.DMA((5, 2)),
            pltpu.SemaphoreType.DMA((2, 2)),
            pltpu.SemaphoreType.DMA((5,)),
            pltpu.SemaphoreType.DMA((5,)),
            pltpu.SemaphoreType.DMA((4, 8)),
            pltpu.SemaphoreType.DMA((2,)),
            pltpu.SemaphoreType.DMA((2,)),
        ],
        compiler_params=pltpu.CompilerParams(collective_id=0, has_side_effects=True, vmem_limit_bytes=60 << 20),
        name="exchange",
    )(
        points, gain.reshape(1, D), w_qkv, jnp.asarray(scale), jnp.asarray(placing(), BF16),
        counts, routes, local, w1, w2,
    )


def per_device(
    points, gain_attn, w_qkv, w_out, gain_mlp, w_fc1, w_fc2, contact_route, contact_patch, counts
):
    slots, q, routes, local, sums, tops, sizes, tallest, joined = exchange(
        points, gain_attn, w_qkv, counts, contact_route.reshape(1, -1), contact_patch, w_fc1, w_fc2
    )
    weights = [joined]
    for step in range(1, 4):
        pairs = [(head, (head + 2 * step) % GROUPS) for head in range(GROUPS)]
        weights.append(lax.ppermute(joined, "head", pairs))
    packed = attend(routes, local, counts, q, slots.reshape(20, PATCH, LANES), sums, tops, sizes, tallest)
    return finish(points, packed, w_out, gain_mlp, weights)


def solution(mesh):
    return jax.shard_map(
        per_device,
        mesh=mesh,
        in_specs=(
            P(("seq", "head"), None), P(), P(), P(), P(), P(None, "head"), P("head", None),
            P("head", None, None), P("head", None), P(),
        ),
        out_specs=P(("seq", "head"), None),
        check_vma=False,
    )
```

```python
import functools
import math

import jax
import jax.numpy as jnp
import numpy as np
from jax import lax
from jax.experimental import pallas as pl
from jax.experimental.pallas import tpu as pltpu
from jax.sharding import PartitionSpec as P

D = 512
HEADS = 32
HEAD_DIM = 16
PATCH = 1024
CB = 2
NPL = 2
REACH = 4
TOK = 256
GROUPS = 8
LANES = 128
CHUNK = 512
F32 = jnp.float32
BF16 = jnp.bfloat16
MASKED = -3.3e38
ROWS = 8 * LANES
MESH = pl.DeviceIdType.MESH


def placing():
    kv = np.zeros((384, 256), np.float32)
    low = np.zeros((384, 256), np.float32)
    high = np.zeros((384, 256), np.float32)
    for group in range(2):
        for head in range(4):
            for dim in range(HEAD_DIM):
                source = group * 192 + head * 48 + dim
                lane = group * 128 + head * 16 + dim
                low[source, lane] = 1
                high[source, lane + 64] = 1
                kv[source + 16, lane] = 1
                kv[source + 32, lane + 64] = 1
    return np.concatenate([kv, low, high], axis=1)


def lane_of(shape):
    return lax.broadcasted_iota(jnp.int32, shape, len(shape) - 1)


def normalise(values, gain):
    centred = values - jnp.mean(values, axis=-1, keepdims=True)
    spread = jnp.mean(centred * centred, axis=-1, keepdims=True)
    return centred * lax.rsqrt(spread + 1e-05) * gain


def swap_ids():
    seq, head = lax.axis_index("seq"), lax.axis_index("head")
    column = seq // 8
    return column, seq - column * 8, head


def iotas(rows):
    shape = (rows, LANES)
    return lax.broadcasted_iota(jnp.int32, shape, 0), lax.broadcasted_iota(jnp.int32, shape, 1)


def value_picker():
    row, lane = iotas(LANES)
    return ((row % 32 < 16) & (lane == 64 + row // 32 * 16 + row % 32)).astype(F32).astype(BF16)


def keyed_rows(block, count):
    row, lane = iotas(TOK)
    zero = jnp.zeros((TOK, LANES), BF16)
    valid = row < count
    flag = jnp.where(valid, zero, jnp.where(lane < 66, jnp.full_like(zero, MASKED), zero))
    keyed = jnp.where((lane < 64) & valid, block, zero)
    return keyed, jnp.where(lane < 64, keyed, flag)


def norms(values):
    row, lane = iotas(LANES)
    sum_of = ((lane == row // 16) & (lane < 4)).astype(F32).astype(BF16)
    size = jnp.minimum(jnp.abs(values), jnp.full_like(values, 1e15))
    size = jnp.where(lax.broadcasted_iota(jnp.int32, values.shape, 1) < 64, size, jnp.zeros_like(size))
    return jnp.max(jnp.dot(size * size, sum_of, preferred_element_type=F32), axis=0, keepdims=True)


def turn_values(vals, turned, at, size):
    ones_row = lax.broadcasted_iota(jnp.int32, (LANES, size), 0) % 32 >= 16
    picked = lax.dot_general(value_picker(), vals, (((1,), (1,)), ((), ())), preferred_element_type=F32)
    turned[:, at] = jnp.where(ones_row, 1.0, picked).astype(BF16)


def half_of(packed, half):
    return packed if half == 0 else pltpu.roll(packed.astype(F32), 64, 1).astype(BF16)


def spread_heads(packed, lhs):
    _, lane = iotas(LANES)
    flags = jnp.where((lane >= 64) & (lane < 66), jnp.ones_like(packed), jnp.zeros_like(packed))
    for half in range(2):
        q = half_of(packed, half)
        for head in range(4):
            mine = (lane >= 16 * head) & (lane < 16 * head + 16)
            lhs[pl.ds((head * 2 + half) * LANES, LANES), :] = jnp.where(mine, q, flags)


def scores_of(keys, lhs):
    return lax.dot_general(keys, lhs[...], (((1,), (1,)), ((), ())), preferred_element_type=F32)


def head_columns(values, head):
    return values[:, TOK * head:TOK * head + TOK]


def attend_kernel(
    routes_hbm, local_hbm, counts_hbm, q_hbm, kv_ref, own_hbm, own_top_hbm, own_size_hbm, own_query_hbm, out_ref,
    routes_ref, local_ref, counts_ref, q_ref, own_ref, own_top_ref, own_size_ref, own_query_ref,
    raw, keys, vals, turned, lhs, acc, top, done, sems, small_sems, out_sems,
):
    column, _, head_index = swap_ids()
    seq = column * 8 + head_index
    core = lax.rem(head_index, 2)
    loads = [
        pltpu.make_async_copy(source, target, small_sems.at[index])
        for index, (source, target) in enumerate((
            (routes_hbm, routes_ref), (local_hbm, local_ref), (counts_hbm, counts_ref),
            (q_hbm, q_ref), (own_hbm, own_ref), (own_top_hbm, own_top_ref),
            (own_size_hbm, own_size_ref), (own_query_hbm, own_query_ref),
        ))
    ]
    for load in loads:
        load.start()
    for load in loads[:3]:
        load.wait()

    def source(patch, which):
        row = seq * NPL * CB + patch * CB + which
        route = routes_ref[0, row]
        offset = jnp.where(route < REACH, route - REACH, route - REACH + 1)
        local = local_ref[0, row]
        owner = lax.rem(seq + offset + 32, 32)
        return (offset + REACH + core) * NPL + local, owner * GROUPS + local * 4

    for patch in range(NPL):
        for which in range(CB):
            slot, _ = source(patch, which)
            pltpu.make_async_copy(kv_ref.at[slot], raw.at[patch * CB + which], sems.at[patch * CB + which]).start()
    for load in loads[3:]:
        load.wait()

    _, lane_kv = iotas(TOK)
    zero = jnp.zeros((TOK, LANES), BF16)

    def patch_body(patch, _):
        for which in range(CB):
            pltpu.make_async_copy(kv_ref.at[0], raw.at[patch * CB + which], sems.at[patch * CB + which]).wait()

        first = jnp.int32(0)
        key_top = jnp.zeros((1, LANES), F32)
        val_top = jnp.zeros((1, LANES), F32)
        for which in range(CB):
            _, shard = source(patch, which)
            for part in range(4):
                count = counts_ref[shard + part]
                block = raw[patch * CB + which, TOK * part:TOK * part + TOK, :]
                keyed, marked = keyed_rows(block, count)
                at = pl.ds(pl.multiple_of(first, 16), TOK)
                keys[at, :] = marked
                vals[at, :] = block
                key_top = jnp.maximum(key_top, norms(keyed))
                size = jnp.max(jnp.where(lane_kv < 64, zero, jnp.abs(block)).astype(F32), axis=0, keepdims=True)
                val_top = jnp.maximum(val_top, size)
                first = first + (count + 15) // 16 * 16
        tail = pl.ds(pl.multiple_of(first, 16), TOK)
        keys[tail, :] = keyed_rows(zero, 0)[1]
        vals[tail, :] = zero
        pieces = (first + TOK - 1) // TOK
        chunks = pieces // 2
        odd = pieces % 2 == 1

        def turn(piece, _):
            at = pl.ds(pl.multiple_of(piece * TOK, TOK), TOK)
            turn_values(vals[at, :], turned, at, TOK)
            return 0

        lax.fori_loop(0, pieces, turn, 0)

        query_top, own_size = own_query_ref[patch * 4], own_size_ref[patch * 4]
        for part in range(1, 4):
            query_top = jnp.maximum(query_top, own_query_ref[patch * 4 + part])
            own_size = jnp.maximum(own_size, own_size_ref[patch * 4 + part])
        sizes = jnp.maximum(query_top * key_top * (1.0 / 3000.0), val_top * 1e-9)
        fits = jnp.maximum(jnp.max(sizes), jnp.max(own_size)) < 1.0

        def shards_body(couple, _):
            shards = [patch * 4 + couple * 2 + side for side in range(2)]
            for side in range(2):
                spread_heads(q_ref[shards[side]], lhs.at[pl.ds(side * ROWS, ROWS)])

            def over_chunks(body):
                def chunk_body(chunk, _):
                    body(pl.ds(pl.multiple_of(chunk * CHUNK, CHUNK), CHUNK))
                    return 0

                lax.fori_loop(0, chunks, chunk_body, 0)

                @pl.when(odd)
                def _():
                    body(pl.ds(pl.multiple_of(chunks * CHUNK, CHUNK), TOK))

            def begin(side, scale):
                for head in range(4):
                    rows = slice(32 * head, 32 * head + 32)
                    acc[side, rows] = own_ref[shards[side], rows] * head_columns(scale, head)

            def gather(at, weights):
                for side in range(2):
                    for head in range(4):
                        rows = slice(32 * head, 32 * head + 32)
                        acc[side, rows] += jnp.dot(
                            turned[rows, at], head_columns(weights, side * 4 + head), preferred_element_type=F32
                        )

            @pl.when(fits)
            def _():
                for side in range(2):
                    begin(side, jnp.exp2(own_top_ref[shards[side]]))
                over_chunks(lambda at: gather(at, jnp.exp2(scores_of(keys[at, :], lhs)).astype(BF16)))

            @pl.when(jnp.logical_not(fits))
            def _():
                for side in range(2):
                    top[:, pl.ds(side * ROWS, ROWS)] = own_top_ref[shards[side]]

                def raise_top(at):
                    top[...] = jnp.maximum(top[...], jnp.max(scores_of(keys[at, :], lhs), axis=0, keepdims=True))

                over_chunks(raise_top)
                for side in range(2):
                    begin(side, jnp.exp2(own_top_ref[shards[side]] - top[:, pl.ds(side * ROWS, ROWS)]))
                over_chunks(lambda at: gather(at, jnp.exp2(scores_of(keys[at, :], lhs) - top[...]).astype(BF16)))

            for side in range(2):
                joined = [
                    acc[side, 32 * head:32 * head + 16] / acc[side, 32 * head + 16:32 * head + 32] for head in range(4)
                ]
                shard = shards[side]
                done[shard] = jnp.concatenate(joined, axis=0).astype(BF16)
                pltpu.make_async_copy(done.at[shard], out_ref.at[shard], out_sems.at[shard]).start()
            return 0

        lax.fori_loop(0, 2, shards_body, 0)
        return 0

    lax.fori_loop(0, NPL, patch_body, 0)
    for shard in range(GROUPS):
        pltpu.make_async_copy(done.at[shard], out_ref.at[shard], out_sems.at[shard]).wait()


def attend(routes, local, counts, q, kv, own, own_top, own_size, own_query):
    hbm = pl.BlockSpec(memory_space=pltpu.HBM)
    most = CB * PATCH + TOK
    return pl.pallas_call(
        attend_kernel,
        out_shape=jax.ShapeDtypeStruct((GROUPS, 64, TOK), BF16),
        in_specs=[hbm] * 9,
        out_specs=hbm,
        scratch_shapes=[
            pltpu.SMEM((1, LANES), jnp.int32),
            pltpu.SMEM((1, LANES), jnp.int32),
            pltpu.SMEM((256,), jnp.int32),
            pltpu.VMEM((GROUPS, LANES, LANES), BF16),
            pltpu.VMEM((GROUPS, LANES, TOK), F32),
            pltpu.VMEM((GROUPS, 1, ROWS), F32),
            pltpu.VMEM((GROUPS, 1, ROWS), F32),
            pltpu.VMEM((GROUPS, 1, LANES), F32),
            pltpu.VMEM((NPL * CB, PATCH, LANES), BF16),
            pltpu.VMEM((most, LANES), BF16),
            pltpu.VMEM((most, LANES), BF16),
            pltpu.VMEM((LANES, most), BF16),
            pltpu.VMEM((2 * ROWS, LANES), BF16),
            pltpu.VMEM((2, LANES, TOK), F32),
            pltpu.VMEM((1, 2 * ROWS), F32),
            pltpu.VMEM((GROUPS, 64, TOK), BF16),
            pltpu.SemaphoreType.DMA((NPL * CB,)),
            pltpu.SemaphoreType.DMA((8,)),
            pltpu.SemaphoreType.DMA((8,)),
        ],
        compiler_params=pltpu.CompilerParams(vmem_limit_bytes=60 << 20),
        cost_estimate=pl.CostEstimate(flops=20_000_000_000, bytes_accessed=6_000_000, transcendentals=17_000_000),
        name="attend",
    )(routes, local, counts, q, kv, own, own_top, own_size, own_query)


def each(body):
    def step(index, _):
        body(index)
        return 0

    lax.fori_loop(0, 8, step, 0)


def finish_kernel(
    points_ref, packed_ref, w_out_ref, gain_ref, w0_ref, w1_ref, w2_ref, w3_ref, out_ref,
    points, w_out, gain, slabs, back, send, recv, local_sem, load_sem, weight_sem, pair_send, pair_recv,
):
    column, plane, head = swap_ids()
    diagonal = plane == head
    across = jnp.logical_not(diagonal)
    barrier = pltpu.get_barrier_semaphore()

    def greet(group):
        @pl.when(across | (group != plane))
        def _():
            pl.semaphore_signal(barrier, inc=1, device_id=(column * 8 + group, plane), device_id_type=MESH)

    each(greet)
    pair = (column * 8 + plane, head + 1 - 2 * lax.rem(head, 2))
    pl.semaphore_signal(barrier, inc=1, device_id=pair, device_id_type=MESH)
    loads = [
        pltpu.make_async_copy(points_ref, points, load_sem.at[0]),
        pltpu.make_async_copy(w_out_ref, w_out, load_sem.at[1]),
        pltpu.make_async_copy(gain_ref, gain, load_sem.at[2]),
    ]
    for load in loads:
        load.start()

    shards = (w0_ref, w1_ref, w2_ref, w3_ref)
    own = [pltpu.make_async_copy(shard, slabs.at[part], weight_sem.at[part]) for part, shard in enumerate(shards)]
    lent = [
        pltpu.make_async_remote_copy(
            src_ref=shard, dst_ref=slabs.at[4 + part], send_sem=pair_send.at[part], recv_sem=pair_recv.at[part],
            device_id=pair, device_id_type=MESH,
        )
        for part, shard in enumerate(shards)
    ]
    for load in own:
        load.start()

    @pl.when(diagonal)
    def _():
        pl.semaphore_wait(barrier, 8)

    @pl.when(across)
    def _():
        pl.semaphore_wait(barrier, 9)

    def copy(shard, group):
        return pltpu.make_async_remote_copy(
            src_ref=packed_ref.at[shard], dst_ref=back.at[group],
            send_sem=send.at[shard], recv_sem=recv.at[group],
            device_id=(column * 8 + head, shard), device_id_type=MESH,
        )

    at_home = pltpu.make_async_copy(packed_ref.at[head], back.at[plane], local_sem.at[0])

    def start(shard):
        @pl.when(across | (shard != head))
        def _():
            copy(shard, plane).start()

    each(start)
    for load in lent:
        load.start()

    @pl.when(diagonal)
    def _():
        at_home.start()
        at_home.wait()

    for load in loads:
        load.wait()

    def wait(index):
        @pl.when(across | (index != plane))
        def _():
            copy(0, index).wait_recv()

    each(wait)

    attended = back[...].reshape(D, TOK)
    updated = points[...].astype(F32) + lax.dot_general(
        attended, w_out[...], (((0,), (0,)), ((), ())), preferred_element_type=F32
    )
    updated = updated.astype(BF16).astype(F32)
    normed = normalise(updated, gain[...]).astype(BF16)
    low, high = updated[:, :256], updated[:, 256:]
    for part in range(GROUPS):
        if part < 4:
            own[part].wait()
        else:
            lent[part - 4].wait_recv()
        hidden = jnp.dot(normed, slabs[part, :D], preferred_element_type=F32)
        hidden = (hidden * (0.5 * (1.0 + lax.erf(hidden * (2.0 ** -0.5))))).astype(BF16)
        low = low + jnp.dot(hidden, slabs[part, D:D + 256], preferred_element_type=F32)
        high = high + jnp.dot(hidden, slabs[part, D + 256:], preferred_element_type=F32)
    out_ref[:, :256] = low.astype(BF16)
    out_ref[:, 256:] = high.astype(BF16)

    def sent(index):
        @pl.when(across | (index != head))
        def _():
            copy(index, plane).wait_send()

    each(sent)
    for load in lent:
        load.wait_send()


def finish(points, packed, w_out, gain, weights):
    hbm = pl.BlockSpec(memory_space=pltpu.HBM)
    return pl.pallas_call(
        finish_kernel,
        out_shape=jax.ShapeDtypeStruct((TOK, D), BF16),
        in_specs=[hbm] * 8,
        out_specs=pl.BlockSpec(memory_space=pltpu.VMEM),
        scratch_shapes=[
            pltpu.VMEM((TOK, D), BF16),
            pltpu.VMEM((D, D), BF16),
            pltpu.VMEM((1, D), F32),
            pltpu.VMEM((GROUPS, 2 * D, 256), BF16),
            pltpu.VMEM((GROUPS, 64, TOK), BF16),
            pltpu.SemaphoreType.DMA((8,)),
            pltpu.SemaphoreType.DMA((8,)),
            pltpu.SemaphoreType.DMA((1,)),
            pltpu.SemaphoreType.DMA((3,)),
            pltpu.SemaphoreType.DMA((4,)),
            pltpu.SemaphoreType.DMA((4,)),
            pltpu.SemaphoreType.DMA((4,)),
        ],
        compiler_params=pltpu.CompilerParams(
            collective_id=1, has_side_effects=True, vmem_limit_bytes=40 << 20
        ),
        name="finish",
    )(points, packed, w_out, gain.reshape(1, D), *weights)


def exchange_kernel(
    points_ref, gain_ref, w_ref, scale_ref, place_ref, counts_ref, route_ref, local_ref, w1_ref, w2_ref,
    kv_out, q_out, route_out, local_out, own_out, own_top_out, own_size_out, own_query_out, weights_out,
    kv_ref, q_ref, raw, queries, keys, turned, lhs, scores, own, own_top, own_size, own_query,
    all_send, all_recv, ring_send, ring_recv, pair_send, pair_recv, route_sem, local_sem, load_sem, own_sem,
):
    column, plane, head = swap_ids()
    core = lax.rem(head, 2)
    spot = column * 4 + head // 2
    after, before = lax.rem(spot + 1, 16), lax.rem(spot + 15, 16)
    right = ((after // 4) * 8 + plane, lax.rem(after, 4) * 2 + core)
    left = ((before // 4) * 8 + plane, lax.rem(before, 4) * 2 + core)
    pair = (column * 8 + plane, head + 1 - 2 * core)
    partner = (column * 8 + head, plane)
    diagonal = plane == head
    across = jnp.logical_not(diagonal)

    barrier = pltpu.get_barrier_semaphore()

    def greet(index, _):
        @pl.when(across | (index != head))
        def _():
            pl.semaphore_signal(barrier, inc=1, device_id=(column * 8 + head, index), device_id_type=MESH)
        return 0

    lax.fori_loop(0, 8, greet, 0)
    for other in (right, left, pair):
        pl.semaphore_signal(barrier, inc=1, device_id=other, device_id_type=MESH)

    def enter():
        @pl.when(diagonal)
        def _():
            pl.semaphore_wait(barrier, 10)

        @pl.when(across)
        def _():
            pl.semaphore_wait(barrier, 11)

    def rows(half):
        return pl.ds(half * LANES, LANES)

    def spread(group, half, shard):
        return pltpu.make_async_remote_copy(
            src_ref=kv_ref.at[group, rows(half)],
            dst_ref=kv_out.at[4 + lax.rem(plane, 2), shard, rows(half)],
            send_sem=all_send.at[half, group],
            recv_sem=all_recv.at[half, shard],
            device_id=(column * 8 + group, plane),
            device_id_type=MESH,
        )

    def landed(half, shard):
        return pltpu.make_async_remote_copy(
            src_ref=kv_ref.at[0, rows(half)],
            dst_ref=kv_out.at[4 + core, shard, rows(half)],
            send_sem=all_send.at[half, 0],
            recv_sem=all_recv.at[half, shard],
            device_id=pair,
            device_id_type=MESH,
        )

    def spread_q(group, shard):
        return pltpu.make_async_remote_copy(
            src_ref=q_ref.at[group],
            dst_ref=q_out.at[shard],
            send_sem=all_send.at[2, group],
            recv_sem=all_recv.at[2, shard],
            device_id=(column * 8 + group, plane),
            device_id_type=MESH,
        )

    def at_home(half):
        return pltpu.make_async_copy(
            kv_ref.at[plane, rows(half)], kv_out.at[4 + core, head, rows(half)], local_sem.at[half]
        )

    q_at_home = pltpu.make_async_copy(q_ref.at[plane], q_out.at[head], local_sem.at[2])
    routes_at_home = [
        pltpu.make_async_copy(route_ref, route_out, local_sem.at[3]),
        pltpu.make_async_copy(local_ref, local_out, local_sem.at[4]),
    ]
    routes_sent = [
        pltpu.make_async_remote_copy(
            src_ref=source, dst_ref=target, send_sem=route_sem.at[0, index], recv_sem=route_sem.at[1, index],
            device_id=partner, device_id_type=MESH,
        )
        for index, (source, target) in enumerate(((route_ref, route_out), (local_ref, local_out)))
    ]

    def start(group):
        @pl.when(across | (group != plane))
        def _():
            spread(group, 0, head).start()
            spread(group, 1, head).start()

    def start_q(group):
        @pl.when(across | (group != plane))
        def _():
            spread_q(group, head).start()

    joins = [
        pltpu.make_async_copy(source, weights_out.at[rows_at], load_sem.at[2 + index])
        for index, (source, rows_at) in enumerate((
            (w1_ref, pl.ds(0, D)), (w2_ref.at[:, pl.ds(0, 256)], pl.ds(D, 256)), (w2_ref.at[:, pl.ds(256, 256)], pl.ds(D + 256, 256)),
        ))
    ]
    for join in joins:
        join.start()

    normed = normalise(points_ref[...].astype(F32), gain_ref[...]).astype(BF16)
    for couple in range(GROUPS // 2):
        columns = slice(384 * couple, 384 * couple + 384)
        projected = jnp.dot(normed, w_ref[:, columns], preferred_element_type=F32)
        projected = (projected * scale_ref[:, columns]).astype(BF16)
        kv = jnp.dot(projected, place_ref[:, :256], preferred_element_type=F32).astype(BF16)
        q = jnp.dot(projected[:128], place_ref[:, 256:512], preferred_element_type=F32)
        q = (q + jnp.dot(projected[128:], place_ref[:, 512:], preferred_element_type=F32)).astype(BF16)
        for side in range(2):
            kv_ref[2 * couple + side] = kv[:, 128 * side:128 * side + 128]
            q_ref[2 * couple + side] = q[:, 128 * side:128 * side + 128]
        if couple == 0:
            enter()
        start(2 * couple)
        start(2 * couple + 1)
    each(start_q)

    @pl.when(diagonal)
    def _():
        at_home(0).start()
        at_home(1).start()
        q_at_home.start()
        for copy in routes_at_home:
            copy.start()

    @pl.when(across)
    def _():
        for copy in routes_sent:
            copy.start()


    def moved(source, target, half, send, recv, to):
        return pltpu.make_async_remote_copy(
            src_ref=kv_out.at[source, :, rows(half)], dst_ref=kv_out.at[target, :, rows(half)],
            send_sem=send, recv_sem=recv, device_id=to, device_id_type=MESH,
        )

    def hop(way, step, half):
        if way == 0:
            source, to = 4 - 2 * step + core, right
            target = 2 - 2 * step + core
        else:
            source, to = 4 + 2 * step + core, left
            target = 6 + 2 * step + core
        return moved(source, target, half, ring_send.at[way, step, half], ring_recv.at[way, step, half], to)

    def shared(place, half):
        return moved(2 * place + core, 2 * place + core, half, pair_send.at[place, half], pair_recv.at[place, half], pair)

    def taken(place, half):
        return moved(2 * place + 1 - core, 2 * place + 1 - core, half, pair_send.at[place, half], pair_recv.at[place, half], pair)

    for half in range(2):
        def wait(shard):
            @pl.when(across | (shard != head))
            def _():
                landed(half, shard).wait_recv()

        each(wait)

        @pl.when(diagonal)
        def _():
            at_home(half).wait()

        hop(0, 0, half).start()
        hop(1, 0, half).start()
        shared(2, half).start()
    def wait_q(shard):
        @pl.when(across | (shard != head))
        def _():
            spread_q(0, shard).wait_recv()

    each(wait_q)

    @pl.when(diagonal)
    def _():
        q_at_home.wait()

    loads = [
        pltpu.make_async_copy(kv_out.at[4 + core], raw, load_sem.at[0]),
        pltpu.make_async_copy(q_out, queries, load_sem.at[1]),
    ]
    for load in loads:
        load.start()
    for load in loads:
        load.wait()

    def own_keys(shard):
        at = pl.ds(pl.multiple_of(shard * TOK, TOK), TOK)
        keys[at, :] = keyed_rows(raw[shard], counts_ref[(column * 8 + head) * GROUPS + shard])[1]
        turn_values(raw[shard], turned, at, TOK)

    each(own_keys)

    def own_saved(shard):
        return (
            pltpu.make_async_copy(own.at[shard], own_out.at[shard], own_sem.at[0, shard]),
            pltpu.make_async_copy(own_top.at[shard], own_top_out.at[shard], own_sem.at[1, shard]),
            pltpu.make_async_copy(own_size.at[shard], own_size_out.at[shard], own_sem.at[2, shard]),
            pltpu.make_async_copy(own_query.at[shard], own_query_out.at[shard], own_sem.at[3, shard]),
        )

    def own_run(begin, end):
        def own_shard(shard, _):
            patch = shard // 4
            packed = queries[shard]
            spread_heads(packed, lhs)
            most = None
            spots = [pl.ds(pl.multiple_of(patch * PATCH + piece * CHUNK, CHUNK), CHUNK) for piece in range(2)]
            for piece in range(2):
                found = scores_of(keys[spots[piece], :], lhs)
                scores[piece] = found
                found = jnp.max(found, axis=0, keepdims=True)
                most = found if piece == 0 else jnp.maximum(most, found)
            own_top[shard] = most
            total = [None] * 4
            for piece in range(2):
                weights = jnp.exp2(scores[piece] - most).astype(BF16)
                for index in range(4):
                    rows_of = slice(32 * index, 32 * index + 32)
                    term = jnp.dot(
                        turned[rows_of, spots[piece]], head_columns(weights, index), preferred_element_type=F32
                    )
                    total[index] = term if piece == 0 else total[index] + term
            for index in range(4):
                own[shard, 32 * index:32 * index + 32] = total[index]
                columns = slice(TOK * index, TOK * index + TOK)
                size = jnp.max(jnp.abs(total[index]), axis=0, keepdims=True) * 1e-12
                own_size[shard, :, columns] = jnp.maximum(size, jnp.abs(most[:, columns]) * (1.0 / 55.0))
            own_query[shard] = jnp.maximum(norms(half_of(packed, 0)), norms(half_of(packed, 1)))
            for save in own_saved(shard):
                save.start()
            return 0

        lax.fori_loop(begin, end, own_shard, 0)

    for half in range(2):
        hop(0, 0, half).wait_recv()
        hop(0, 1, half).start()
        hop(1, 0, half).wait_recv()
        hop(1, 1, half).start()
        shared(1, half).start()
        shared(3, half).start()
        own_run(4 * half, 4 * half + 4)
    for half in range(2):
        hop(0, 1, half).wait_recv()
        shared(0, half).start()
        hop(1, 1, half).wait_recv()
        shared(4, half).start()

    def sent(group):
        @pl.when(across | (group != plane))
        def _():
            spread(group, 0, head).wait_send()
            spread(group, 1, head).wait_send()
            spread_q(group, head).wait_send()

    each(sent)

    @pl.when(diagonal)
    def _():
        for copy in routes_at_home:
            copy.wait()

    @pl.when(across)
    def _():
        for copy in routes_sent:
            copy.wait()


    for half in range(2):
        for way in range(2):
            for step in range(2):
                hop(way, step, half).wait_send()
        for place in range(5):
            shared(place, half).wait_send()
            taken(place, half).wait_recv()
    for join in joins:
        join.wait()

    def saved(shard):
        for save in own_saved(shard):
            save.wait()

    each(saved)


def exchange(points, gain, w_qkv, counts, routes, local, w1, w2):
    scale = np.ones((1, 1536), np.float32)
    scale[0, np.arange(1536) % 48 < 16] = HEAD_DIM ** -0.5 * math.log2(math.e)
    vmem = pl.BlockSpec(memory_space=pltpu.VMEM)
    anywhere = pl.BlockSpec(memory_space=pltpu.HBM)
    return pl.pallas_call(
        exchange_kernel,
        out_shape=(
            jax.ShapeDtypeStruct((10, GROUPS, TOK, LANES), BF16),
            jax.ShapeDtypeStruct((GROUPS, LANES, LANES), BF16),
            jax.ShapeDtypeStruct((1, LANES), jnp.int32),
            jax.ShapeDtypeStruct((1, LANES), jnp.int32),
            jax.ShapeDtypeStruct((GROUPS, LANES, TOK), F32),
            jax.ShapeDtypeStruct((GROUPS, 1, ROWS), F32),
            jax.ShapeDtypeStruct((GROUPS, 1, ROWS), F32),
            jax.ShapeDtypeStruct((GROUPS, 1, LANES), F32),
            jax.ShapeDtypeStruct((2 * D, 256), BF16),
        ),
        in_specs=[vmem] * 5 + [pl.BlockSpec(memory_space=pltpu.SMEM)] + [anywhere] * 4,
        out_specs=(anywhere,) * 9,
        scratch_shapes=[
            pltpu.VMEM((GROUPS, TOK, LANES), BF16),
            pltpu.VMEM((GROUPS, LANES, LANES), BF16),
            pltpu.VMEM((GROUPS, TOK, LANES), BF16),
            pltpu.VMEM((GROUPS, LANES, LANES), BF16),
            pltpu.VMEM((NPL * PATCH, LANES), BF16),
            pltpu.VMEM((LANES, NPL * PATCH), BF16),
            pltpu.VMEM((ROWS, LANES), BF16),
            pltpu.VMEM((2, CHUNK, ROWS), F32),
            pltpu.VMEM((GROUPS, LANES, TOK), F32),
            pltpu.VMEM((GROUPS, 1, ROWS), F32),
            pltpu.VMEM((GROUPS, 1, ROWS), F32),
            pltpu.VMEM((GROUPS, 1, LANES), F32),
            pltpu.SemaphoreType.DMA((3, 8)),
            pltpu.SemaphoreType.DMA((3, 8)),
            pltpu.SemaphoreType.DMA((2, 2, 2)),
            pltpu.SemaphoreType.DMA((2, 2, 2)),
            pltpu.SemaphoreType.DMA((5, 2)),
            pltpu.SemaphoreType.DMA((5, 2)),
            pltpu.SemaphoreType.DMA((2, 2)),
            pltpu.SemaphoreType.DMA((5,)),
            pltpu.SemaphoreType.DMA((5,)),
            pltpu.SemaphoreType.DMA((4, 8)),
        ],
        compiler_params=pltpu.CompilerParams(collective_id=0, has_side_effects=True, vmem_limit_bytes=60 << 20),
        name="exchange",
    )(
        points, gain.reshape(1, D), w_qkv, jnp.asarray(scale), jnp.asarray(placing(), BF16),
        counts, routes, local, w1, w2,
    )


def per_device(
    points, gain_attn, w_qkv, w_out, gain_mlp, w_fc1, w_fc2, contact_route, contact_patch, counts
):
    slots, q, routes, local, sums, tops, sizes, tallest, joined = exchange(
        points, gain_attn, w_qkv, counts, contact_route.reshape(1, -1), contact_patch, w_fc1, w_fc2
    )
    weights = [joined]
    for step in range(1, 4):
        pairs = [(head, (head + 2 * step) % GROUPS) for head in range(GROUPS)]
        weights.append(lax.ppermute(joined, "head", pairs))
    packed = attend(routes, local, counts, q, slots.reshape(20, PATCH, LANES), sums, tops, sizes, tallest)
    return finish(points, packed, w_out, gain_mlp, weights)


def solution(mesh):
    return jax.shard_map(
        per_device,
        mesh=mesh,
        in_specs=(
            P(("seq", "head"), None), P(), P(), P(), P(), P(None, "head"), P("head", None),
            P("head", None, None), P("head", None), P(),
        ),
        out_specs=P(("seq", "head"), None),
        check_vma=False,
    )
```

```python
import functools
import math

import jax
import jax.numpy as jnp
import numpy as np
from jax import lax
from jax.experimental import pallas as pl
from jax.experimental.pallas import tpu as pltpu
from jax.sharding import PartitionSpec as P

D = 512
HEADS = 32
HEAD_DIM = 16
PATCH = 1024
CB = 2
NPL = 2
REACH = 4
TOK = 256
GROUPS = 8
LANES = 128
CHUNK = 512
F32 = jnp.float32
BF16 = jnp.bfloat16
MASKED = -3.3e38
ROWS = 8 * LANES
MESH = pl.DeviceIdType.MESH


def placing():
    kv = np.zeros((384, 256), np.float32)
    low = np.zeros((384, 256), np.float32)
    high = np.zeros((384, 256), np.float32)
    for group in range(2):
        for head in range(4):
            for dim in range(HEAD_DIM):
                source = group * 192 + head * 48 + dim
                lane = group * 128 + head * 16 + dim
                low[source, lane] = 1
                high[source, lane + 64] = 1
                kv[source + 16, lane] = 1
                kv[source + 32, lane + 64] = 1
    return np.concatenate([kv, low, high], axis=1)


def lane_of(shape):
    return lax.broadcasted_iota(jnp.int32, shape, len(shape) - 1)


def normalise(values, gain):
    centred = values - jnp.mean(values, axis=-1, keepdims=True)
    spread = jnp.mean(centred * centred, axis=-1, keepdims=True)
    return centred * lax.rsqrt(spread + 1e-05) * gain


def swap_ids():
    seq, head = lax.axis_index("seq"), lax.axis_index("head")
    column = seq // 8
    return column, seq - column * 8, head


def iotas(rows):
    shape = (rows, LANES)
    return lax.broadcasted_iota(jnp.int32, shape, 0), lax.broadcasted_iota(jnp.int32, shape, 1)


def value_picker():
    row, lane = iotas(LANES)
    return ((row % 32 < 16) & (lane == 64 + row // 32 * 16 + row % 32)).astype(F32).astype(BF16)


def keyed_rows(block, count):
    row, lane = iotas(TOK)
    zero = jnp.zeros((TOK, LANES), BF16)
    valid = row < count
    flag = jnp.where(valid, zero, jnp.where(lane < 66, jnp.full_like(zero, MASKED), zero))
    keyed = jnp.where((lane < 64) & valid, block, zero)
    return keyed, jnp.where(lane < 64, keyed, flag)


def norms(values):
    row, lane = iotas(LANES)
    sum_of = ((lane == row // 16) & (lane < 4)).astype(F32).astype(BF16)
    size = jnp.minimum(jnp.abs(values), jnp.full_like(values, 1e15))
    size = jnp.where(lax.broadcasted_iota(jnp.int32, values.shape, 1) < 64, size, jnp.zeros_like(size))
    return jnp.max(jnp.dot(size * size, sum_of, preferred_element_type=F32), axis=0, keepdims=True)


def turn_values(vals, turned, at, size):
    ones_row = lax.broadcasted_iota(jnp.int32, (LANES, size), 0) % 32 >= 16
    picked = lax.dot_general(value_picker(), vals, (((1,), (1,)), ((), ())), preferred_element_type=F32)
    turned[:, at] = jnp.where(ones_row, 1.0, picked).astype(BF16)


def half_of(packed, half):
    return packed if half == 0 else pltpu.roll(packed.astype(F32), 64, 1).astype(BF16)


def spread_heads(packed, lhs):
    _, lane = iotas(LANES)
    flags = jnp.where((lane >= 64) & (lane < 66), jnp.ones_like(packed), jnp.zeros_like(packed))
    for half in range(2):
        q = half_of(packed, half)
        for head in range(4):
            mine = (lane >= 16 * head) & (lane < 16 * head + 16)
            lhs[pl.ds((head * 2 + half) * LANES, LANES), :] = jnp.where(mine, q, flags)


def scores_of(keys, lhs):
    return lax.dot_general(keys, lhs[...], (((1,), (1,)), ((), ())), preferred_element_type=F32)


def head_columns(values, head):
    return values[:, TOK * head:TOK * head + TOK]


def attend_kernel(
    routes_hbm, local_hbm, counts_hbm, q_hbm, kv_ref, own_hbm, own_top_hbm, own_size_hbm, own_query_hbm, out_ref,
    routes_ref, local_ref, counts_ref, q_ref, own_ref, own_top_ref, own_size_ref, own_query_ref,
    raw, keys, vals, turned, lhs, acc, top, done, sems, small_sems, out_sems,
):
    column, _, head_index = swap_ids()
    seq = column * 8 + head_index
    core = lax.rem(head_index, 2)
    loads = [
        pltpu.make_async_copy(source, target, small_sems.at[index])
        for index, (source, target) in enumerate((
            (routes_hbm, routes_ref), (local_hbm, local_ref), (counts_hbm, counts_ref),
            (q_hbm, q_ref), (own_hbm, own_ref), (own_top_hbm, own_top_ref),
            (own_size_hbm, own_size_ref), (own_query_hbm, own_query_ref),
        ))
    ]
    for load in loads:
        load.start()
    for load in loads[:3]:
        load.wait()

    def source(patch, which):
        row = seq * NPL * CB + patch * CB + which
        route = routes_ref[0, row]
        offset = jnp.where(route < REACH, route - REACH, route - REACH + 1)
        local = local_ref[0, row]
        owner = lax.rem(seq + offset + 32, 32)
        return (offset + REACH + core) * NPL + local, owner * GROUPS + local * 4

    for patch in range(NPL):
        for which in range(CB):
            slot, _ = source(patch, which)
            pltpu.make_async_copy(kv_ref.at[slot], raw.at[patch * CB + which], sems.at[patch * CB + which]).start()
    for load in loads[3:]:
        load.wait()

    _, lane_kv = iotas(TOK)
    zero = jnp.zeros((TOK, LANES), BF16)

    def patch_body(patch, _):
        for which in range(CB):
            pltpu.make_async_copy(kv_ref.at[0], raw.at[patch * CB + which], sems.at[patch * CB + which]).wait()

        first = jnp.int32(0)
        key_top = jnp.zeros((1, LANES), F32)
        val_top = jnp.zeros((1, LANES), F32)
        for which in range(CB):
            _, shard = source(patch, which)
            for part in range(4):
                count = counts_ref[shard + part]
                block = raw[patch * CB + which, TOK * part:TOK * part + TOK, :]
                keyed, marked = keyed_rows(block, count)
                at = pl.ds(pl.multiple_of(first, 16), TOK)
                keys[at, :] = marked
                vals[at, :] = block
                key_top = jnp.maximum(key_top, norms(keyed))
                size = jnp.max(jnp.where(lane_kv < 64, zero, jnp.abs(block)).astype(F32), axis=0, keepdims=True)
                val_top = jnp.maximum(val_top, size)
                first = first + (count + 15) // 16 * 16
        tail = pl.ds(pl.multiple_of(first, 16), TOK)
        keys[tail, :] = keyed_rows(zero, 0)[1]
        vals[tail, :] = zero
        pieces = (first + TOK - 1) // TOK
        chunks = pieces // 2
        odd = pieces % 2 == 1

        def turn(piece, _):
            at = pl.ds(pl.multiple_of(piece * TOK, TOK), TOK)
            turn_values(vals[at, :], turned, at, TOK)
            return 0

        lax.fori_loop(0, pieces, turn, 0)

        query_top, own_size = own_query_ref[patch * 4], own_size_ref[patch * 4]
        for part in range(1, 4):
            query_top = jnp.maximum(query_top, own_query_ref[patch * 4 + part])
            own_size = jnp.maximum(own_size, own_size_ref[patch * 4 + part])
        sizes = jnp.maximum(query_top * key_top * (1.0 / 3000.0), val_top * 1e-9)
        fits = jnp.maximum(jnp.max(sizes), jnp.max(own_size)) < 1.0

        def shards_body(couple, _):
            shards = [patch * 4 + couple * 2 + side for side in range(2)]
            for side in range(2):
                spread_heads(q_ref[shards[side]], lhs.at[pl.ds(side * ROWS, ROWS)])

            def over_chunks(body):
                def chunk_body(chunk, _):
                    body(pl.ds(pl.multiple_of(chunk * CHUNK, CHUNK), CHUNK))
                    return 0

                lax.fori_loop(0, chunks, chunk_body, 0)

                @pl.when(odd)
                def _():
                    body(pl.ds(pl.multiple_of(chunks * CHUNK, CHUNK), TOK))

            def begin(side, scale):
                for head in range(4):
                    rows = slice(32 * head, 32 * head + 32)
                    acc[side, rows] = own_ref[shards[side], rows] * head_columns(scale, head)

            def gather(at, weights):
                for side in range(2):
                    for head in range(4):
                        rows = slice(32 * head, 32 * head + 32)
                        acc[side, rows] += jnp.dot(
                            turned[rows, at], head_columns(weights, side * 4 + head), preferred_element_type=F32
                        )

            @pl.when(fits)
            def _():
                for side in range(2):
                    begin(side, jnp.exp2(own_top_ref[shards[side]]))
                over_chunks(lambda at: gather(at, jnp.exp2(scores_of(keys[at, :], lhs)).astype(BF16)))

            @pl.when(jnp.logical_not(fits))
            def _():
                for side in range(2):
                    top[:, pl.ds(side * ROWS, ROWS)] = own_top_ref[shards[side]]

                def raise_top(at):
                    top[...] = jnp.maximum(top[...], jnp.max(scores_of(keys[at, :], lhs), axis=0, keepdims=True))

                over_chunks(raise_top)
                for side in range(2):
                    begin(side, jnp.exp2(own_top_ref[shards[side]] - top[:, pl.ds(side * ROWS, ROWS)]))
                over_chunks(lambda at: gather(at, jnp.exp2(scores_of(keys[at, :], lhs) - top[...]).astype(BF16)))

            for side in range(2):
                joined = [
                    acc[side, 32 * head:32 * head + 16] / acc[side, 32 * head + 16:32 * head + 32] for head in range(4)
                ]
                shard = shards[side]
                done[shard] = jnp.concatenate(joined, axis=0).astype(BF16)
                pltpu.make_async_copy(done.at[shard], out_ref.at[shard], out_sems.at[shard]).start()
            return 0

        lax.fori_loop(0, 2, shards_body, 0)
        return 0

    lax.fori_loop(0, NPL, patch_body, 0)
    for shard in range(GROUPS):
        pltpu.make_async_copy(done.at[shard], out_ref.at[shard], out_sems.at[shard]).wait()


def attend(routes, local, counts, q, kv, own, own_top, own_size, own_query):
    hbm = pl.BlockSpec(memory_space=pltpu.HBM)
    most = CB * PATCH + TOK
    return pl.pallas_call(
        attend_kernel,
        out_shape=jax.ShapeDtypeStruct((GROUPS, 64, TOK), BF16),
        in_specs=[hbm] * 9,
        out_specs=hbm,
        scratch_shapes=[
            pltpu.SMEM((1, LANES), jnp.int32),
            pltpu.SMEM((1, LANES), jnp.int32),
            pltpu.SMEM((256,), jnp.int32),
            pltpu.VMEM((GROUPS, LANES, LANES), BF16),
            pltpu.VMEM((GROUPS, LANES, TOK), F32),
            pltpu.VMEM((GROUPS, 1, ROWS), F32),
            pltpu.VMEM((GROUPS, 1, ROWS), F32),
            pltpu.VMEM((GROUPS, 1, LANES), F32),
            pltpu.VMEM((NPL * CB, PATCH, LANES), BF16),
            pltpu.VMEM((most, LANES), BF16),
            pltpu.VMEM((most, LANES), BF16),
            pltpu.VMEM((LANES, most), BF16),
            pltpu.VMEM((2 * ROWS, LANES), BF16),
            pltpu.VMEM((2, LANES, TOK), F32),
            pltpu.VMEM((1, 2 * ROWS), F32),
            pltpu.VMEM((GROUPS, 64, TOK), BF16),
            pltpu.SemaphoreType.DMA((NPL * CB,)),
            pltpu.SemaphoreType.DMA((8,)),
            pltpu.SemaphoreType.DMA((8,)),
        ],
        compiler_params=pltpu.CompilerParams(vmem_limit_bytes=60 << 20),
        cost_estimate=pl.CostEstimate(flops=20_000_000_000, bytes_accessed=6_000_000, transcendentals=17_000_000),
        name="attend",
    )(routes, local, counts, q, kv, own, own_top, own_size, own_query)


def each(body):
    def step(index, _):
        body(index)
        return 0

    lax.fori_loop(0, 8, step, 0)


def finish_kernel(
    points_ref, packed_ref, w_out_ref, gain_ref, w0_ref, w1_ref, w2_ref, w3_ref, out_ref,
    points, w_out, gain, slabs, mid, back, send, recv, local_sem, load_sem, weight_sem, pair_send, pair_recv,
):
    column, plane, head = swap_ids()
    barrier = pltpu.get_barrier_semaphore()

    def greet(index):
        @pl.when(index != head)
        def _():
            pl.semaphore_signal(barrier, inc=1, device_id=(column * 8 + plane, index), device_id_type=MESH)

        @pl.when(index != plane)
        def _():
            pl.semaphore_signal(barrier, inc=1, device_id=(column * 8 + index, head), device_id_type=MESH)

    each(greet)
    pair = (column * 8 + plane, head + 1 - 2 * lax.rem(head, 2))
    loads = [
        pltpu.make_async_copy(points_ref, points, load_sem.at[0]),
        pltpu.make_async_copy(w_out_ref, w_out, load_sem.at[1]),
        pltpu.make_async_copy(gain_ref, gain, load_sem.at[2]),
    ]
    for load in loads:
        load.start()

    shards = (w0_ref, w1_ref, w2_ref, w3_ref)
    own = [pltpu.make_async_copy(shard, slabs.at[part], weight_sem.at[part]) for part, shard in enumerate(shards)]
    lent = [
        pltpu.make_async_remote_copy(
            src_ref=shard, dst_ref=slabs.at[4 + part], send_sem=pair_send.at[part], recv_sem=pair_recv.at[part],
            device_id=pair, device_id_type=MESH,
        )
        for part, shard in enumerate(shards)
    ]
    for load in own:
        load.start()

    pl.semaphore_wait(barrier, 14)

    def level_leg(shard, slot):
        return pltpu.make_async_remote_copy(
            src_ref=packed_ref.at[shard], dst_ref=mid.at[slot],
            send_sem=send.at[0, shard], recv_sem=recv.at[0, slot],
            device_id=(column * 8 + plane, shard), device_id_type=MESH,
        )

    def plane_leg(home, slot):
        return pltpu.make_async_remote_copy(
            src_ref=mid.at[home], dst_ref=back.at[slot],
            send_sem=send.at[1, home], recv_sem=recv.at[1, slot],
            device_id=(column * 8 + home, head), device_id_type=MESH,
        )

    level_stay = pltpu.make_async_copy(packed_ref.at[head], mid.at[head], local_sem.at[0])
    plane_stay = pltpu.make_async_copy(mid.at[plane], back.at[plane], local_sem.at[1])
    level_stay.start()

    def start(step):
        shard = lax.rem(head + step, 8)

        @pl.when(shard != head)
        def _():
            level_leg(shard, head).start()

    each(start)

    def forward(step):
        home = lax.rem(plane + step, 8)

        @pl.when(home == head)
        def _():
            level_stay.wait()

        @pl.when(home != head)
        def _():
            level_leg(0, home).wait_recv()

        @pl.when(home == plane)
        def _():
            plane_stay.start()

        @pl.when(home != plane)
        def _():
            plane_leg(home, plane).start()

    each(forward)
    for load in lent:
        load.start()
    for load in loads:
        load.wait()

    def wait(group):
        @pl.when(group == plane)
        def _():
            plane_stay.wait()

        @pl.when(group != plane)
        def _():
            plane_leg(0, group).wait_recv()

    each(wait)

    attended = back[...].reshape(D, TOK)
    updated = points[...].astype(F32) + lax.dot_general(
        attended, w_out[...], (((0,), (0,)), ((), ())), preferred_element_type=F32
    )
    updated = updated.astype(BF16).astype(F32)
    normed = normalise(updated, gain[...]).astype(BF16)
    low, high = updated[:, :256], updated[:, 256:]
    for part in range(GROUPS):
        if part < 4:
            own[part].wait()
        else:
            lent[part - 4].wait_recv()
        hidden = jnp.dot(normed, slabs[part, :D], preferred_element_type=F32)
        hidden = (hidden * (0.5 * (1.0 + lax.erf(hidden * (2.0 ** -0.5))))).astype(BF16)
        low = low + jnp.dot(hidden, slabs[part, D:D + 256], preferred_element_type=F32)
        high = high + jnp.dot(hidden, slabs[part, D + 256:], preferred_element_type=F32)
    out_ref[:, :256] = low.astype(BF16)
    out_ref[:, 256:] = high.astype(BF16)

    def sent(index):
        @pl.when(index != head)
        def _():
            level_leg(index, head).wait_send()

        @pl.when(index != plane)
        def _():
            plane_leg(index, plane).wait_send()

    each(sent)
    for load in lent:
        load.wait_send()


def finish(points, packed, w_out, gain, weights):
    hbm = pl.BlockSpec(memory_space=pltpu.HBM)
    return pl.pallas_call(
        finish_kernel,
        out_shape=jax.ShapeDtypeStruct((TOK, D), BF16),
        in_specs=[hbm] * 8,
        out_specs=pl.BlockSpec(memory_space=pltpu.VMEM),
        scratch_shapes=[
            pltpu.VMEM((TOK, D), BF16),
            pltpu.VMEM((D, D), BF16),
            pltpu.VMEM((1, D), F32),
            pltpu.VMEM((GROUPS, 2 * D, 256), BF16),
            pltpu.VMEM((GROUPS, 64, TOK), BF16),
            pltpu.VMEM((GROUPS, 64, TOK), BF16),
            pltpu.SemaphoreType.DMA((2, 8)),
            pltpu.SemaphoreType.DMA((2, 8)),
            pltpu.SemaphoreType.DMA((2,)),
            pltpu.SemaphoreType.DMA((3,)),
            pltpu.SemaphoreType.DMA((4,)),
            pltpu.SemaphoreType.DMA((4,)),
            pltpu.SemaphoreType.DMA((4,)),
        ],
        compiler_params=pltpu.CompilerParams(
            collective_id=1, has_side_effects=True, vmem_limit_bytes=40 << 20
        ),
        name="finish",
    )(points, packed, w_out, gain.reshape(1, D), *weights)


def exchange_kernel(
    points_ref, gain_ref, w_ref, scale_ref, place_ref, counts_ref, route_ref, local_ref, w1_ref, w2_ref,
    kv_out, q_out, route_out, local_out, own_out, own_top_out, own_size_out, own_query_out, weights_out,
    kv_ref, q_ref, raw, queries, keys, turned, lhs, scores, own, own_top, own_size, own_query,
    all_send, all_recv, ring_send, ring_recv, pair_send, pair_recv, route_sem, local_sem, load_sem, own_sem,
):
    column, plane, head = swap_ids()
    core = lax.rem(head, 2)
    spot = column * 4 + head // 2
    after, before = lax.rem(spot + 1, 16), lax.rem(spot + 15, 16)
    right = ((after // 4) * 8 + plane, lax.rem(after, 4) * 2 + core)
    left = ((before // 4) * 8 + plane, lax.rem(before, 4) * 2 + core)
    pair = (column * 8 + plane, head + 1 - 2 * core)
    partner = (column * 8 + head, plane)
    diagonal = plane == head
    across = jnp.logical_not(diagonal)

    barrier = pltpu.get_barrier_semaphore()

    def greet(index, _):
        @pl.when(across | (index != head))
        def _():
            pl.semaphore_signal(barrier, inc=1, device_id=(column * 8 + head, index), device_id_type=MESH)
        return 0

    lax.fori_loop(0, 8, greet, 0)
    for other in (right, left, pair):
        pl.semaphore_signal(barrier, inc=1, device_id=other, device_id_type=MESH)

    def enter():
        @pl.when(diagonal)
        def _():
            pl.semaphore_wait(barrier, 10)

        @pl.when(across)
        def _():
            pl.semaphore_wait(barrier, 11)

    def rows(half):
        return pl.ds(half * LANES, LANES)

    def spread(group, half, shard):
        return pltpu.make_async_remote_copy(
            src_ref=kv_ref.at[group, rows(half)],
            dst_ref=kv_out.at[4 + lax.rem(plane, 2), shard, rows(half)],
            send_sem=all_send.at[half, group],
            recv_sem=all_recv.at[half, shard],
            device_id=(column * 8 + group, plane),
            device_id_type=MESH,
        )

    def landed(half, shard):
        return pltpu.make_async_remote_copy(
            src_ref=kv_ref.at[0, rows(half)],
            dst_ref=kv_out.at[4 + core, shard, rows(half)],
            send_sem=all_send.at[half, 0],
            recv_sem=all_recv.at[half, shard],
            device_id=pair,
            device_id_type=MESH,
        )

    def spread_q(group, shard):
        return pltpu.make_async_remote_copy(
            src_ref=q_ref.at[group],
            dst_ref=q_out.at[shard],
            send_sem=all_send.at[2, group],
            recv_sem=all_recv.at[2, shard],
            device_id=(column * 8 + group, plane),
            device_id_type=MESH,
        )

    def at_home(half):
        return pltpu.make_async_copy(
            kv_ref.at[plane, rows(half)], kv_out.at[4 + core, head, rows(half)], local_sem.at[half]
        )

    q_at_home = pltpu.make_async_copy(q_ref.at[plane], q_out.at[head], local_sem.at[2])
    routes_at_home = [
        pltpu.make_async_copy(route_ref, route_out, local_sem.at[3]),
        pltpu.make_async_copy(local_ref, local_out, local_sem.at[4]),
    ]
    routes_sent = [
        pltpu.make_async_remote_copy(
            src_ref=source, dst_ref=target, send_sem=route_sem.at[0, index], recv_sem=route_sem.at[1, index],
            device_id=partner, device_id_type=MESH,
        )
        for index, (source, target) in enumerate(((route_ref, route_out), (local_ref, local_out)))
    ]

    def start(group):
        @pl.when(across | (group != plane))
        def _():
            spread(group, 0, head).start()
            spread(group, 1, head).start()

    def start_q(group):
        @pl.when(across | (group != plane))
        def _():
            spread_q(group, head).start()

    joins = [
        pltpu.make_async_copy(source, weights_out.at[rows_at], load_sem.at[2 + index])
        for index, (source, rows_at) in enumerate((
            (w1_ref, pl.ds(0, D)), (w2_ref.at[:, pl.ds(0, 256)], pl.ds(D, 256)), (w2_ref.at[:, pl.ds(256, 256)], pl.ds(D + 256, 256)),
        ))
    ]
    for join in joins:
        join.start()

    normed = normalise(points_ref[...].astype(F32), gain_ref[...]).astype(BF16)
    for couple in range(GROUPS // 2):
        columns = slice(384 * couple, 384 * couple + 384)
        projected = jnp.dot(normed, w_ref[:, columns], preferred_element_type=F32)
        projected = (projected * scale_ref[:, columns]).astype(BF16)
        kv = jnp.dot(projected, place_ref[:, :256], preferred_element_type=F32).astype(BF16)
        q = jnp.dot(projected[:128], place_ref[:, 256:512], preferred_element_type=F32)
        q = (q + jnp.dot(projected[128:], place_ref[:, 512:], preferred_element_type=F32)).astype(BF16)
        for side in range(2):
            kv_ref[2 * couple + side] = kv[:, 128 * side:128 * side + 128]
            q_ref[2 * couple + side] = q[:, 128 * side:128 * side + 128]
        if couple == 0:
            enter()
        start(2 * couple)
        start(2 * couple + 1)
    each(start_q)

    @pl.when(diagonal)
    def _():
        at_home(0).start()
        at_home(1).start()
        q_at_home.start()
        for copy in routes_at_home:
            copy.start()

    @pl.when(across)
    def _():
        for copy in routes_sent:
            copy.start()


    def moved(source, target, half, send, recv, to):
        return pltpu.make_async_remote_copy(
            src_ref=kv_out.at[source, :, rows(half)], dst_ref=kv_out.at[target, :, rows(half)],
            send_sem=send, recv_sem=recv, device_id=to, device_id_type=MESH,
        )

    def hop(way, step, half):
        if way == 0:
            source, to = 4 - 2 * step + core, right
            target = 2 - 2 * step + core
        else:
            source, to = 4 + 2 * step + core, left
            target = 6 + 2 * step + core
        return moved(source, target, half, ring_send.at[way, step, half], ring_recv.at[way, step, half], to)

    def shared(place, half):
        return moved(2 * place + core, 2 * place + core, half, pair_send.at[place, half], pair_recv.at[place, half], pair)

    def taken(place, half):
        return moved(2 * place + 1 - core, 2 * place + 1 - core, half, pair_send.at[place, half], pair_recv.at[place, half], pair)

    for half in range(2):
        def wait(shard):
            @pl.when(across | (shard != head))
            def _():
                landed(half, shard).wait_recv()

        each(wait)

        @pl.when(diagonal)
        def _():
            at_home(half).wait()

        hop(0, 0, half).start()
        hop(1, 0, half).start()
        shared(2, half).start()
    def wait_q(shard):
        @pl.when(across | (shard != head))
        def _():
            spread_q(0, shard).wait_recv()

    each(wait_q)

    @pl.when(diagonal)
    def _():
        q_at_home.wait()

    loads = [
        pltpu.make_async_copy(kv_out.at[4 + core], raw, load_sem.at[0]),
        pltpu.make_async_copy(q_out, queries, load_sem.at[1]),
    ]
    for load in loads:
        load.start()
    for load in loads:
        load.wait()

    def own_keys(shard):
        at = pl.ds(pl.multiple_of(shard * TOK, TOK), TOK)
        keys[at, :] = keyed_rows(raw[shard], counts_ref[(column * 8 + head) * GROUPS + shard])[1]
        turn_values(raw[shard], turned, at, TOK)

    each(own_keys)

    def own_saved(shard):
        return (
            pltpu.make_async_copy(own.at[shard], own_out.at[shard], own_sem.at[0, shard]),
            pltpu.make_async_copy(own_top.at[shard], own_top_out.at[shard], own_sem.at[1, shard]),
            pltpu.make_async_copy(own_size.at[shard], own_size_out.at[shard], own_sem.at[2, shard]),
            pltpu.make_async_copy(own_query.at[shard], own_query_out.at[shard], own_sem.at[3, shard]),
        )

    def own_run(begin, end):
        def own_shard(shard, _):
            patch = shard // 4
            packed = queries[shard]
            spread_heads(packed, lhs)
            most = None
            spots = [pl.ds(pl.multiple_of(patch * PATCH + piece * CHUNK, CHUNK), CHUNK) for piece in range(2)]
            for piece in range(2):
                found = scores_of(keys[spots[piece], :], lhs)
                scores[piece] = found
                found = jnp.max(found, axis=0, keepdims=True)
                most = found if piece == 0 else jnp.maximum(most, found)
            own_top[shard] = most
            total = [None] * 4
            for piece in range(2):
                weights = jnp.exp2(scores[piece] - most).astype(BF16)
                for index in range(4):
                    rows_of = slice(32 * index, 32 * index + 32)
                    term = jnp.dot(
                        turned[rows_of, spots[piece]], head_columns(weights, index), preferred_element_type=F32
                    )
                    total[index] = term if piece == 0 else total[index] + term
            for index in range(4):
                own[shard, 32 * index:32 * index + 32] = total[index]
                columns = slice(TOK * index, TOK * index + TOK)
                size = jnp.max(jnp.abs(total[index]), axis=0, keepdims=True) * 1e-12
                own_size[shard, :, columns] = jnp.maximum(size, jnp.abs(most[:, columns]) * (1.0 / 55.0))
            own_query[shard] = jnp.maximum(norms(half_of(packed, 0)), norms(half_of(packed, 1)))
            for save in own_saved(shard):
                save.start()
            return 0

        lax.fori_loop(begin, end, own_shard, 0)

    for half in range(2):
        hop(0, 0, half).wait_recv()
        hop(0, 1, half).start()
        hop(1, 0, half).wait_recv()
        hop(1, 1, half).start()
        shared(1, half).start()
        shared(3, half).start()
        own_run(4 * half, 4 * half + 4)
    for half in range(2):
        hop(0, 1, half).wait_recv()
        shared(0, half).start()
        hop(1, 1, half).wait_recv()
        shared(4, half).start()

    def sent(group):
        @pl.when(across | (group != plane))
        def _():
            spread(group, 0, head).wait_send()
            spread(group, 1, head).wait_send()
            spread_q(group, head).wait_send()

    each(sent)

    @pl.when(diagonal)
    def _():
        for copy in routes_at_home:
            copy.wait()

    @pl.when(across)
    def _():
        for copy in routes_sent:
            copy.wait()


    for half in range(2):
        for way in range(2):
            for step in range(2):
                hop(way, step, half).wait_send()
        for place in range(5):
            shared(place, half).wait_send()
            taken(place, half).wait_recv()
    for join in joins:
        join.wait()

    def saved(shard):
        for save in own_saved(shard):
            save.wait()

    each(saved)


def exchange(points, gain, w_qkv, counts, routes, local, w1, w2):
    scale = np.ones((1, 1536), np.float32)
    scale[0, np.arange(1536) % 48 < 16] = HEAD_DIM ** -0.5 * math.log2(math.e)
    vmem = pl.BlockSpec(memory_space=pltpu.VMEM)
    anywhere = pl.BlockSpec(memory_space=pltpu.HBM)
    return pl.pallas_call(
        exchange_kernel,
        out_shape=(
            jax.ShapeDtypeStruct((10, GROUPS, TOK, LANES), BF16),
            jax.ShapeDtypeStruct((GROUPS, LANES, LANES), BF16),
            jax.ShapeDtypeStruct((1, LANES), jnp.int32),
            jax.ShapeDtypeStruct((1, LANES), jnp.int32),
            jax.ShapeDtypeStruct((GROUPS, LANES, TOK), F32),
            jax.ShapeDtypeStruct((GROUPS, 1, ROWS), F32),
            jax.ShapeDtypeStruct((GROUPS, 1, ROWS), F32),
            jax.ShapeDtypeStruct((GROUPS, 1, LANES), F32),
            jax.ShapeDtypeStruct((2 * D, 256), BF16),
        ),
        in_specs=[vmem] * 5 + [pl.BlockSpec(memory_space=pltpu.SMEM)] + [anywhere] * 4,
        out_specs=(anywhere,) * 9,
        scratch_shapes=[
            pltpu.VMEM((GROUPS, TOK, LANES), BF16),
            pltpu.VMEM((GROUPS, LANES, LANES), BF16),
            pltpu.VMEM((GROUPS, TOK, LANES), BF16),
            pltpu.VMEM((GROUPS, LANES, LANES), BF16),
            pltpu.VMEM((NPL * PATCH, LANES), BF16),
            pltpu.VMEM((LANES, NPL * PATCH), BF16),
            pltpu.VMEM((ROWS, LANES), BF16),
            pltpu.VMEM((2, CHUNK, ROWS), F32),
            pltpu.VMEM((GROUPS, LANES, TOK), F32),
            pltpu.VMEM((GROUPS, 1, ROWS), F32),
            pltpu.VMEM((GROUPS, 1, ROWS), F32),
            pltpu.VMEM((GROUPS, 1, LANES), F32),
            pltpu.SemaphoreType.DMA((3, 8)),
            pltpu.SemaphoreType.DMA((3, 8)),
            pltpu.SemaphoreType.DMA((2, 2, 2)),
            pltpu.SemaphoreType.DMA((2, 2, 2)),
            pltpu.SemaphoreType.DMA((5, 2)),
            pltpu.SemaphoreType.DMA((5, 2)),
            pltpu.SemaphoreType.DMA((2, 2)),
            pltpu.SemaphoreType.DMA((5,)),
            pltpu.SemaphoreType.DMA((5,)),
            pltpu.SemaphoreType.DMA((4, 8)),
        ],
        compiler_params=pltpu.CompilerParams(collective_id=0, has_side_effects=True, vmem_limit_bytes=60 << 20),
        name="exchange",
    )(
        points, gain.reshape(1, D), w_qkv, jnp.asarray(scale), jnp.asarray(placing(), BF16),
        counts, routes, local, w1, w2,
    )


def per_device(
    points, gain_attn, w_qkv, w_out, gain_mlp, w_fc1, w_fc2, contact_route, contact_patch, counts
):
    slots, q, routes, local, sums, tops, sizes, tallest, joined = exchange(
        points, gain_attn, w_qkv, counts, contact_route.reshape(1, -1), contact_patch, w_fc1, w_fc2
    )
    weights = [joined]
    for step in range(1, 4):
        pairs = [(head, (head + 2 * step) % GROUPS) for head in range(GROUPS)]
        weights.append(lax.ppermute(joined, "head", pairs))
    packed = attend(routes, local, counts, q, slots.reshape(20, PATCH, LANES), sums, tops, sizes, tallest)
    return finish(points, packed, w_out, gain_mlp, weights)


def solution(mesh):
    return jax.shard_map(
        per_device,
        mesh=mesh,
        in_specs=(
            P(("seq", "head"), None), P(), P(), P(), P(), P(None, "head"), P("head", None),
            P("head", None, None), P("head", None), P(),
        ),
        out_specs=P(("seq", "head"), None),
        check_vma=False,
    )
```

```python
import functools
import math

import jax
import jax.numpy as jnp
import numpy as np
from jax import lax
from jax.experimental import pallas as pl
from jax.experimental.pallas import tpu as pltpu
from jax.sharding import PartitionSpec as P

D = 512
HEADS = 32
HEAD_DIM = 16
PATCH = 1024
CB = 2
NPL = 2
REACH = 4
TOK = 256
GROUPS = 8
LANES = 128
CHUNK = 512
F32 = jnp.float32
BF16 = jnp.bfloat16
MASKED = -3.3e38
ROWS = 8 * LANES
MESH = pl.DeviceIdType.MESH


def placing():
    kv = np.zeros((384, 256), np.float32)
    low = np.zeros((384, 256), np.float32)
    high = np.zeros((384, 256), np.float32)
    for group in range(2):
        for head in range(4):
            for dim in range(HEAD_DIM):
                source = group * 192 + head * 48 + dim
                lane = group * 128 + head * 16 + dim
                low[source, lane] = 1
                high[source, lane + 64] = 1
                kv[source + 16, lane] = 1
                kv[source + 32, lane + 64] = 1
    return np.concatenate([kv, low, high], axis=1)


def lane_of(shape):
    return lax.broadcasted_iota(jnp.int32, shape, len(shape) - 1)


def normalise(values, gain):
    centred = values - jnp.mean(values, axis=-1, keepdims=True)
    spread = jnp.mean(centred * centred, axis=-1, keepdims=True)
    return centred * lax.rsqrt(spread + 1e-05) * gain


def swap_ids():
    seq, head = lax.axis_index("seq"), lax.axis_index("head")
    column = seq // 8
    return column, seq - column * 8, head


def iotas(rows):
    shape = (rows, LANES)
    return lax.broadcasted_iota(jnp.int32, shape, 0), lax.broadcasted_iota(jnp.int32, shape, 1)


def value_picker():
    row, lane = iotas(LANES)
    return ((row % 32 < 16) & (lane == 64 + row // 32 * 16 + row % 32)).astype(F32).astype(BF16)


def keyed_rows(block, count):
    row, lane = iotas(TOK)
    zero = jnp.zeros((TOK, LANES), BF16)
    valid = row < count
    flag = jnp.where(valid, zero, jnp.where(lane < 66, jnp.full_like(zero, MASKED), zero))
    keyed = jnp.where((lane < 64) & valid, block, zero)
    return keyed, jnp.where(lane < 64, keyed, flag)


def norms(values):
    row, lane = iotas(LANES)
    sum_of = ((lane == row // 16) & (lane < 4)).astype(F32).astype(BF16)
    size = jnp.minimum(jnp.abs(values), jnp.full_like(values, 1e15))
    size = jnp.where(lax.broadcasted_iota(jnp.int32, values.shape, 1) < 64, size, jnp.zeros_like(size))
    return jnp.max(jnp.dot(size * size, sum_of, preferred_element_type=F32), axis=0, keepdims=True)


def turn_values(vals, turned, at, size):
    ones_row = lax.broadcasted_iota(jnp.int32, (LANES, size), 0) % 32 >= 16
    picked = lax.dot_general(value_picker(), vals, (((1,), (1,)), ((), ())), preferred_element_type=F32)
    turned[:, at] = jnp.where(ones_row, 1.0, picked).astype(BF16)


def half_of(packed, half):
    return packed if half == 0 else pltpu.roll(packed.astype(F32), 64, 1).astype(BF16)


def spread_heads(packed, lhs):
    _, lane = iotas(LANES)
    flags = jnp.where((lane >= 64) & (lane < 66), jnp.ones_like(packed), jnp.zeros_like(packed))
    for half in range(2):
        q = half_of(packed, half)
        for head in range(4):
            mine = (lane >= 16 * head) & (lane < 16 * head + 16)
            lhs[pl.ds((head * 2 + half) * LANES, LANES), :] = jnp.where(mine, q, flags)


def scores_of(keys, lhs):
    return lax.dot_general(keys, lhs[...], (((1,), (1,)), ((), ())), preferred_element_type=F32)


def head_columns(values, head):
    return values[:, TOK * head:TOK * head + TOK]


def attend_kernel(
    routes_hbm, local_hbm, counts_hbm, q_hbm, kv_ref, own_hbm, own_top_hbm, own_size_hbm, own_query_hbm, out_ref,
    routes_ref, local_ref, counts_ref, q_ref, own_ref, own_top_ref, own_size_ref, own_query_ref,
    raw, keys, vals, turned, lhs, acc, top, done, sems, small_sems, out_sems,
):
    column, _, head_index = swap_ids()
    seq = column * 8 + head_index
    core = lax.rem(head_index, 2)
    loads = [
        pltpu.make_async_copy(source, target, small_sems.at[index])
        for index, (source, target) in enumerate((
            (routes_hbm, routes_ref), (local_hbm, local_ref), (counts_hbm, counts_ref),
            (q_hbm, q_ref), (own_hbm, own_ref), (own_top_hbm, own_top_ref),
            (own_size_hbm, own_size_ref), (own_query_hbm, own_query_ref),
        ))
    ]
    for load in loads:
        load.start()
    for load in loads[:3]:
        load.wait()

    def source(patch, which):
        row = seq * NPL * CB + patch * CB + which
        route = routes_ref[0, row]
        offset = jnp.where(route < REACH, route - REACH, route - REACH + 1)
        local = local_ref[0, row]
        owner = lax.rem(seq + offset + 32, 32)
        return (offset + REACH + core) * NPL + local, owner * GROUPS + local * 4

    for patch in range(NPL):
        for which in range(CB):
            slot, _ = source(patch, which)
            pltpu.make_async_copy(kv_ref.at[slot], raw.at[patch * CB + which], sems.at[patch * CB + which]).start()
    for load in loads[3:]:
        load.wait()

    _, lane_kv = iotas(TOK)
    zero = jnp.zeros((TOK, LANES), BF16)

    def patch_body(patch, _):
        for which in range(CB):
            pltpu.make_async_copy(kv_ref.at[0], raw.at[patch * CB + which], sems.at[patch * CB + which]).wait()

        first = jnp.int32(0)
        key_top = jnp.zeros((1, LANES), F32)
        val_top = jnp.zeros((1, LANES), F32)
        for which in range(CB):
            _, shard = source(patch, which)
            for part in range(4):
                count = counts_ref[shard + part]
                block = raw[patch * CB + which, TOK * part:TOK * part + TOK, :]
                keyed, marked = keyed_rows(block, count)
                at = pl.ds(pl.multiple_of(first, 16), TOK)
                keys[at, :] = marked
                vals[at, :] = block
                key_top = jnp.maximum(key_top, norms(keyed))
                size = jnp.max(jnp.where(lane_kv < 64, zero, jnp.abs(block)).astype(F32), axis=0, keepdims=True)
                val_top = jnp.maximum(val_top, size)
                first = first + (count + 15) // 16 * 16
        tail = pl.ds(pl.multiple_of(first, 16), TOK)
        keys[tail, :] = keyed_rows(zero, 0)[1]
        vals[tail, :] = zero
        pieces = (first + TOK - 1) // TOK
        chunks = pieces // 2
        odd = pieces % 2 == 1

        def turn(piece, _):
            at = pl.ds(pl.multiple_of(piece * TOK, TOK), TOK)
            turn_values(vals[at, :], turned, at, TOK)
            return 0

        lax.fori_loop(0, pieces, turn, 0)

        query_top, own_size = own_query_ref[patch * 4], own_size_ref[patch * 4]
        for part in range(1, 4):
            query_top = jnp.maximum(query_top, own_query_ref[patch * 4 + part])
            own_size = jnp.maximum(own_size, own_size_ref[patch * 4 + part])
        sizes = jnp.maximum(query_top * key_top * (1.0 / 3000.0), val_top * 1e-9)
        fits = jnp.maximum(jnp.max(sizes), jnp.max(own_size)) < 1.0

        def shards_body(couple, _):
            shards = [patch * 4 + couple * 2 + side for side in range(2)]
            for side in range(2):
                spread_heads(q_ref[shards[side]], lhs.at[pl.ds(side * ROWS, ROWS)])

            def over_chunks(body):
                def chunk_body(chunk, _):
                    body(pl.ds(pl.multiple_of(chunk * CHUNK, CHUNK), CHUNK))
                    return 0

                lax.fori_loop(0, chunks, chunk_body, 0)

                @pl.when(odd)
                def _():
                    body(pl.ds(pl.multiple_of(chunks * CHUNK, CHUNK), TOK))

            def begin(side, scale):
                for head in range(4):
                    rows = slice(32 * head, 32 * head + 32)
                    acc[side, rows] = own_ref[shards[side], rows] * head_columns(scale, head)

            def gather(at, weights):
                for side in range(2):
                    for head in range(4):
                        rows = slice(32 * head, 32 * head + 32)
                        acc[side, rows] += jnp.dot(
                            turned[rows, at], head_columns(weights, side * 4 + head), preferred_element_type=F32
                        )

            @pl.when(fits)
            def _():
                for side in range(2):
                    begin(side, jnp.exp2(own_top_ref[shards[side]]))
                over_chunks(lambda at: gather(at, jnp.exp2(scores_of(keys[at, :], lhs)).astype(BF16)))

            @pl.when(jnp.logical_not(fits))
            def _():
                for side in range(2):
                    top[:, pl.ds(side * ROWS, ROWS)] = own_top_ref[shards[side]]

                def raise_top(at):
                    top[...] = jnp.maximum(top[...], jnp.max(scores_of(keys[at, :], lhs), axis=0, keepdims=True))

                over_chunks(raise_top)
                for side in range(2):
                    begin(side, jnp.exp2(own_top_ref[shards[side]] - top[:, pl.ds(side * ROWS, ROWS)]))
                over_chunks(lambda at: gather(at, jnp.exp2(scores_of(keys[at, :], lhs) - top[...]).astype(BF16)))

            for side in range(2):
                joined = [
                    acc[side, 32 * head:32 * head + 16] / acc[side, 32 * head + 16:32 * head + 32] for head in range(4)
                ]
                shard = shards[side]
                done[shard] = jnp.concatenate(joined, axis=0).astype(BF16)
                pltpu.make_async_copy(done.at[shard], out_ref.at[shard], out_sems.at[shard]).start()
            return 0

        lax.fori_loop(0, 2, shards_body, 0)
        return 0

    lax.fori_loop(0, NPL, patch_body, 0)
    for shard in range(GROUPS):
        pltpu.make_async_copy(done.at[shard], out_ref.at[shard], out_sems.at[shard]).wait()


def attend(routes, local, counts, q, kv, own, own_top, own_size, own_query):
    hbm = pl.BlockSpec(memory_space=pltpu.HBM)
    most = CB * PATCH + TOK
    return pl.pallas_call(
        attend_kernel,
        out_shape=jax.ShapeDtypeStruct((GROUPS, 64, TOK), BF16),
        in_specs=[hbm] * 9,
        out_specs=hbm,
        scratch_shapes=[
            pltpu.SMEM((1, LANES), jnp.int32),
            pltpu.SMEM((1, LANES), jnp.int32),
            pltpu.SMEM((256,), jnp.int32),
            pltpu.VMEM((GROUPS, LANES, LANES), BF16),
            pltpu.VMEM((GROUPS, LANES, TOK), F32),
            pltpu.VMEM((GROUPS, 1, ROWS), F32),
            pltpu.VMEM((GROUPS, 1, ROWS), F32),
            pltpu.VMEM((GROUPS, 1, LANES), F32),
            pltpu.VMEM((NPL * CB, PATCH, LANES), BF16),
            pltpu.VMEM((most, LANES), BF16),
            pltpu.VMEM((most, LANES), BF16),
            pltpu.VMEM((LANES, most), BF16),
            pltpu.VMEM((2 * ROWS, LANES), BF16),
            pltpu.VMEM((2, LANES, TOK), F32),
            pltpu.VMEM((1, 2 * ROWS), F32),
            pltpu.VMEM((GROUPS, 64, TOK), BF16),
            pltpu.SemaphoreType.DMA((NPL * CB,)),
            pltpu.SemaphoreType.DMA((8,)),
            pltpu.SemaphoreType.DMA((8,)),
        ],
        compiler_params=pltpu.CompilerParams(vmem_limit_bytes=60 << 20),
        cost_estimate=pl.CostEstimate(flops=20_000_000_000, bytes_accessed=6_000_000, transcendentals=17_000_000),
        name="attend",
    )(routes, local, counts, q, kv, own, own_top, own_size, own_query)


def each(body):
    def step(index, _):
        body(index)
        return 0

    lax.fori_loop(0, 8, step, 0)


def finish_kernel(
    points_ref, packed_ref, w_out_ref, gain_ref, w0_ref, w1_ref, w2_ref, w3_ref, out_ref,
    points, w_out, gain, slabs, mid, back, send, recv, local_sem, load_sem, weight_sem, pair_send, pair_recv,
):
    column, plane, head = swap_ids()
    barrier = pltpu.get_barrier_semaphore()

    def greet(index):
        @pl.when(index != head)
        def _():
            pl.semaphore_signal(barrier, inc=1, device_id=(column * 8 + plane, index), device_id_type=MESH)

        @pl.when(index != plane)
        def _():
            pl.semaphore_signal(barrier, inc=1, device_id=(column * 8 + index, head), device_id_type=MESH)

    each(greet)
    pair = (column * 8 + plane, head + 1 - 2 * lax.rem(head, 2))
    loads = [
        pltpu.make_async_copy(points_ref, points, load_sem.at[0]),
        pltpu.make_async_copy(w_out_ref, w_out, load_sem.at[1]),
        pltpu.make_async_copy(gain_ref, gain, load_sem.at[2]),
    ]
    for load in loads:
        load.start()

    shards = (w0_ref, w1_ref, w2_ref, w3_ref)
    own = [pltpu.make_async_copy(shard, slabs.at[part], weight_sem.at[part]) for part, shard in enumerate(shards)]
    lent = [
        pltpu.make_async_remote_copy(
            src_ref=shard, dst_ref=slabs.at[4 + part], send_sem=pair_send.at[part], recv_sem=pair_recv.at[part],
            device_id=pair, device_id_type=MESH,
        )
        for part, shard in enumerate(shards)
    ]
    for load in own:
        load.start()

    pl.semaphore_wait(barrier, 14)

    def level_leg(shard, slot):
        return pltpu.make_async_remote_copy(
            src_ref=packed_ref.at[shard], dst_ref=mid.at[slot],
            send_sem=send.at[0, shard], recv_sem=recv.at[0, slot],
            device_id=(column * 8 + plane, shard), device_id_type=MESH,
        )

    def plane_leg(home, slot):
        return pltpu.make_async_remote_copy(
            src_ref=mid.at[home], dst_ref=back.at[slot],
            send_sem=send.at[1, home], recv_sem=recv.at[1, slot],
            device_id=(column * 8 + home, head), device_id_type=MESH,
        )

    level_stay = pltpu.make_async_copy(packed_ref.at[head], mid.at[head], local_sem.at[0])
    plane_stay = pltpu.make_async_copy(mid.at[plane], back.at[plane], local_sem.at[1])
    level_stay.start()

    def start(step):
        shard = step

        @pl.when(shard != head)
        def _():
            level_leg(shard, head).start()

    each(start)

    def forward(step):
        home = step

        @pl.when(home == head)
        def _():
            level_stay.wait()

        @pl.when(home != head)
        def _():
            level_leg(0, home).wait_recv()

        @pl.when(home == plane)
        def _():
            plane_stay.start()

        @pl.when(home != plane)
        def _():
            plane_leg(home, plane).start()

    each(forward)
    for load in lent:
        load.start()
    for load in loads:
        load.wait()

    def wait(group):
        @pl.when(group == plane)
        def _():
            plane_stay.wait()

        @pl.when(group != plane)
        def _():
            plane_leg(0, group).wait_recv()

    each(wait)

    attended = back[...].reshape(D, TOK)
    updated = points[...].astype(F32) + lax.dot_general(
        attended, w_out[...], (((0,), (0,)), ((), ())), preferred_element_type=F32
    )
    updated = updated.astype(BF16).astype(F32)
    normed = normalise(updated, gain[...]).astype(BF16)
    low, high = updated[:, :256], updated[:, 256:]
    for part in range(GROUPS):
        if part < 4:
            own[part].wait()
        else:
            lent[part - 4].wait_recv()
        hidden = jnp.dot(normed, slabs[part, :D], preferred_element_type=F32)
        hidden = (hidden * (0.5 * (1.0 + lax.erf(hidden * (2.0 ** -0.5))))).astype(BF16)
        low = low + jnp.dot(hidden, slabs[part, D:D + 256], preferred_element_type=F32)
        high = high + jnp.dot(hidden, slabs[part, D + 256:], preferred_element_type=F32)
    out_ref[:, :256] = low.astype(BF16)
    out_ref[:, 256:] = high.astype(BF16)

    def sent(index):
        @pl.when(index != head)
        def _():
            level_leg(index, head).wait_send()

        @pl.when(index != plane)
        def _():
            plane_leg(index, plane).wait_send()

    each(sent)
    for load in lent:
        load.wait_send()


def finish(points, packed, w_out, gain, weights):
    hbm = pl.BlockSpec(memory_space=pltpu.HBM)
    return pl.pallas_call(
        finish_kernel,
        out_shape=jax.ShapeDtypeStruct((TOK, D), BF16),
        in_specs=[hbm] * 8,
        out_specs=pl.BlockSpec(memory_space=pltpu.VMEM),
        scratch_shapes=[
            pltpu.VMEM((TOK, D), BF16),
            pltpu.VMEM((D, D), BF16),
            pltpu.VMEM((1, D), F32),
            pltpu.VMEM((GROUPS, 2 * D, 256), BF16),
            pltpu.VMEM((GROUPS, 64, TOK), BF16),
            pltpu.VMEM((GROUPS, 64, TOK), BF16),
            pltpu.SemaphoreType.DMA((2, 8)),
            pltpu.SemaphoreType.DMA((2, 8)),
            pltpu.SemaphoreType.DMA((2,)),
            pltpu.SemaphoreType.DMA((3,)),
            pltpu.SemaphoreType.DMA((4,)),
            pltpu.SemaphoreType.DMA((4,)),
            pltpu.SemaphoreType.DMA((4,)),
        ],
        compiler_params=pltpu.CompilerParams(
            collective_id=1, has_side_effects=True, vmem_limit_bytes=60 << 20
        ),
        name="finish",
    )(points, packed, w_out, gain.reshape(1, D), *weights)


def exchange_kernel(
    points_ref, gain_ref, w_ref, scale_ref, place_ref, counts_ref, route_ref, local_ref, w1_ref, w2_ref,
    kv_out, q_out, route_out, local_out, own_out, own_top_out, own_size_out, own_query_out, weights_out, weights_below, weights_above,
    kv_ref, q_ref, raw, queries, keys, turned, lhs, scores, own, own_top, own_size, own_query,
    all_send, all_recv, ring_send, ring_recv, pair_send, pair_recv, route_sem, local_sem, load_sem, own_sem, near_send, near_recv,
):
    column, plane, head = swap_ids()
    core = lax.rem(head, 2)
    spot = column * 4 + head // 2
    after, before = lax.rem(spot + 1, 16), lax.rem(spot + 15, 16)
    right = ((after // 4) * 8 + plane, lax.rem(after, 4) * 2 + core)
    left = ((before // 4) * 8 + plane, lax.rem(before, 4) * 2 + core)
    pair = (column * 8 + plane, head + 1 - 2 * core)
    partner = (column * 8 + head, plane)
    diagonal = plane == head
    across = jnp.logical_not(diagonal)

    barrier = pltpu.get_barrier_semaphore()

    def greet(index, _):
        @pl.when(across | (index != head))
        def _():
            pl.semaphore_signal(barrier, inc=1, device_id=(column * 8 + head, index), device_id_type=MESH)
        return 0

    lax.fori_loop(0, 8, greet, 0)
    level = head // 2
    above = (column * 8 + plane, lax.rem(level + 1, 4) * 2 + core)
    below = (column * 8 + plane, lax.rem(level + 3, 4) * 2 + core)
    for other in (right, left, pair, above, below):
        pl.semaphore_signal(barrier, inc=1, device_id=other, device_id_type=MESH)

    def enter():
        @pl.when(diagonal)
        def _():
            pl.semaphore_wait(barrier, 12)

        @pl.when(across)
        def _():
            pl.semaphore_wait(barrier, 13)

    def rows(half):
        return pl.ds(half * LANES, LANES)

    def spread(group, half, shard):
        return pltpu.make_async_remote_copy(
            src_ref=kv_ref.at[group, rows(half)],
            dst_ref=kv_out.at[4 + lax.rem(plane, 2), shard, rows(half)],
            send_sem=all_send.at[half, group],
            recv_sem=all_recv.at[half, shard],
            device_id=(column * 8 + group, plane),
            device_id_type=MESH,
        )

    def landed(half, shard):
        return pltpu.make_async_remote_copy(
            src_ref=kv_ref.at[0, rows(half)],
            dst_ref=kv_out.at[4 + core, shard, rows(half)],
            send_sem=all_send.at[half, 0],
            recv_sem=all_recv.at[half, shard],
            device_id=pair,
            device_id_type=MESH,
        )

    def spread_q(group, shard):
        return pltpu.make_async_remote_copy(
            src_ref=q_ref.at[group],
            dst_ref=q_out.at[shard],
            send_sem=all_send.at[2, group],
            recv_sem=all_recv.at[2, shard],
            device_id=(column * 8 + group, plane),
            device_id_type=MESH,
        )

    def at_home(half):
        return pltpu.make_async_copy(
            kv_ref.at[plane, rows(half)], kv_out.at[4 + core, head, rows(half)], local_sem.at[half]
        )

    q_at_home = pltpu.make_async_copy(q_ref.at[plane], q_out.at[head], local_sem.at[2])
    routes_at_home = [
        pltpu.make_async_copy(route_ref, route_out, local_sem.at[3]),
        pltpu.make_async_copy(local_ref, local_out, local_sem.at[4]),
    ]
    routes_sent = [
        pltpu.make_async_remote_copy(
            src_ref=source, dst_ref=target, send_sem=route_sem.at[0, index], recv_sem=route_sem.at[1, index],
            device_id=partner, device_id_type=MESH,
        )
        for index, (source, target) in enumerate(((route_ref, route_out), (local_ref, local_out)))
    ]

    def start(group):
        @pl.when(across | (group != plane))
        def _():
            spread(group, 0, head).start()
            spread(group, 1, head).start()

    def start_q(group):
        @pl.when(across | (group != plane))
        def _():
            spread_q(group, head).start()

    parts = (
        (w1_ref, pl.ds(0, D)), (w2_ref.at[:, pl.ds(0, 256)], pl.ds(D, 256)), (w2_ref.at[:, pl.ds(256, 256)], pl.ds(D + 256, 256)),
    )
    joins = [
        pltpu.make_async_copy(source, weights_out.at[rows_at], load_sem.at[2 + index])
        for index, (source, rows_at) in enumerate(parts)
    ]
    nears = [
        pltpu.make_async_remote_copy(
            src_ref=source, dst_ref=target.at[rows_at], send_sem=near_send.at[way, index],
            recv_sem=near_recv.at[way, index], device_id=to, device_id_type=MESH,
        )
        for way, (target, to) in enumerate(((weights_below, above), (weights_above, below)))
        for index, (source, rows_at) in enumerate(parts)
    ]
    for join in joins:
        join.start()

    normed = normalise(points_ref[...].astype(F32), gain_ref[...]).astype(BF16)
    for couple in range(GROUPS // 2):
        columns = slice(384 * couple, 384 * couple + 384)
        projected = jnp.dot(normed, w_ref[:, columns], preferred_element_type=F32)
        projected = (projected * scale_ref[:, columns]).astype(BF16)
        kv = jnp.dot(projected, place_ref[:, :256], preferred_element_type=F32).astype(BF16)
        q = jnp.dot(projected[:128], place_ref[:, 256:512], preferred_element_type=F32)
        q = (q + jnp.dot(projected[128:], place_ref[:, 512:], preferred_element_type=F32)).astype(BF16)
        for side in range(2):
            kv_ref[2 * couple + side] = kv[:, 128 * side:128 * side + 128]
            q_ref[2 * couple + side] = q[:, 128 * side:128 * side + 128]
        if couple == 0:
            enter()
        start(2 * couple)
        start(2 * couple + 1)
    each(start_q)
    for near in nears:
        near.start()

    @pl.when(diagonal)
    def _():
        at_home(0).start()
        at_home(1).start()
        q_at_home.start()
        for copy in routes_at_home:
            copy.start()

    @pl.when(across)
    def _():
        for copy in routes_sent:
            copy.start()


    def moved(source, target, half, send, recv, to):
        return pltpu.make_async_remote_copy(
            src_ref=kv_out.at[source, :, rows(half)], dst_ref=kv_out.at[target, :, rows(half)],
            send_sem=send, recv_sem=recv, device_id=to, device_id_type=MESH,
        )

    def hop(way, step, half):
        if way == 0:
            source, to = 4 - 2 * step + core, right
            target = 2 - 2 * step + core
        else:
            source, to = 4 + 2 * step + core, left
            target = 6 + 2 * step + core
        return moved(source, target, half, ring_send.at[way, step, half], ring_recv.at[way, step, half], to)

    def shared(place, half):
        return moved(2 * place + core, 2 * place + core, half, pair_send.at[place, half], pair_recv.at[place, half], pair)

    def taken(place, half):
        return moved(2 * place + 1 - core, 2 * place + 1 - core, half, pair_send.at[place, half], pair_recv.at[place, half], pair)

    for half in range(2):
        def wait(shard):
            @pl.when(across | (shard != head))
            def _():
                landed(half, shard).wait_recv()

        each(wait)

        @pl.when(diagonal)
        def _():
            at_home(half).wait()

        hop(0, 0, half).start()
        hop(1, 0, half).start()
        shared(2, half).start()
    def wait_q(shard):
        @pl.when(across | (shard != head))
        def _():
            spread_q(0, shard).wait_recv()

    each(wait_q)

    @pl.when(diagonal)
    def _():
        q_at_home.wait()

    loads = [
        pltpu.make_async_copy(kv_out.at[4 + core], raw, load_sem.at[0]),
        pltpu.make_async_copy(q_out, queries, load_sem.at[1]),
    ]
    for load in loads:
        load.start()
    for load in loads:
        load.wait()

    def own_keys(shard):
        at = pl.ds(pl.multiple_of(shard * TOK, TOK), TOK)
        keys[at, :] = keyed_rows(raw[shard], counts_ref[(column * 8 + head) * GROUPS + shard])[1]
        turn_values(raw[shard], turned, at, TOK)

    each(own_keys)

    def own_saved(shard):
        return (
            pltpu.make_async_copy(own.at[shard], own_out.at[shard], own_sem.at[0, shard]),
            pltpu.make_async_copy(own_top.at[shard], own_top_out.at[shard], own_sem.at[1, shard]),
            pltpu.make_async_copy(own_size.at[shard], own_size_out.at[shard], own_sem.at[2, shard]),
            pltpu.make_async_copy(own_query.at[shard], own_query_out.at[shard], own_sem.at[3, shard]),
        )

    def own_run(begin, end):
        def own_shard(shard, _):
            patch = shard // 4
            packed = queries[shard]
            spread_heads(packed, lhs)
            most = None
            spots = [pl.ds(pl.multiple_of(patch * PATCH + piece * CHUNK, CHUNK), CHUNK) for piece in range(2)]
            for piece in range(2):
                found = scores_of(keys[spots[piece], :], lhs)
                scores[piece] = found
                found = jnp.max(found, axis=0, keepdims=True)
                most = found if piece == 0 else jnp.maximum(most, found)
            own_top[shard] = most
            total = [None] * 4
            for piece in range(2):
                weights = jnp.exp2(scores[piece] - most).astype(BF16)
                for index in range(4):
                    rows_of = slice(32 * index, 32 * index + 32)
                    term = jnp.dot(
                        turned[rows_of, spots[piece]], head_columns(weights, index), preferred_element_type=F32
                    )
                    total[index] = term if piece == 0 else total[index] + term
            for index in range(4):
                own[shard, 32 * index:32 * index + 32] = total[index]
                columns = slice(TOK * index, TOK * index + TOK)
                size = jnp.max(jnp.abs(total[index]), axis=0, keepdims=True) * 1e-12
                own_size[shard, :, columns] = jnp.maximum(size, jnp.abs(most[:, columns]) * (1.0 / 55.0))
            own_query[shard] = jnp.maximum(norms(half_of(packed, 0)), norms(half_of(packed, 1)))
            for save in own_saved(shard):
                save.start()
            return 0

        lax.fori_loop(begin, end, own_shard, 0)

    for half in range(2):
        hop(0, 0, half).wait_recv()
        hop(0, 1, half).start()
        hop(1, 0, half).wait_recv()
        hop(1, 1, half).start()
        shared(1, half).start()
        shared(3, half).start()
        own_run(4 * half, 4 * half + 4)
    for half in range(2):
        hop(0, 1, half).wait_recv()
        shared(0, half).start()
        hop(1, 1, half).wait_recv()
        shared(4, half).start()

    def sent(group):
        @pl.when(across | (group != plane))
        def _():
            spread(group, 0, head).wait_send()
            spread(group, 1, head).wait_send()
            spread_q(group, head).wait_send()

    each(sent)

    @pl.when(diagonal)
    def _():
        for copy in routes_at_home:
            copy.wait()

    @pl.when(across)
    def _():
        for copy in routes_sent:
            copy.wait()


    for half in range(2):
        for way in range(2):
            for step in range(2):
                hop(way, step, half).wait_send()
        for place in range(5):
            shared(place, half).wait_send()
            taken(place, half).wait_recv()
    for copy in (*joins, *nears):
        copy.wait()

    def saved(shard):
        for save in own_saved(shard):
            save.wait()

    each(saved)


def exchange(points, gain, w_qkv, counts, routes, local, w1, w2):
    scale = np.ones((1, 1536), np.float32)
    scale[0, np.arange(1536) % 48 < 16] = HEAD_DIM ** -0.5 * math.log2(math.e)
    vmem = pl.BlockSpec(memory_space=pltpu.VMEM)
    anywhere = pl.BlockSpec(memory_space=pltpu.HBM)
    return pl.pallas_call(
        exchange_kernel,
        out_shape=(
            jax.ShapeDtypeStruct((10, GROUPS, TOK, LANES), BF16),
            jax.ShapeDtypeStruct((GROUPS, LANES, LANES), BF16),
            jax.ShapeDtypeStruct((1, LANES), jnp.int32),
            jax.ShapeDtypeStruct((1, LANES), jnp.int32),
            jax.ShapeDtypeStruct((GROUPS, LANES, TOK), F32),
            jax.ShapeDtypeStruct((GROUPS, 1, ROWS), F32),
            jax.ShapeDtypeStruct((GROUPS, 1, ROWS), F32),
            jax.ShapeDtypeStruct((GROUPS, 1, LANES), F32),
            jax.ShapeDtypeStruct((2 * D, 256), BF16),
            jax.ShapeDtypeStruct((2 * D, 256), BF16),
            jax.ShapeDtypeStruct((2 * D, 256), BF16),
        ),
        in_specs=[vmem] * 5 + [pl.BlockSpec(memory_space=pltpu.SMEM)] + [anywhere] * 4,
        out_specs=(anywhere,) * 11,
        scratch_shapes=[
            pltpu.VMEM((GROUPS, TOK, LANES), BF16),
            pltpu.VMEM((GROUPS, LANES, LANES), BF16),
            pltpu.VMEM((GROUPS, TOK, LANES), BF16),
            pltpu.VMEM((GROUPS, LANES, LANES), BF16),
            pltpu.VMEM((NPL * PATCH, LANES), BF16),
            pltpu.VMEM((LANES, NPL * PATCH), BF16),
            pltpu.VMEM((ROWS, LANES), BF16),
            pltpu.VMEM((2, CHUNK, ROWS), F32),
            pltpu.VMEM((GROUPS, LANES, TOK), F32),
            pltpu.VMEM((GROUPS, 1, ROWS), F32),
            pltpu.VMEM((GROUPS, 1, ROWS), F32),
            pltpu.VMEM((GROUPS, 1, LANES), F32),
            pltpu.SemaphoreType.DMA((3, 8)),
            pltpu.SemaphoreType.DMA((3, 8)),
            pltpu.SemaphoreType.DMA((2, 2, 2)),
            pltpu.SemaphoreType.DMA((2, 2, 2)),
            pltpu.SemaphoreType.DMA((5, 2)),
            pltpu.SemaphoreType.DMA((5, 2)),
            pltpu.SemaphoreType.DMA((2, 2)),
            pltpu.SemaphoreType.DMA((5,)),
            pltpu.SemaphoreType.DMA((5,)),
            pltpu.SemaphoreType.DMA((4, 8)),
            pltpu.SemaphoreType.DMA((2, 3)),
            pltpu.SemaphoreType.DMA((2, 3)),
        ],
        compiler_params=pltpu.CompilerParams(collective_id=0, has_side_effects=True, vmem_limit_bytes=60 << 20),
        name="exchange",
    )(
        points, gain.reshape(1, D), w_qkv, jnp.asarray(scale), jnp.asarray(placing(), BF16),
        counts, routes, local, w1, w2,
    )


def per_device(
    points, gain_attn, w_qkv, w_out, gain_mlp, w_fc1, w_fc2, contact_route, contact_patch, counts
):
    slots, q, routes, local, sums, tops, sizes, tallest, joined, low, high = exchange(
        points, gain_attn, w_qkv, counts, contact_route.reshape(1, -1), contact_patch, w_fc1, w_fc2
    )
    far = lax.ppermute(joined, "head", [(head, (head + 4) % GROUPS) for head in range(GROUPS)])
    weights = [joined, low, high, far]
    packed = attend(routes, local, counts, q, slots.reshape(20, PATCH, LANES), sums, tops, sizes, tallest)
    return finish(points, packed, w_out, gain_mlp, weights)


def solution(mesh):
    return jax.shard_map(
        per_device,
        mesh=mesh,
        in_specs=(
            P(("seq", "head"), None), P(), P(), P(), P(), P(None, "head"), P("head", None),
            P("head", None, None), P("head", None), P(),
        ),
        out_specs=P(("seq", "head"), None),
        check_vma=False,
    )
```

```python
import functools
import math

import jax
import jax.numpy as jnp
import numpy as np
from jax import lax
from jax.experimental import pallas as pl
from jax.experimental.pallas import tpu as pltpu
from jax.sharding import PartitionSpec as P

D = 512
HEADS = 32
HEAD_DIM = 16
PATCH = 1024
CB = 2
NPL = 2
REACH = 4
TOK = 256
GROUPS = 8
LANES = 128
CHUNK = 512
F32 = jnp.float32
BF16 = jnp.bfloat16
MASKED = -3.3e38
ROWS = 8 * LANES
MESH = pl.DeviceIdType.MESH


def placing():
    kv = np.zeros((384, 256), np.float32)
    low = np.zeros((384, 256), np.float32)
    high = np.zeros((384, 256), np.float32)
    for group in range(2):
        for head in range(4):
            for dim in range(HEAD_DIM):
                source = group * 192 + head * 48 + dim
                lane = group * 128 + head * 16 + dim
                low[source, lane] = 1
                high[source, lane + 64] = 1
                kv[source + 16, lane] = 1
                kv[source + 32, lane + 64] = 1
    return np.concatenate([kv, low, high], axis=1)


def lane_of(shape):
    return lax.broadcasted_iota(jnp.int32, shape, len(shape) - 1)


def normalise(values, gain):
    centred = values - jnp.mean(values, axis=-1, keepdims=True)
    spread = jnp.mean(centred * centred, axis=-1, keepdims=True)
    return centred * lax.rsqrt(spread + 1e-05) * gain


def swap_ids():
    seq, head = lax.axis_index("seq"), lax.axis_index("head")
    column = seq // 8
    return column, seq - column * 8, head


def iotas(rows):
    shape = (rows, LANES)
    return lax.broadcasted_iota(jnp.int32, shape, 0), lax.broadcasted_iota(jnp.int32, shape, 1)


def value_picker():
    row, lane = iotas(LANES)
    return ((row % 32 < 16) & (lane == 64 + row // 32 * 16 + row % 32)).astype(F32).astype(BF16)


def keyed_rows(block, count):
    row, lane = iotas(TOK)
    zero = jnp.zeros((TOK, LANES), BF16)
    valid = row < count
    flag = jnp.where(valid, zero, jnp.where(lane < 66, jnp.full_like(zero, MASKED), zero))
    keyed = jnp.where((lane < 64) & valid, block, zero)
    return keyed, jnp.where(lane < 64, keyed, flag)


def norms(values):
    row, lane = iotas(LANES)
    sum_of = ((lane == row // 16) & (lane < 4)).astype(F32).astype(BF16)
    size = jnp.minimum(jnp.abs(values), jnp.full_like(values, 1e15))
    size = jnp.where(lax.broadcasted_iota(jnp.int32, values.shape, 1) < 64, size, jnp.zeros_like(size))
    return jnp.max(jnp.dot(size * size, sum_of, preferred_element_type=F32), axis=0, keepdims=True)


def turn_values(vals, turned, at, size):
    ones_row = lax.broadcasted_iota(jnp.int32, (LANES, size), 0) % 32 >= 16
    picked = lax.dot_general(value_picker(), vals, (((1,), (1,)), ((), ())), preferred_element_type=F32)
    turned[:, at] = jnp.where(ones_row, 1.0, picked).astype(BF16)


def half_of(packed, half):
    return packed if half == 0 else pltpu.roll(packed.astype(F32), 64, 1).astype(BF16)


def spread_heads(packed, lhs):
    _, lane = iotas(LANES)
    flags = jnp.where((lane >= 64) & (lane < 66), jnp.ones_like(packed), jnp.zeros_like(packed))
    for half in range(2):
        q = half_of(packed, half)
        for head in range(4):
            mine = (lane >= 16 * head) & (lane < 16 * head + 16)
            lhs[pl.ds((head * 2 + half) * LANES, LANES), :] = jnp.where(mine, q, flags)


def scores_of(keys, lhs):
    return lax.dot_general(keys, lhs[...], (((1,), (1,)), ((), ())), preferred_element_type=F32)


def head_columns(values, head):
    return values[:, TOK * head:TOK * head + TOK]


def attend_kernel(
    routes_hbm, local_hbm, counts_hbm, q_hbm, kv_ref, own_hbm, own_top_hbm, own_size_hbm, own_query_hbm, out_ref,
    routes_ref, local_ref, counts_ref, q_ref, own_ref, own_top_ref, own_size_ref, own_query_ref,
    raw, keys, vals, turned, lhs, acc, top, done, sems, small_sems, out_sems,
):
    column, _, head_index = swap_ids()
    seq = column * 8 + head_index
    core = lax.rem(head_index, 2)
    loads = [
        pltpu.make_async_copy(source, target, small_sems.at[index])
        for index, (source, target) in enumerate((
            (routes_hbm, routes_ref), (local_hbm, local_ref), (counts_hbm, counts_ref),
            (q_hbm, q_ref), (own_hbm, own_ref), (own_top_hbm, own_top_ref),
            (own_size_hbm, own_size_ref), (own_query_hbm, own_query_ref),
        ))
    ]
    for load in loads:
        load.start()
    for load in loads[:3]:
        load.wait()

    def source(patch, which):
        row = seq * NPL * CB + patch * CB + which
        route = routes_ref[0, row]
        offset = jnp.where(route < REACH, route - REACH, route - REACH + 1)
        local = local_ref[0, row]
        owner = lax.rem(seq + offset + 32, 32)
        return (offset + REACH + core) * NPL + local, owner * GROUPS + local * 4

    for patch in range(NPL):
        for which in range(CB):
            slot, _ = source(patch, which)
            pltpu.make_async_copy(kv_ref.at[slot], raw.at[patch * CB + which], sems.at[patch * CB + which]).start()
    for load in loads[3:]:
        load.wait()

    _, lane_kv = iotas(TOK)
    zero = jnp.zeros((TOK, LANES), BF16)

    def patch_body(patch, _):
        for which in range(CB):
            pltpu.make_async_copy(kv_ref.at[0], raw.at[patch * CB + which], sems.at[patch * CB + which]).wait()

        first = jnp.int32(0)
        key_top = jnp.zeros((1, LANES), F32)
        val_top = jnp.zeros((1, LANES), F32)
        for which in range(CB):
            _, shard = source(patch, which)
            for part in range(4):
                count = counts_ref[shard + part]
                block = raw[patch * CB + which, TOK * part:TOK * part + TOK, :]
                keyed, marked = keyed_rows(block, count)
                at = pl.ds(pl.multiple_of(first, 16), TOK)
                keys[at, :] = marked
                vals[at, :] = block
                key_top = jnp.maximum(key_top, norms(keyed))
                size = jnp.max(jnp.where(lane_kv < 64, zero, jnp.abs(block)).astype(F32), axis=0, keepdims=True)
                val_top = jnp.maximum(val_top, size)
                first = first + (count + 15) // 16 * 16
        tail = pl.ds(pl.multiple_of(first, 16), TOK)
        keys[tail, :] = keyed_rows(zero, 0)[1]
        vals[tail, :] = zero
        pieces = (first + TOK - 1) // TOK
        chunks = pieces // 2
        odd = pieces % 2 == 1

        def turn(piece, _):
            at = pl.ds(pl.multiple_of(piece * TOK, TOK), TOK)
            turn_values(vals[at, :], turned, at, TOK)
            return 0

        lax.fori_loop(0, pieces, turn, 0)

        query_top, own_size = own_query_ref[patch * 4], own_size_ref[patch * 4]
        for part in range(1, 4):
            query_top = jnp.maximum(query_top, own_query_ref[patch * 4 + part])
            own_size = jnp.maximum(own_size, own_size_ref[patch * 4 + part])
        sizes = jnp.maximum(query_top * key_top * (1.0 / 3000.0), val_top * 1e-9)
        fits = jnp.maximum(jnp.max(sizes), jnp.max(own_size)) < 1.0

        def shards_body(couple, _):
            shards = [patch * 4 + couple * 2 + side for side in range(2)]
            for side in range(2):
                spread_heads(q_ref[shards[side]], lhs.at[pl.ds(side * ROWS, ROWS)])

            def over_chunks(body):
                def chunk_body(chunk, _):
                    body(pl.ds(pl.multiple_of(chunk * CHUNK, CHUNK), CHUNK))
                    return 0

                lax.fori_loop(0, chunks, chunk_body, 0)

                @pl.when(odd)
                def _():
                    body(pl.ds(pl.multiple_of(chunks * CHUNK, CHUNK), TOK))

            def begin(side, scale):
                for head in range(4):
                    rows = slice(32 * head, 32 * head + 32)
                    acc[side, rows] = own_ref[shards[side], rows] * head_columns(scale, head)

            def gather(at, weights):
                for side in range(2):
                    for head in range(4):
                        rows = slice(32 * head, 32 * head + 32)
                        acc[side, rows] += jnp.dot(
                            turned[rows, at], head_columns(weights, side * 4 + head), preferred_element_type=F32
                        )

            @pl.when(fits)
            def _():
                for side in range(2):
                    begin(side, jnp.exp2(own_top_ref[shards[side]]))
                over_chunks(lambda at: gather(at, jnp.exp2(scores_of(keys[at, :], lhs)).astype(BF16)))

            @pl.when(jnp.logical_not(fits))
            def _():
                for side in range(2):
                    top[:, pl.ds(side * ROWS, ROWS)] = own_top_ref[shards[side]]

                def raise_top(at):
                    top[...] = jnp.maximum(top[...], jnp.max(scores_of(keys[at, :], lhs), axis=0, keepdims=True))

                over_chunks(raise_top)
                for side in range(2):
                    begin(side, jnp.exp2(own_top_ref[shards[side]] - top[:, pl.ds(side * ROWS, ROWS)]))
                over_chunks(lambda at: gather(at, jnp.exp2(scores_of(keys[at, :], lhs) - top[...]).astype(BF16)))

            for side in range(2):
                joined = [
                    acc[side, 32 * head:32 * head + 16] / acc[side, 32 * head + 16:32 * head + 32] for head in range(4)
                ]
                shard = shards[side]
                done[shard] = jnp.concatenate(joined, axis=0).astype(BF16)
                pltpu.make_async_copy(done.at[shard], out_ref.at[shard], out_sems.at[shard]).start()
            return 0

        lax.fori_loop(0, 2, shards_body, 0)
        return 0

    lax.fori_loop(0, NPL, patch_body, 0)
    for shard in range(GROUPS):
        pltpu.make_async_copy(done.at[shard], out_ref.at[shard], out_sems.at[shard]).wait()


def attend(routes, local, counts, q, kv, own, own_top, own_size, own_query):
    hbm = pl.BlockSpec(memory_space=pltpu.HBM)
    most = CB * PATCH + TOK
    return pl.pallas_call(
        attend_kernel,
        out_shape=jax.ShapeDtypeStruct((GROUPS, 64, TOK), BF16),
        in_specs=[hbm] * 9,
        out_specs=hbm,
        scratch_shapes=[
            pltpu.SMEM((1, LANES), jnp.int32),
            pltpu.SMEM((1, LANES), jnp.int32),
            pltpu.SMEM((256,), jnp.int32),
            pltpu.VMEM((GROUPS, LANES, LANES), BF16),
            pltpu.VMEM((GROUPS, LANES, TOK), F32),
            pltpu.VMEM((GROUPS, 1, ROWS), F32),
            pltpu.VMEM((GROUPS, 1, ROWS), F32),
            pltpu.VMEM((GROUPS, 1, LANES), F32),
            pltpu.VMEM((NPL * CB, PATCH, LANES), BF16),
            pltpu.VMEM((most, LANES), BF16),
            pltpu.VMEM((most, LANES), BF16),
            pltpu.VMEM((LANES, most), BF16),
            pltpu.VMEM((2 * ROWS, LANES), BF16),
            pltpu.VMEM((2, LANES, TOK), F32),
            pltpu.VMEM((1, 2 * ROWS), F32),
            pltpu.VMEM((GROUPS, 64, TOK), BF16),
            pltpu.SemaphoreType.DMA((NPL * CB,)),
            pltpu.SemaphoreType.DMA((8,)),
            pltpu.SemaphoreType.DMA((8,)),
        ],
        compiler_params=pltpu.CompilerParams(vmem_limit_bytes=60 << 20),
        cost_estimate=pl.CostEstimate(flops=20_000_000_000, bytes_accessed=6_000_000, transcendentals=17_000_000),
        name="attend",
    )(routes, local, counts, q, kv, own, own_top, own_size, own_query)


def each(body):
    def step(index, _):
        body(index)
        return 0

    lax.fori_loop(0, 8, step, 0)


def finish_kernel(
    points_ref, packed_ref, w_out_ref, gain_ref, w0_ref, w1_ref, w2_ref, w3_ref, out_ref,
    points, w_out, gain, slabs, mid, back, send, recv, local_sem, load_sem, weight_sem, pair_send, pair_recv,
):
    column, plane, head = swap_ids()
    barrier = pltpu.get_barrier_semaphore()

    def greet(index):
        @pl.when(index != head)
        def _():
            pl.semaphore_signal(barrier, inc=1, device_id=(column * 8 + plane, index), device_id_type=MESH)

        @pl.when(index != plane)
        def _():
            pl.semaphore_signal(barrier, inc=1, device_id=(column * 8 + index, head), device_id_type=MESH)

    each(greet)
    pair = (column * 8 + plane, head + 1 - 2 * lax.rem(head, 2))
    loads = [
        pltpu.make_async_copy(points_ref, points, load_sem.at[0]),
        pltpu.make_async_copy(w_out_ref, w_out, load_sem.at[1]),
        pltpu.make_async_copy(gain_ref, gain, load_sem.at[2]),
    ]
    for load in loads:
        load.start()

    shards = (w0_ref, w1_ref, w2_ref, w3_ref)
    own = [pltpu.make_async_copy(shard, slabs.at[part], weight_sem.at[part]) for part, shard in enumerate(shards)]
    lent = [
        pltpu.make_async_remote_copy(
            src_ref=shard, dst_ref=slabs.at[4 + part], send_sem=pair_send.at[part], recv_sem=pair_recv.at[part],
            device_id=pair, device_id_type=MESH,
        )
        for part, shard in enumerate(shards)
    ]
    for load in own:
        load.start()

    pl.semaphore_wait(barrier, 14)

    def level_leg(shard, slot):
        return pltpu.make_async_remote_copy(
            src_ref=packed_ref.at[shard], dst_ref=mid.at[slot],
            send_sem=send.at[0, shard], recv_sem=recv.at[0, slot],
            device_id=(column * 8 + plane, shard), device_id_type=MESH,
        )

    def plane_leg(home, slot):
        return pltpu.make_async_remote_copy(
            src_ref=mid.at[home], dst_ref=back.at[slot],
            send_sem=send.at[1, home], recv_sem=recv.at[1, slot],
            device_id=(column * 8 + home, head), device_id_type=MESH,
        )

    level_stay = pltpu.make_async_copy(packed_ref.at[head], mid.at[head], local_sem.at[0])
    plane_stay = pltpu.make_async_copy(mid.at[plane], back.at[plane], local_sem.at[1])
    level_stay.start()

    def start(step):
        shard = step

        @pl.when(shard != head)
        def _():
            level_leg(shard, head).start()

    each(start)

    def forward(step):
        home = step

        @pl.when(home == head)
        def _():
            level_stay.wait()

        @pl.when(home != head)
        def _():
            level_leg(0, home).wait_recv()

        @pl.when(home == plane)
        def _():
            plane_stay.start()

        @pl.when(home != plane)
        def _():
            plane_leg(home, plane).start()

    each(forward)
    for load in lent:
        load.start()
    for load in loads:
        load.wait()

    def wait(group):
        @pl.when(group == plane)
        def _():
            plane_stay.wait()

        @pl.when(group != plane)
        def _():
            plane_leg(0, group).wait_recv()

    each(wait)

    attended = back[...].reshape(D, TOK)
    updated = points[...].astype(F32) + lax.dot_general(
        attended, w_out[...], (((0,), (0,)), ((), ())), preferred_element_type=F32
    )
    updated = updated.astype(BF16).astype(F32)
    normed = normalise(updated, gain[...]).astype(BF16)
    low, high = updated[:, :256], updated[:, 256:]
    for part in range(GROUPS):
        if part < 4:
            own[part].wait()
        else:
            lent[part - 4].wait_recv()
        hidden = jnp.dot(normed, slabs[part, :D], preferred_element_type=F32)
        hidden = (hidden * (0.5 * (1.0 + lax.erf(hidden * (2.0 ** -0.5))))).astype(BF16)
        low = low + jnp.dot(hidden, slabs[part, D:D + 256], preferred_element_type=F32)
        high = high + jnp.dot(hidden, slabs[part, D + 256:], preferred_element_type=F32)
    out_ref[:, :256] = low.astype(BF16)
    out_ref[:, 256:] = high.astype(BF16)

    def sent(index):
        @pl.when(index != head)
        def _():
            level_leg(index, head).wait_send()

        @pl.when(index != plane)
        def _():
            plane_leg(index, plane).wait_send()

    each(sent)
    for load in lent:
        load.wait_send()


def finish(points, packed, w_out, gain, weights):
    hbm = pl.BlockSpec(memory_space=pltpu.HBM)
    return pl.pallas_call(
        finish_kernel,
        out_shape=jax.ShapeDtypeStruct((TOK, D), BF16),
        in_specs=[hbm] * 8,
        out_specs=pl.BlockSpec(memory_space=pltpu.VMEM),
        scratch_shapes=[
            pltpu.VMEM((TOK, D), BF16),
            pltpu.VMEM((D, D), BF16),
            pltpu.VMEM((1, D), F32),
            pltpu.VMEM((GROUPS, 2 * D, 256), BF16),
            pltpu.VMEM((GROUPS, 64, TOK), BF16),
            pltpu.VMEM((GROUPS, 64, TOK), BF16),
            pltpu.SemaphoreType.DMA((2, 8)),
            pltpu.SemaphoreType.DMA((2, 8)),
            pltpu.SemaphoreType.DMA((2,)),
            pltpu.SemaphoreType.DMA((3,)),
            pltpu.SemaphoreType.DMA((4,)),
            pltpu.SemaphoreType.DMA((4,)),
            pltpu.SemaphoreType.DMA((4,)),
        ],
        compiler_params=pltpu.CompilerParams(
            collective_id=1, has_side_effects=True, vmem_limit_bytes=50 << 20
        ),
        name="finish",
    )(points, packed, w_out, gain.reshape(1, D), *weights)


def exchange_kernel(
    points_ref, gain_ref, w_ref, scale_ref, place_ref, counts_ref, route_ref, local_ref, w1_ref, w2_ref,
    kv_out, q_out, route_out, local_out, own_out, own_top_out, own_size_out, own_query_out, weights_out, weights_below, weights_above,
    kv_ref, q_ref, raw, queries, keys, turned, lhs, scores, own, own_top, own_size, own_query,
    all_send, all_recv, ring_send, ring_recv, pair_send, pair_recv, route_sem, local_sem, load_sem, own_sem, near_send, near_recv,
):
    column, plane, head = swap_ids()
    core = lax.rem(head, 2)
    spot = column * 4 + head // 2
    after, before = lax.rem(spot + 1, 16), lax.rem(spot + 15, 16)
    right = ((after // 4) * 8 + plane, lax.rem(after, 4) * 2 + core)
    left = ((before // 4) * 8 + plane, lax.rem(before, 4) * 2 + core)
    pair = (column * 8 + plane, head + 1 - 2 * core)
    partner = (column * 8 + head, plane)
    diagonal = plane == head
    across = jnp.logical_not(diagonal)

    barrier = pltpu.get_barrier_semaphore()

    def greet(index, _):
        @pl.when(across | (index != head))
        def _():
            pl.semaphore_signal(barrier, inc=1, device_id=(column * 8 + head, index), device_id_type=MESH)
        return 0

    lax.fori_loop(0, 8, greet, 0)
    level = head // 2
    above = (column * 8 + plane, lax.rem(level + 1, 4) * 2 + core)
    below = (column * 8 + plane, lax.rem(level + 3, 4) * 2 + core)
    for other in (right, left, pair, above, below):
        pl.semaphore_signal(barrier, inc=1, device_id=other, device_id_type=MESH)

    def enter():
        @pl.when(diagonal)
        def _():
            pl.semaphore_wait(barrier, 12)

        @pl.when(across)
        def _():
            pl.semaphore_wait(barrier, 13)

    def rows(half):
        return pl.ds(half * LANES, LANES)

    def spread(group, half, shard):
        return pltpu.make_async_remote_copy(
            src_ref=kv_ref.at[group, rows(half)],
            dst_ref=kv_out.at[4 + lax.rem(plane, 2), shard, rows(half)],
            send_sem=all_send.at[half, group],
            recv_sem=all_recv.at[half, shard],
            device_id=(column * 8 + group, plane),
            device_id_type=MESH,
        )

    def landed(half, shard):
        return pltpu.make_async_remote_copy(
            src_ref=kv_ref.at[0, rows(half)],
            dst_ref=kv_out.at[4 + core, shard, rows(half)],
            send_sem=all_send.at[half, 0],
            recv_sem=all_recv.at[half, shard],
            device_id=pair,
            device_id_type=MESH,
        )

    def spread_q(group, shard):
        return pltpu.make_async_remote_copy(
            src_ref=q_ref.at[group],
            dst_ref=q_out.at[shard],
            send_sem=all_send.at[2, group],
            recv_sem=all_recv.at[2, shard],
            device_id=(column * 8 + group, plane),
            device_id_type=MESH,
        )

    def at_home(half):
        return pltpu.make_async_copy(
            kv_ref.at[plane, rows(half)], kv_out.at[4 + core, head, rows(half)], local_sem.at[half]
        )

    q_at_home = pltpu.make_async_copy(q_ref.at[plane], q_out.at[head], local_sem.at[2])
    routes_at_home = [
        pltpu.make_async_copy(route_ref, route_out, local_sem.at[3]),
        pltpu.make_async_copy(local_ref, local_out, local_sem.at[4]),
    ]
    routes_sent = [
        pltpu.make_async_remote_copy(
            src_ref=source, dst_ref=target, send_sem=route_sem.at[0, index], recv_sem=route_sem.at[1, index],
            device_id=partner, device_id_type=MESH,
        )
        for index, (source, target) in enumerate(((route_ref, route_out), (local_ref, local_out)))
    ]

    def start(group):
        @pl.when(across | (group != plane))
        def _():
            spread(group, 0, head).start()
            spread(group, 1, head).start()

    def start_q(group):
        @pl.when(across | (group != plane))
        def _():
            spread_q(group, head).start()

    parts = (
        (w1_ref, pl.ds(0, D)), (w2_ref.at[:, pl.ds(0, 256)], pl.ds(D, 256)), (w2_ref.at[:, pl.ds(256, 256)], pl.ds(D + 256, 256)),
    )
    joins = [
        pltpu.make_async_copy(source, weights_out.at[rows_at], load_sem.at[2 + index])
        for index, (source, rows_at) in enumerate(parts)
    ]
    nears = [
        pltpu.make_async_remote_copy(
            src_ref=source, dst_ref=target.at[rows_at], send_sem=near_send.at[way, index],
            recv_sem=near_recv.at[way, index], device_id=to, device_id_type=MESH,
        )
        for way, (target, to) in enumerate(((weights_below, above), (weights_above, below)))
        for index, (source, rows_at) in enumerate(parts)
    ]
    for join in joins:
        join.start()

    normed = normalise(points_ref[...].astype(F32), gain_ref[...]).astype(BF16)
    for couple in range(GROUPS // 2):
        columns = slice(384 * couple, 384 * couple + 384)
        projected = jnp.dot(normed, w_ref[:, columns], preferred_element_type=F32)
        projected = (projected * scale_ref[:, columns]).astype(BF16)
        kv = jnp.dot(projected, place_ref[:, :256], preferred_element_type=F32).astype(BF16)
        q = jnp.dot(projected[:128], place_ref[:, 256:512], preferred_element_type=F32)
        q = (q + jnp.dot(projected[128:], place_ref[:, 512:], preferred_element_type=F32)).astype(BF16)
        for side in range(2):
            kv_ref[2 * couple + side] = kv[:, 128 * side:128 * side + 128]
            q_ref[2 * couple + side] = q[:, 128 * side:128 * side + 128]
        if couple == 0:
            enter()
        start(2 * couple)
        start(2 * couple + 1)
    each(start_q)
    for near in nears:
        near.start()

    @pl.when(diagonal)
    def _():
        at_home(0).start()
        at_home(1).start()
        q_at_home.start()
        for copy in routes_at_home:
            copy.start()

    @pl.when(across)
    def _():
        for copy in routes_sent:
            copy.start()


    def moved(source, target, half, send, recv, to):
        return pltpu.make_async_remote_copy(
            src_ref=kv_out.at[source, :, rows(half)], dst_ref=kv_out.at[target, :, rows(half)],
            send_sem=send, recv_sem=recv, device_id=to, device_id_type=MESH,
        )

    def hop(way, step, half):
        if way == 0:
            source, to = 4 - 2 * step + core, right
            target = 2 - 2 * step + core
        else:
            source, to = 4 + 2 * step + core, left
            target = 6 + 2 * step + core
        return moved(source, target, half, ring_send.at[way, step, half], ring_recv.at[way, step, half], to)

    def shared(place, half):
        return moved(2 * place + core, 2 * place + core, half, pair_send.at[place, half], pair_recv.at[place, half], pair)

    def taken(place, half):
        return moved(2 * place + 1 - core, 2 * place + 1 - core, half, pair_send.at[place, half], pair_recv.at[place, half], pair)

    for half in range(2):
        def wait(shard):
            @pl.when(across | (shard != head))
            def _():
                landed(half, shard).wait_recv()

        each(wait)

        @pl.when(diagonal)
        def _():
            at_home(half).wait()

        hop(0, 0, half).start()
        hop(1, 0, half).start()
        shared(2, half).start()
    def wait_q(shard):
        @pl.when(across | (shard != head))
        def _():
            spread_q(0, shard).wait_recv()

    each(wait_q)

    @pl.when(diagonal)
    def _():
        q_at_home.wait()

    loads = [
        pltpu.make_async_copy(kv_out.at[4 + core], raw, load_sem.at[0]),
        pltpu.make_async_copy(q_out, queries, load_sem.at[1]),
    ]
    for load in loads:
        load.start()
    for load in loads:
        load.wait()

    def own_keys(shard):
        at = pl.ds(pl.multiple_of(shard * TOK, TOK), TOK)
        keys[at, :] = keyed_rows(raw[shard], counts_ref[(column * 8 + head) * GROUPS + shard])[1]
        turn_values(raw[shard], turned, at, TOK)

    each(own_keys)

    def own_saved(shard):
        return (
            pltpu.make_async_copy(own.at[shard], own_out.at[shard], own_sem.at[0, shard]),
            pltpu.make_async_copy(own_top.at[shard], own_top_out.at[shard], own_sem.at[1, shard]),
            pltpu.make_async_copy(own_size.at[shard], own_size_out.at[shard], own_sem.at[2, shard]),
            pltpu.make_async_copy(own_query.at[shard], own_query_out.at[shard], own_sem.at[3, shard]),
        )

    def own_run(begin, end):
        def own_shard(shard, _):
            patch = shard // 4
            packed = queries[shard]
            spread_heads(packed, lhs)
            most = None
            spots = [pl.ds(pl.multiple_of(patch * PATCH + piece * CHUNK, CHUNK), CHUNK) for piece in range(2)]
            for piece in range(2):
                found = scores_of(keys[spots[piece], :], lhs)
                scores[piece] = found
                found = jnp.max(found, axis=0, keepdims=True)
                most = found if piece == 0 else jnp.maximum(most, found)
            own_top[shard] = most
            total = [None] * 4
            for piece in range(2):
                weights = jnp.exp2(scores[piece] - most).astype(BF16)
                for index in range(4):
                    rows_of = slice(32 * index, 32 * index + 32)
                    term = jnp.dot(
                        turned[rows_of, spots[piece]], head_columns(weights, index), preferred_element_type=F32
                    )
                    total[index] = term if piece == 0 else total[index] + term
            for index in range(4):
                own[shard, 32 * index:32 * index + 32] = total[index]
                columns = slice(TOK * index, TOK * index + TOK)
                size = jnp.max(jnp.abs(total[index]), axis=0, keepdims=True) * 1e-12
                own_size[shard, :, columns] = jnp.maximum(size, jnp.abs(most[:, columns]) * (1.0 / 55.0))
            own_query[shard] = jnp.maximum(norms(half_of(packed, 0)), norms(half_of(packed, 1)))
            for save in own_saved(shard):
                save.start()
            return 0

        lax.fori_loop(begin, end, own_shard, 0)

    for half in range(2):
        hop(0, 0, half).wait_recv()
        hop(0, 1, half).start()
        hop(1, 0, half).wait_recv()
        hop(1, 1, half).start()
        shared(1, half).start()
        shared(3, half).start()
        own_run(4 * half, 4 * half + 4)
    for half in range(2):
        hop(0, 1, half).wait_recv()
        shared(0, half).start()
        hop(1, 1, half).wait_recv()
        shared(4, half).start()

    def sent(group):
        @pl.when(across | (group != plane))
        def _():
            spread(group, 0, head).wait_send()
            spread(group, 1, head).wait_send()
            spread_q(group, head).wait_send()

    each(sent)

    @pl.when(diagonal)
    def _():
        for copy in routes_at_home:
            copy.wait()

    @pl.when(across)
    def _():
        for copy in routes_sent:
            copy.wait()


    for half in range(2):
        for way in range(2):
            for step in range(2):
                hop(way, step, half).wait_send()
        for place in range(5):
            shared(place, half).wait_send()
            taken(place, half).wait_recv()
    for copy in (*joins, *nears):
        copy.wait()

    def saved(shard):
        for save in own_saved(shard):
            save.wait()

    each(saved)


def exchange(points, gain, w_qkv, counts, routes, local, w1, w2):
    scale = np.ones((1, 1536), np.float32)
    scale[0, np.arange(1536) % 48 < 16] = HEAD_DIM ** -0.5 * math.log2(math.e)
    vmem = pl.BlockSpec(memory_space=pltpu.VMEM)
    anywhere = pl.BlockSpec(memory_space=pltpu.HBM)
    return pl.pallas_call(
        exchange_kernel,
        out_shape=(
            jax.ShapeDtypeStruct((10, GROUPS, TOK, LANES), BF16),
            jax.ShapeDtypeStruct((GROUPS, LANES, LANES), BF16),
            jax.ShapeDtypeStruct((1, LANES), jnp.int32),
            jax.ShapeDtypeStruct((1, LANES), jnp.int32),
            jax.ShapeDtypeStruct((GROUPS, LANES, TOK), F32),
            jax.ShapeDtypeStruct((GROUPS, 1, ROWS), F32),
            jax.ShapeDtypeStruct((GROUPS, 1, ROWS), F32),
            jax.ShapeDtypeStruct((GROUPS, 1, LANES), F32),
            jax.ShapeDtypeStruct((2 * D, 256), BF16),
            jax.ShapeDtypeStruct((2 * D, 256), BF16),
            jax.ShapeDtypeStruct((2 * D, 256), BF16),
        ),
        in_specs=[vmem] * 5 + [pl.BlockSpec(memory_space=pltpu.SMEM)] + [anywhere] * 4,
        out_specs=(anywhere,) * 11,
        scratch_shapes=[
            pltpu.VMEM((GROUPS, TOK, LANES), BF16),
            pltpu.VMEM((GROUPS, LANES, LANES), BF16),
            pltpu.VMEM((GROUPS, TOK, LANES), BF16),
            pltpu.VMEM((GROUPS, LANES, LANES), BF16),
            pltpu.VMEM((NPL * PATCH, LANES), BF16),
            pltpu.VMEM((LANES, NPL * PATCH), BF16),
            pltpu.VMEM((ROWS, LANES), BF16),
            pltpu.VMEM((2, CHUNK, ROWS), F32),
            pltpu.VMEM((GROUPS, LANES, TOK), F32),
            pltpu.VMEM((GROUPS, 1, ROWS), F32),
            pltpu.VMEM((GROUPS, 1, ROWS), F32),
            pltpu.VMEM((GROUPS, 1, LANES), F32),
            pltpu.SemaphoreType.DMA((3, 8)),
            pltpu.SemaphoreType.DMA((3, 8)),
            pltpu.SemaphoreType.DMA((2, 2, 2)),
            pltpu.SemaphoreType.DMA((2, 2, 2)),
            pltpu.SemaphoreType.DMA((5, 2)),
            pltpu.SemaphoreType.DMA((5, 2)),
            pltpu.SemaphoreType.DMA((2, 2)),
            pltpu.SemaphoreType.DMA((5,)),
            pltpu.SemaphoreType.DMA((5,)),
            pltpu.SemaphoreType.DMA((4, 8)),
            pltpu.SemaphoreType.DMA((2, 3)),
            pltpu.SemaphoreType.DMA((2, 3)),
        ],
        compiler_params=pltpu.CompilerParams(collective_id=0, has_side_effects=True, vmem_limit_bytes=60 << 20),
        name="exchange",
    )(
        points, gain.reshape(1, D), w_qkv, jnp.asarray(scale), jnp.asarray(placing(), BF16),
        counts, routes, local, w1, w2,
    )


def per_device(
    points, gain_attn, w_qkv, w_out, gain_mlp, w_fc1, w_fc2, contact_route, contact_patch, counts
):
    slots, q, routes, local, sums, tops, sizes, tallest, joined, low, high = exchange(
        points, gain_attn, w_qkv, counts, contact_route.reshape(1, -1), contact_patch, w_fc1, w_fc2
    )
    far = lax.ppermute(joined, "head", [(head, (head + 4) % GROUPS) for head in range(GROUPS)])
    weights = [joined, low, high, far]
    packed = attend(routes, local, counts, q, slots.reshape(20, PATCH, LANES), sums, tops, sizes, tallest)
    return finish(points, packed, w_out, gain_mlp, weights)


def solution(mesh):
    return jax.shard_map(
        per_device,
        mesh=mesh,
        in_specs=(
            P(("seq", "head"), None), P(), P(), P(), P(), P(None, "head"), P("head", None),
            P("head", None, None), P("head", None), P(),
        ),
        out_specs=P(("seq", "head"), None),
        check_vma=False,
    )
```
